768 devices in a mesh: gx: 12 (over z_lo, x), gy: 8 (over z_hi, core), gz: 8 (over y).
Axes of the slice: x: 4, y: 8, z: 12 (z_hi: 4, z_lo: 3; z = z_hi * 3 + z_lo), core: 2. Of those that a mesh axis runs over, the one named last changes fastest.
Arguments:
- positions: float32 [3, 36, 24, 24, 2], P(None, 'gx', 'gy', 'gz'), may hold values from 0.7 to 17.3, as said below
- velocity: float32 [3, 36, 24, 24, 2], P(None, 'gx', 'gy', 'gz'), may hold values from -2 to 2
- species: int32 [36, 24, 24, 2], P('gx', 'gy', 'gz'), may hold values from 0 to 4
- region_count: int32 [36, 24, 24], P('gx', 'gy', 'gz'), may hold values from 0 to 2, as said below
- neighbours: int32 [36, 24, 24, 2, 40], P('gx', 'gy', 'gz'), may hold values from -1 to 249, as said below
- basis_weight: bfloat16 [8, 128], replicated, may hold values from -2 to 2
- species_embed: bfloat16 [5, 128], replicated, may hold values from -3 to 3
- weight_map: bfloat16 [128, 64], replicated, may hold values from -0.5 to 0.5
- scalar_map: bfloat16 [64, 128], replicated, may hold values from -0.75 to 0.75
- energy_out: float32 [128], replicated, may hold values from -0.5 to 0.5
- species_energy: float32 [5], replicated, may hold values from -2 to -0.5
Outputs:
- forces: float32 [2, 3, 36, 24, 24, 2], P(None, None, 'gx', 'gy', 'gz')
- energy: float32 [2], replicated
The draws below stay inside these ranges and needn't reach their ends.
Inputs may be any that keep to these rules, and one draw needn't show every extreme that they name: `region_count`: slots at or above a region's count are empty. every region of the last x layer is full. `positions`: atoms sit on a jittered lattice of spacing 2 inside their region, region (X, Y, Z) covering [6 (X % 3), 6 (X % 3) + 6) and likewise along y and z in its domain's frame; any two slots are 1.4 or more apart. `neighbours`: entries follow the numbering of the steps and name live atoms within lattice distance below 3 spacings; live entries come first, then -1; an empty slot's list is all -1; each unordered pair of atoms appears in at most one list: with p the pair's lattice point that comes first in x, then y, then z, and o the lattice offset from p to the other point, the pair is listed by p's atom if the components of o sum to an even number, else by the other atom. Entries index a 5 x 5 x 5 block of regions around the domain.
All inputs are finite; a program needn't handle non-finite values.
Results may differ from the reference program's by a relative error of at most 0.013.
Values sent between devices are 32-bit elements; how exact they have to be, the bound alone decides.
No kernel may reach another device: no remote copies, remote signals or barrier semaphores. Data moves between devices by JAX's collectives and lax.ppermute only.
A program may use at most 64 MiB of HBM per device.

```python
import math
import jax
import jax.numpy as jnp
import numpy as np
from jax import lax

CH = 64
LAT = 128
NB = 8
NSPEC = 5
SITES = 2
MAXNB = 40
REG_X = 36
REG_Y = 24
REG_Z = 24


def shell_offsets():
    listed = []
    for step_x in range(-2, 3):
        for step_y in range(-2, 3):
            for step_z in range(-2, 3):
                length = step_x * step_x + step_y * step_y + step_z * step_z
                upward = step_x > 0 or (step_x == 0 and step_y > 0) or (step_x == 0 and step_y == 0 and (step_z > 0))
                parity_even = (step_x + step_y + step_z) % 2 == 0
                keeps = upward and parity_even or (not upward and (not parity_even))
                if 0 < length < 9 and keeps:
                    listed.append((length, step_x, step_y, step_z))
    listed = sorted(listed)
    return np.array([item[1:] for item in listed], dtype=np.int32)


def lattice_layout(key):
    count_key = jax.random.fold_in(key, 101)
    perm_key = jax.random.fold_in(key, 202)
    layer = jnp.arange(REG_X, dtype=jnp.int32)
    lowest = SITES // 4 + (SITES - SITES // 4) * layer // (REG_X - 1)
    extra = jax.random.randint(count_key, (REG_X, REG_Y, REG_Z), 0, 3)
    counts = jnp.minimum(SITES, lowest[:, None, None] + extra).astype(jnp.int32)
    region_keys = jax.random.split(perm_key, REG_X * REG_Y * REG_Z)
    orders = jax.vmap(lambda one_key: jax.random.permutation(one_key, 27))(region_keys)
    places = orders.reshape(REG_X, REG_Y, REG_Z, 27)[..., :SITES].astype(jnp.int32)
    return (counts, places)


def draw_region_count(key, part):
    return lattice_layout(key)[0]


def draw_positions(key, part):
    counts, places = lattice_layout(key)
    region_x = (jnp.arange(REG_X) % 3)[:, None, None, None]
    region_y = (jnp.arange(REG_Y) % 3)[None, :, None, None]
    region_z = (jnp.arange(REG_Z) % 3)[None, None, :, None]
    coord_x = 3 * region_x + places // 9
    coord_y = 3 * region_y + places // 3 % 3
    coord_z = 3 * region_z + places % 3
    lattice = jnp.stack([coord_x, coord_y, coord_z]).astype(jnp.float32) * 2.0 + 1.0
    jitter_key = jax.random.fold_in(key, 303)
    jitter = jnp.clip(0.12 * jax.random.normal(jitter_key, lattice.shape, jnp.float32), -0.3, 0.3)
    return lattice + jitter


def draw_neighbours(key, part):
    counts, places = lattice_layout(key)
    offsets = jnp.asarray(shell_offsets())
    shell_count = offsets.shape[0]
    region_x = jnp.arange(REG_X)[:, None, None, None]
    region_y = jnp.arange(REG_Y)[None, :, None, None]
    region_z = jnp.arange(REG_Z)[None, None, :, None]
    slot_ids = jnp.arange(SITES)[None, None, None, :]
    occupied = slot_ids < counts[..., None]
    lattice_x = 3 * region_x + places // 9
    lattice_y = 3 * region_y + places // 3 % 3
    lattice_z = 3 * region_z + places % 3
    atom_ids = jnp.arange(REG_X * REG_Y * REG_Z * SITES, dtype=jnp.int32).reshape(REG_X, REG_Y, REG_Z, SITES)
    occupancy = jnp.full((3 * REG_X, 3 * REG_Y, 3 * REG_Z), -1, jnp.int32)
    occupancy = occupancy.at[lattice_x, lattice_y, lattice_z].set(jnp.where(occupied, atom_ids, -1))
    target_x = (lattice_x[..., None] + offsets[:, 0]) % (3 * REG_X)
    target_y = (lattice_y[..., None] + offsets[:, 1]) % (3 * REG_Y)
    target_z = (lattice_z[..., None] + offsets[:, 2]) % (3 * REG_Z)
    target = occupancy[target_x, target_y, target_z]
    valid = occupied[..., None] & (target >= 0)
    block_x = (target_x // 3 - 3 * (region_x[..., None] // 3) + 1) % REG_X
    block_y = (target_y // 3 - 3 * (region_y[..., None] // 3) + 1) % REG_Y
    block_z = (target_z // 3 - 3 * (region_z[..., None] // 3) + 1) % REG_Z
    extended = ((block_x * 5 + block_y) * 5 + block_z) * SITES + target % SITES
    entry = jnp.where(valid, extended, -1).astype(jnp.int32)
    sort_key = jnp.where(valid, 0, 1) * shell_count + jnp.arange(shell_count)
    order = jnp.argsort(sort_key, axis=-1)
    entry = jnp.take_along_axis(entry, order, axis=-1)
    spare = max(MAXNB - shell_count, 0)
    padding = jnp.full(entry.shape[:-1] + (spare,), -1, jnp.int32)
    return jnp.concatenate([entry, padding], axis=-1)[..., :MAXNB]


def set_ends(values, stream_key, smallest, high):
    index_at = [jax.random.randint(jax.random.fold_in(stream_key, axis), (), 0, length) for axis, length in enumerate(values.shape)]
    widest = values.shape.index(max(values.shape))
    next_to = index_at[:widest] + [(index_at[widest] + 1) % values.shape[widest]] + index_at[widest + 1:]
    return values.at[tuple(index_at)].set(smallest).at[tuple(next_to)].set(high)


def level_of(stream_key, extent, cuts, least, top_value):
    loudness, own = 1.0, jax.random.fold_in(stream_key, 6)
    for dim, parts in cuts:
        heights = jnp.exp(jax.random.uniform(jax.random.fold_in(own, dim), (parts,), jnp.float32, least / len(cuts), top_value / len(cuts)))
        loudness = loudness * jnp.repeat(heights, extent[dim] // parts).reshape([-1 if axis == dim else 1 for axis in range(len(extent))])
    return loudness


def scatter_about(own_key, shape, scale, bound, shards=(), kind=jnp.bfloat16):
    result = scale * jax.random.normal(own_key, shape, jnp.float32)
    if shards:
        result = result * level_of(own_key, shape, shards, -0.22, 0.18)
    return jnp.clip(result, -bound, bound).astype(kind)


def setup_inputs(seed: int = 0) -> dict:
    seeds = jax.random.split(jax.random.key(seed), 12)
    positions = draw_positions(jax.random.fold_in(seeds[11], 71), 0)
    velocity = scatter_about(seeds[1], (3, REG_X, REG_Y, REG_Z, SITES), 0.5, 2.0, ((1, 12), (2, 8), (3, 8)), jnp.float32)
    species = set_ends(jax.random.randint(seeds[2], (REG_X, REG_Y, REG_Z, SITES), 0, NSPEC), jax.random.fold_in(seeds[2], 1), 0, NSPEC - 1).astype(jnp.int32)
    region_count = draw_region_count(jax.random.fold_in(seeds[11], 71), 0)
    neighbours = draw_neighbours(jax.random.fold_in(seeds[11], 71), 0)
    basis_weight = scatter_about(seeds[5], (NB, LAT), NB ** -0.5, 2.0)
    species_embed = scatter_about(seeds[6], (NSPEC, LAT), 0.5, 3.0)
    weight_map = scatter_about(seeds[7], (LAT, CH), LAT ** -0.5, 0.5)
    scalar_map = scatter_about(seeds[8], (CH, LAT), CH ** -0.5, 0.75)
    energy_out = scatter_about(seeds[9], (LAT,), LAT ** -0.5, 0.5, (), jnp.float32)
    species_energy = jnp.clip(jax.random.uniform(seeds[10], (NSPEC,), jnp.float32, -2.0, -0.5), -2.0, -0.5)
    return {"positions": positions, "velocity": velocity, "species": species, "region_count": region_count, "neighbours": neighbours, "basis_weight": basis_weight, "species_embed": species_embed, "weight_map": weight_map, "scalar_map": scalar_map, "energy_out": energy_out, "species_energy": species_energy}


cutoff = 6.0
env_scale = 0.25
domain_side = 18.0
time_step = 0.15
atom_masses = (1.008, 12.011, 14.007, 15.999, 32.06)

def contract(weight, values):
    return lax.dot_general(weight, values, (((0,), (0,)), ((), ())), preferred_element_type=jnp.float32)

def edge_front(displace, species_pair, basis_weight, species_embed, weight_map):
    radius = jnp.sqrt(lax.optimization_barrier(jnp.sum(displace * displace, axis=0)))
    direction = displace / radius[None, :]
    scaled = jnp.minimum(radius / cutoff, 1.0)
    envelope = 1.0 - 28.0 * scaled ** 6 + 48.0 * scaled ** 7 - 21.0 * scaled ** 8
    orders = jnp.arange(1, basis_weight.shape[0] + 1).astype(jnp.float32)
    radial = math.sqrt(2.0 / cutoff) * jnp.sin(orders[:, None] * (math.pi / cutoff) * radius[None, :]) / radius[None, :]
    preact = contract(basis_weight, radial.astype(jnp.bfloat16)) + contract(species_embed, species_pair)
    latent = jax.nn.silu(preact).astype(jnp.bfloat16)
    weights = contract(weight_map, latent) * envelope[None, :]
    moments = jnp.concatenate([weights, weights * direction[0:1], weights * direction[1:2], weights * direction[2:3]], axis=0)
    return (latent, weights, direction, envelope, moments)

def spread_rows(centre, list_width):
    return jnp.broadcast_to(centre[:, :, None], (centre.shape[0], centre.shape[1], list_width)).reshape(centre.shape[0], centre.shape[1] * list_width)

def edge_energy(latent, weights, direction, envelope, centre_env, pair_mask, scalar_map, energy_out):
    channels = weights.shape[0]
    spread = spread_rows(centre_env, weights.shape[1] // centre_env.shape[1])
    aligned = spread[:channels] + direction[0:1] * spread[channels:2 * channels] + direction[1:2] * spread[2 * channels:3 * channels] + direction[2:3] * spread[3 * channels:]
    coupling = (env_scale * weights * aligned).astype(jnp.bfloat16)
    hidden = jax.nn.silu(latent.astype(jnp.float32) + contract(scalar_map, coupling))
    per_pair = envelope * lax.optimization_barrier(jnp.sum(hidden * energy_out[:, None], axis=0))
    return jnp.sum(per_pair * pair_mask)

def flip_signs(channels):
    return jnp.concatenate([jnp.ones((channels,), jnp.float32), -jnp.ones((3 * channels,), jnp.float32)])[:, None]

def inverse_mass(species):
    table = 1.0 / jnp.array(atom_masses, dtype=jnp.float32)
    return lax.optimization_barrier(jnp.sum((species[..., None] == jnp.arange(table.shape[0])).astype(jnp.float32) * table, axis=-1))

def pair_inputs(extended, own_pos, own_kind, neighbours, kind_values):
    offset_base = ((jnp.arange(5) + 2) // 3 - 1).astype(jnp.float32) * domain_side
    cube_zero = jnp.zeros((5, 5, 5), jnp.float32)
    shifts = jnp.stack([cube_zero + offset_base[:, None, None], cube_zero + offset_base[None, :, None], cube_zero + offset_base[None, None, :]])
    far_pos = (extended[:3] + shifts[..., None]).reshape(3, -1)
    far_kind = extended[3].reshape(-1)
    entries = neighbours.reshape(-1)
    pair_mask = (entries >= 0).astype(jnp.float32)
    safe_index = jnp.maximum(entries, 0)
    centres = own_pos.reshape(3, -1)
    list_width = neighbours.shape[-1]
    near_pos = jnp.broadcast_to(centres[:, :, None], (3, centres.shape[1], list_width)).reshape(3, -1)
    near_kind = jnp.broadcast_to(own_kind.reshape(-1)[:, None], (centres.shape[1], list_width)).reshape(-1)
    displace = jnp.take(far_pos, safe_index, axis=1) - near_pos
    far_species = jnp.take(far_kind, safe_index)
    species_pair = ((far_species[None, :] == kind_values[:, None]).astype(jnp.float32) + (near_kind[None, :] == kind_values[:, None]).astype(jnp.float32)).astype(jnp.bfloat16)
    return (displace, species_pair, pair_mask, safe_index)

def to_devices(values):
    shaped = values.reshape(values.shape[0], values.shape[1] // 3, 3, values.shape[2] // 3, 3, values.shape[3] // 3, 3, values.shape[4])
    return shaped.transpose(1, 3, 5, 0, 2, 4, 6, 7)

def to_regions(values):
    shaped = values.transpose(3, 0, 4, 1, 5, 2, 6, 7)
    return shaped.reshape(values.shape[3], values.shape[0] * 3, values.shape[1] * 3, values.shape[2] * 3, values.shape[7])

def ghost_window(values):
    for axis_id in range(3):
        lower = jnp.roll(lax.index_in_dim(values, 2, 4 + axis_id), 1, axis=axis_id)
        upper = jnp.roll(lax.index_in_dim(values, 0, 4 + axis_id), -1, axis=axis_id)
        values = jnp.concatenate([lower, values, upper], axis=4 + axis_id)
    return values

def owner_fold(values):
    for axis_id in range(3):
        first = lax.index_in_dim(values, 1, 4 + axis_id) + jnp.roll(lax.index_in_dim(values, 4, 4 + axis_id), 1, axis=axis_id)
        middle = lax.index_in_dim(values, 2, 4 + axis_id)
        last = lax.index_in_dim(values, 3, 4 + axis_id) + jnp.roll(lax.index_in_dim(values, 0, 4 + axis_id), -1, axis=axis_id)
        values = jnp.concatenate([first, middle, last], axis=4 + axis_id)
    return values

def device_front(extended, own_pos, own_kind, neighbours, params):
    basis_weight, species_embed, weight_map, scalar_map, energy_out = params
    kind_values = jnp.arange(species_embed.shape[0]).astype(jnp.float32)
    displace, species_pair, pair_mask, safe_index = pair_inputs(extended, own_pos, own_kind, neighbours, kind_values)
    latent, weights, direction, envelope, moments = edge_front(displace, species_pair, basis_weight, species_embed, weight_map)
    channels = weights.shape[0]
    sites = own_pos.shape[-1]
    own_count = 27 * sites
    masked = moments * pair_mask[None, :]
    centre_sum = lax.optimization_barrier(jnp.sum(masked.reshape(4 * channels, own_count, neighbours.shape[-1]), axis=2))
    scattered = jnp.zeros((4 * channels, 125 * sites), jnp.float32).at[:, safe_index].add(masked * flip_signs(channels))
    return (scattered.reshape(4 * channels, 5, 5, 5, sites), centre_sum)

def device_energy(extended, own_pos, own_kind, neighbours, environment, params):
    basis_weight, species_embed, weight_map, scalar_map, energy_out = params
    kind_values = jnp.arange(species_embed.shape[0]).astype(jnp.float32)
    displace, species_pair, pair_mask, safe_index = pair_inputs(extended, own_pos, own_kind, neighbours, kind_values)
    latent, weights, direction, envelope, moments = edge_front(displace, species_pair, basis_weight, species_embed, weight_map)

    def energy_fn(latent_in, weights_in, direction_in, envelope_in, env_in):
        return edge_energy(latent_in, weights_in, direction_in, envelope_in, env_in, pair_mask, scalar_map, energy_out)
    pair_total, energy_pull = jax.vjp(energy_fn, latent, weights, direction, envelope, environment)
    grads = energy_pull(jnp.ones((), jnp.float32))
    return (pair_total, grads[4])

def device_force(extended, own_pos, own_kind, neighbours, environment, ghost_grad, params):
    basis_weight, species_embed, weight_map, scalar_map, energy_out = params
    kind_values = jnp.arange(species_embed.shape[0]).astype(jnp.float32)
    displace, species_pair, pair_mask, safe_index = pair_inputs(extended, own_pos, own_kind, neighbours, kind_values)

    def front(displace_in):
        return edge_front(displace_in, species_pair, basis_weight, species_embed, weight_map)
    outputs, front_pull = jax.vjp(front, displace)
    latent, weights, direction, envelope, moments = outputs

    def energy_fn(latent_in, weights_in, direction_in, envelope_in, env_in):
        return edge_energy(latent_in, weights_in, direction_in, envelope_in, env_in, pair_mask, scalar_map, energy_out)
    pair_total, energy_pull = jax.vjp(energy_fn, latent, weights, direction, envelope, environment)
    grad_latent, grad_weights, grad_direction, grad_envelope, grad_env = energy_pull(jnp.ones((), jnp.float32))
    channels = weights.shape[0]
    sites = own_pos.shape[-1]
    own_count = 27 * sites
    list_width = neighbours.shape[-1]
    far_grad = jnp.take(ghost_grad.reshape(4 * channels, 125 * sites), safe_index, axis=1)
    grad_moments = pair_mask[None, :] * (spread_rows(grad_env, list_width) + flip_signs(channels) * far_grad)
    grad_displace, = front_pull((grad_latent, grad_weights, grad_direction, grad_envelope, grad_moments))
    pushed = jnp.zeros((3, 125 * sites), jnp.float32).at[:, safe_index].add(grad_displace * pair_mask[None, :])
    pulled = -lax.optimization_barrier(jnp.sum(grad_displace.reshape(3, own_count, list_width), axis=2))
    return (pushed.reshape(3, 5, 5, 5, sites), pulled)

def evaluate_all(positions, kind_field, live_field, neigh_dev, params, species_energy):
    pos_dev = to_devices(positions)
    kind_dev = to_devices(kind_field[None])
    grid_x, grid_y, grid_z = (pos_dev.shape[0], pos_dev.shape[1], pos_dev.shape[2])
    count = grid_x * grid_y * grid_z
    sites = positions.shape[-1]
    channels = params[2].shape[1]
    packed = jnp.concatenate([pos_dev, kind_dev], axis=3)
    extended = ghost_window(packed).reshape(count, 4, 5, 5, 5, sites)
    pos_flat = pos_dev.reshape(count, 3, 3, 3, 3, sites)
    kind_flat = kind_dev.reshape(count, 3, 3, 3, sites)
    scattered, centre_sum = lax.map(lambda item: device_front(item[0], item[1], item[2], item[3], params), (extended, pos_flat, kind_flat, neigh_dev))
    folded = owner_fold(scattered.reshape(grid_x, grid_y, grid_z, 4 * channels, 5, 5, 5, sites))
    environment = folded.reshape(count, 4 * channels, 27 * sites) + centre_sum
    pair_totals, grad_env = lax.map(lambda item: device_energy(item[0], item[1], item[2], item[3], item[4], params), (extended, pos_flat, kind_flat, neigh_dev, environment))
    ghost_grad = ghost_window(grad_env.reshape(grid_x, grid_y, grid_z, 4 * channels, 3, 3, 3, sites)).reshape(count, 4 * channels, 5, 5, 5, sites)
    pushed, pulled = lax.map(lambda item: device_force(item[0], item[1], item[2], item[3], item[4], item[5], params), (extended, pos_flat, kind_flat, neigh_dev, environment, ghost_grad))
    gradient = owner_fold(pushed.reshape(grid_x, grid_y, grid_z, 3, 5, 5, 5, sites)).reshape(count, 3, 27 * sites) + pulled
    gradient_regions = to_regions(gradient.reshape(grid_x, grid_y, grid_z, 3, 3, 3, 3, sites))
    force = -gradient_regions * live_field[None]
    kind_values = jnp.arange(species_energy.shape[0]).astype(jnp.float32)
    atom_term = jnp.sum(live_field * lax.optimization_barrier(jnp.sum((kind_field[..., None] == kind_values).astype(jnp.float32) * species_energy, axis=-1)))
    return (force, jnp.sum(pair_totals) + atom_term)

def reference(positions, velocity, species, region_count, neighbours, basis_weight, species_embed, weight_map, scalar_map, energy_out, species_energy):
    params = (basis_weight, species_embed, weight_map, scalar_map, energy_out)
    sites = positions.shape[-1]
    slot_ids = lax.broadcasted_iota(jnp.int32, species.shape, 3)
    live_field = (slot_ids < region_count[..., None]).astype(jnp.float32)
    kind_field = species.astype(jnp.float32)
    grid_x, grid_y, grid_z = (REG_X // 3, REG_Y // 3, REG_Z // 3)
    neigh_dev = neighbours.reshape(grid_x, 3, grid_y, 3, grid_z, 3, sites, neighbours.shape[-1]).transpose(0, 2, 4, 1, 3, 5, 6, 7)
    neigh_dev = neigh_dev.reshape(grid_x * grid_y * grid_z, 3, 3, 3, sites, neighbours.shape[-1])
    force_one, energy_one = evaluate_all(positions, kind_field, live_field, neigh_dev, params, species_energy)
    moved = positions + time_step * velocity + 0.5 * time_step * time_step * inverse_mass(species)[None] * force_one
    force_two, energy_two = evaluate_all(moved, kind_field, live_field, neigh_dev, params, species_energy)
    total_live = jnp.sum(live_field)
    forces = jnp.stack([force_one, force_two])
    energy = jnp.stack([energy_one, energy_two]) / total_live
    return (forces, energy)
```

```python
import functools
import math

import jax
import jax.numpy as jnp
from jax import lax
from jax.experimental import pallas as pl
from jax.experimental.pallas import tpu as pltpu
from jax.sharding import PartitionSpec as P

cutoff = 6.0
env_scale = 0.25
domain_side = 18.0
time_step = 0.15
atom_masses = (1.008, 12.011, 14.007, 15.999, 32.06)

CH = 64
LAT = 128
NB = 8
NSPEC = 5
LIST = 24
USED = 392
ROWS = 400
DEPTH = 512
INNER = 256
OWN = 80
TILES = 52
LANES = 128
POS, KIND, KIND3, NEIGH, VEL, LIVE3, LIVE = 0, 6, 8, 16, 64, 72, 80
MISC = NEIGH + 2 * LIST
F32 = jnp.float32
BF16 = jnp.bfloat16


def mm(a, b):
    return lax.dot_general(a, b, (((1,), (0,)), ((), ())), preferred_element_type=F32)


def mm_nt(a, b):
    return lax.dot_general(a, b, (((1,), (1,)), ((), ())), preferred_element_type=F32)


def split2(v):
    high = v.astype(BF16)
    return high, (v - high.astype(F32)).astype(BF16)


def iota(shape, dim):
    return lax.broadcasted_iota(jnp.int32, shape, dim).astype(F32)


def sigmoid(v):
    return 1.0 / (1.0 + jnp.exp(-v))


def row_coords(row):
    xy = jnp.floor(row * 0.125)
    z = row - 8.0 * xy
    x = jnp.floor((xy + 0.5) * (1.0 / 7.0))
    return x, xy - 7.0 * x, z


def away(x, y, z):
    return jnp.maximum(jnp.maximum(jnp.abs(x - 3.0), jnp.abs(y - 3.0)), jnp.abs(z - 3.0))


def far_coords(x, y, z, entry):
    q = jnp.floor(entry * 0.5)
    a = jnp.floor((q + 0.5) * (1.0 / 25.0))
    ab = jnp.floor((q + 0.5) * (1.0 / 5.0))
    steps = (a, ab - 5.0 * a, q - 5.0 * ab)
    far = [3.0 * jnp.floor((v + 1.5) * (1.0 / 3.0)) + s - 2.0 for v, s in zip((x, y, z), steps)]
    shift = [(jnp.floor((s + 2.5) * (1.0 / 3.0)) - 1.0) * domain_side for s in steps]
    return far, shift, entry - 2.0 * q


def one_hot(index, count, depth):
    hit = (iota((count, LANES), 0) == index).astype(F32).astype(BF16)
    if depth > count:
        hit = jnp.concatenate([hit, jnp.zeros((depth - count, LANES), BF16)], axis=0)
    return hit


def build_pairs(rows_ref, table, off_ref, end_ref, pairs_ref, listed_t):
    shape = (ROWS, LANES)
    lane = iota(shape, 1)
    row = iota(shape, 0)
    x, y, z = row_coords(row)
    entry = rows_ref[0:ROWS]
    in_list = (lane >= NEIGH) & (lane < MISC)
    listed = in_list & (entry >= 0.0) & (z < 6.5) & (row < USED)
    far, _, _ = far_coords(x, y, z, entry)
    nearest = jnp.minimum(away(x, y, z), away(*far))
    kept = (listed & (nearest < 1.5), listed & (nearest > 1.5) & (nearest < 2.5))
    upper = (iota((LANES, LANES), 0) <= iota((LANES, LANES), 1)).astype(F32).astype(BF16)
    ones = jnp.ones((LANES, LANES), BF16)
    below = (iota((ROWS, DEPTH), 1) < iota((ROWS, DEPTH), 0)).astype(F32).astype(BF16)
    start = jnp.int32(0)
    counts = []
    for keep in kept:
        keep = keep.astype(F32)
        keep16 = keep.astype(BF16)
        rank = mm(keep16, upper) * keep
        count = mm(keep16, ones)
        padded = jnp.concatenate(
            [count.astype(BF16), jnp.zeros((DEPTH - ROWS, LANES), BF16)], axis=0
        )
        offset = mm(below, padded)
        end = offset + count
        off_ref[...] = offset
        end_ref[...] = end
        total = jnp.max(end)
        high = jnp.floor(offset * (1.0 / 256.0))
        fields = jnp.where(in_list, rank, 0.0)
        for at, value in enumerate((high, offset - 256.0 * high, x, y, z)):
            fields = jnp.where(lane == float(MISC + at), value, fields)
        fields = jnp.concatenate([fields, jnp.zeros((DEPTH - ROWS, LANES), F32)], axis=0)
        fields_t = jnp.transpose(fields)
        table[0 : 2 * LIST] = listed_t
        table[2 * LIST : 4 * LIST + 16] = fields_t[NEIGH : MISC + 16].astype(BF16)
        tiles = (total.astype(jnp.int32) + (LANES - 1)) // LANES

        def body(k, carry, start=start, total=total):
            place = iota((1, LANES), 1) + (k * LANES).astype(F32)
            hit = (off_ref[...] <= place) & (end_ref[...] > place)
            hit = hit.astype(F32).astype(BF16)
            hit = jnp.concatenate([hit, jnp.zeros((DEPTH - ROWS, LANES), BF16)], axis=0)
            got = mm(table[...], hit)
            misc = got[4 * LIST :]
            wanted = place - (256.0 * misc[0:1] + misc[1:2]) + 1.0
            chosen = (got[2 * LIST : 4 * LIST] == wanted).astype(F32)
            entry = jnp.sum(chosen * got[0 : 2 * LIST], axis=0, keepdims=True)
            slot = jnp.sum(chosen[LIST:], axis=0, keepdims=True)
            x, y, z = misc[2:3], misc[3:4], misc[4:5]
            far, shift, far_slot = far_coords(x, y, z, entry)
            valid = place < total
            away_i, away_j = away(x, y, z), away(*far)

            def where(flag, value):
                return jnp.where(flag, value, -1.0)

            def region(c):
                return (c[0] * 7.0 + c[1]) * 8.0 + c[2]

            def inner(c, s):
                return (((c[0] - 1.0) * 5.0 + (c[1] - 1.0)) * 5.0 + (c[2] - 1.0)) * 2.0 + s

            def own(c):
                return ((c[0] - 2.0) * 3.0 + (c[1] - 2.0)) * 8.0 + c[2]

            near = (x, y, z)
            lines = [
                where(valid, region(near)),
                slot,
                where(valid, region(far)),
                far_slot,
                where(valid & (away_i < 2.5), inner(near, slot)),
                where(valid & (away_j < 2.5), inner(far, far_slot)),
                where(valid & (away_i < 1.5), own(near)),
                where(valid & (away_j < 1.5), own(far)),
                valid.astype(F32),
                *shift,
                (valid & (away_i < 1.5)).astype(F32),
                jnp.zeros((3, LANES), F32),
            ]
            pairs_ref[start + k] = jnp.concatenate(lines, axis=0)
            return carry

        lax.fori_loop(0, tiles, body, jnp.int32(0))
        start = start + tiles
        counts.append(start)
    return counts


def turns(radius):
    part = radius * (1.0 / 12.0)
    part = part - jnp.floor(part + 0.5)
    half = part * math.pi
    sq = half * half
    s = jnp.full_like(sq, -1.0 / 39916800.0)
    for c in (1.0 / 362880.0, -1.0 / 5040.0, 1.0 / 120.0, -1.0 / 6.0, 1.0):
        s = s * sq + c
    s = s * half
    c = jnp.full_like(sq, 1.0 / 479001600.0)
    for k in (-1.0 / 3628800.0, 1.0 / 40320.0, -1.0 / 720.0, 1.0 / 24.0, -0.5, 1.0):
        c = c * sq + k
    return 2.0 * s * c, 1.0 - 2.0 * s * s


def evaluate(refs, scratch, counts, own_out):
    pos_t, pairs_ref, w1t, w1, wmt, wm, smt, sm, eo = refs
    env_ref, envs_ref, grad_ref, geo_ref, lat_ref, slope_ref, h_ref, wb_ref, hp_ref, en_ref = (
        scratch
    )
    front, every = counts
    norm = math.sqrt(2.0 / cutoff)

    env_ref[...] = jnp.zeros(env_ref.shape, F32)
    grad_ref[...] = jnp.zeros(grad_ref.shape, F32)
    en_ref[...] = jnp.zeros(en_ref.shape, F32)
    own_out[...] = jnp.zeros(own_out.shape, F32)

    def gathered(index, slot):
        got = mm(pos_t[...], one_hot(index, ROWS, DEPTH))
        full = got[0:8] + got[8:16] + got[16:24]
        second = slot > 0.5
        point = jnp.where(second, full[3:6], full[0:3])
        return point, jnp.where(second, full[7:8], full[6:7])

    def stage_one(t, carry):
        pair = pairs_ref[t]
        valid = pair[8:9]
        near, near_kind = gathered(pair[0:1], pair[1:2])
        far, far_kind = gathered(pair[2:3], pair[3:4])
        d = far - near + pair[9:12]
        square = jnp.sum(d * d, axis=0, keepdims=True)
        square = jnp.where(valid > 0.5, square, 1.0)
        radius = jnp.sqrt(square)
        inverse = 1.0 / radius
        u = d * inverse
        y = jnp.minimum(radius * (1.0 / cutoff), 1.0)
        y2 = y * y
        y5 = y2 * y2 * y
        f = 1.0 + y5 * y * (-28.0 + y * (48.0 - 21.0 * y))
        fd = y5 * (-168.0 + y * (336.0 - 168.0 * y)) * (1.0 / cutoff)
        sin1, cos1 = turns(radius)
        sines, cosines = [jnp.zeros_like(sin1), sin1], [jnp.ones_like(cos1), cos1]
        for _ in range(NB - 1):
            sines.append(2.0 * cos1 * sines[-1] - sines[-2])
            cosines.append(2.0 * cos1 * cosines[-1] - cosines[-2])
        basis = [norm * inverse * s for s in sines[1:]]
        slope = [
            norm * (k * (math.pi / cutoff)) * inverse * c - inverse * b
            for k, (c, b) in enumerate(zip(cosines[1:], basis), 1)
        ]
        kinds = [
            (near_kind == float(k)).astype(F32) + (far_kind == float(k)).astype(F32)
            for k in range(NSPEC)
        ]
        feats = jnp.concatenate(basis + kinds + [jnp.zeros((3, LANES), F32)], axis=0)
        geo_ref[t] = jnp.concatenate(
            [u, inverse, f, fd, jnp.zeros((2, LANES), F32)] + slope, axis=0
        )
        pre = mm(w1t[...], feats.astype(BF16))
        gate = sigmoid(pre)
        lat = (pre * gate).astype(BF16)
        lat_ref[t] = lat
        slope_ref[t] = gate * (1.0 + pre * (1.0 - gate))
        h = mm(wmt[...], lat)
        h_ref[t] = h
        w = h * (f * valid)
        hit_i = one_hot(pair[4:5], INNER, INNER)
        hit_j = one_hot(pair[5:6], INNER, INNER)
        high, low = split2(
            jnp.concatenate([w, w * u[0:1], w * u[1:2], w * u[2:3]], axis=0)
        )
        moments = jnp.concatenate([high, low], axis=1)
        plus, minus = hit_i + hit_j, hit_i - hit_j
        env_ref[0:CH] += mm_nt(moments[0:CH], jnp.concatenate([plus, plus], axis=1))
        env_ref[CH:] += mm_nt(moments[CH:], jnp.concatenate([minus, minus], axis=1))
        return carry

    lax.fori_loop(0, every, stage_one, jnp.int32(0))
    high, low = split2(env_ref[...])
    envs_ref[...] = jnp.concatenate([high, low], axis=1)

    def stage_two(t, carry):
        pair = pairs_ref[t]
        geo = geo_ref[t]
        valid = pair[8:9]
        u = geo[0:3]
        f = geo[4:5]
        hit = one_hot(pair[4:5], INNER, INNER)
        env = mm(envs_ref[...], jnp.concatenate([hit, hit], axis=0))
        aligned = (
            env[0:CH]
            + u[0:1] * env[CH : 2 * CH]
            + u[1:2] * env[2 * CH : 3 * CH]
            + u[2:3] * env[3 * CH :]
        )
        w = h_ref[t] * (f * valid)
        coupling = (env_scale * w * aligned).astype(BF16)
        arg = lat_ref[t].astype(F32) + mm(smt[...], coupling)
        gate = sigmoid(arg)
        hidden = arg * gate
        dotted = jnp.sum(hidden * eo[...], axis=0, keepdims=True)
        en_ref[0:1] += f * dotted * pair[12:13]
        arg_bar = (f * valid) * eo[...] * (gate * (1.0 + arg * (1.0 - gate)))
        arg_bar = arg_bar.astype(BF16)
        hp_ref[t] = arg_bar
        c_bar = mm(sm[...], arg_bar).astype(BF16).astype(F32)
        wb_ref[t] = env_scale * aligned * c_bar
        al_bar = env_scale * w * c_bar
        geo_ref[t, 6:7] = dotted * valid
        u_bar = [
            jnp.sum(al_bar * env[(k + 1) * CH : (k + 2) * CH], axis=0, keepdims=True)
            for k in range(3)
        ]
        pairs_ref[t, 13:16] = jnp.concatenate(u_bar, axis=0)
        high, low = split2(
            jnp.concatenate([al_bar, al_bar * u[0:1], al_bar * u[1:2], al_bar * u[2:3]], axis=0)
        )
        grad_ref[...] += mm_nt(
            jnp.concatenate([high, low], axis=1), jnp.concatenate([hit, hit], axis=1)
        )
        return carry

    lax.fori_loop(0, every, stage_two, jnp.int32(0))
    high, low = split2(grad_ref[...])
    envs_ref[...] = jnp.concatenate([high, low], axis=1)

    def stage_three(t, carry):
        pair = pairs_ref[t]
        geo = geo_ref[t]
        valid = pair[8:9]
        u, inverse, f, fd = geo[0:3], geo[3:4], geo[4:5], geo[5:6]
        hit_i = one_hot(pair[4:5], INNER, INNER)
        hit_j = one_hot(pair[5:6], INNER, INNER)
        plus, minus = hit_i + hit_j, hit_i - hit_j
        grad = envs_ref[...]
        g0 = mm(grad[0:CH], jnp.concatenate([plus, plus], axis=0))
        gv = mm(grad[CH:], jnp.concatenate([minus, minus], axis=0))
        parts = [gv[k * CH : (k + 1) * CH] for k in range(3)]
        h = h_ref[t]
        w = h * (f * valid)
        w_bar = wb_ref[t] + g0 + u[0:1] * parts[0] + u[1:2] * parts[1] + u[2:3] * parts[2]
        u_bar = pair[13:16] + jnp.concatenate(
            [jnp.sum(w * part, axis=0, keepdims=True) for part in parts], axis=0
        )
        f_bar = geo[6:7] + jnp.sum(h * w_bar, axis=0, keepdims=True)
        h_bar = (w_bar * (f * valid)).astype(BF16)
        lat_bar = (mm(wm[...], h_bar).astype(BF16) + hp_ref[t]).astype(F32)
        pre_bar = (lat_bar * slope_ref[t]).astype(BF16)
        basis_bar = mm(w1[...], pre_bar)[0:NB].astype(BF16).astype(F32)
        r_bar = jnp.sum(basis_bar * geo[8:16], axis=0, keepdims=True) + f_bar * fd
        along = jnp.sum(u * u_bar, axis=0, keepdims=True)
        d_bar = (r_bar * u + (u_bar - u * along) * inverse) * valid
        blank = jnp.zeros((2, LANES), F32)

        def slotted(values, slot):
            second = slot > 0.5
            return jnp.concatenate(
                [jnp.where(second, 0.0, values), jnp.where(second, values, 0.0), blank], axis=0
            )

        pulls = jnp.concatenate(
            [slotted(d_bar, pair[1:2]), slotted(-d_bar, pair[3:4])], axis=1
        )
        high, low = split2(jnp.concatenate([pulls, jnp.zeros((120, 2 * LANES), F32)], axis=0))
        where = jnp.concatenate([one_hot(pair[6:7], OWN, OWN), one_hot(pair[7:8], OWN, OWN)], axis=1)
        own_out[...] += mm_nt(where, high) + mm_nt(where, low)
        return carry

    lax.fori_loop(0, front, stage_three, jnp.int32(0))


def load_rows(rows_ref, low, own, high):
    rows_ref[0:ROWS] = jnp.zeros((ROWS, LANES), F32)
    for i in range(7):
        for piece, start, width in ((low, 0, 2), (own, 2, 3), (high, 5, 2)):
            for j in range(width):
                at = (i * 7 + start + j) * 8
                rows_ref[at : at + 8] = piece[i, j]


def own_rows(rows_ref):
    return jnp.concatenate(
        [rows_ref[(i * 7 + 2) * 8 : (i * 7 + 5) * 8] for i in range(2, 5)], axis=0
    )


def position_rows(rows_ref, pos_t):
    rows = jnp.concatenate([rows_ref[0:ROWS], jnp.zeros((DEPTH - ROWS, LANES), F32)], axis=0)
    turned = jnp.transpose(rows)
    top = turned[0:8]
    one = top.astype(BF16)
    rest = top - one.astype(F32)
    two = rest.astype(BF16)
    three = (rest - two.astype(F32)).astype(BF16)
    pos_t[...] = jnp.concatenate(
        [one.astype(F32), two.astype(F32), three.astype(F32), jnp.zeros((8, DEPTH), F32)], axis=0
    ).astype(BF16)
    return turned


def energy_rows(pair_energy, atom_energy, live):
    row = iota((8, LANES), 0)
    return jnp.where(row == 0.0, pair_energy, 0.0) + jnp.where(
        row == 1.0, atom_energy, 0.0
    ) + jnp.where(row == 2.0, live, 0.0)


def first_kernel(low, own, high, w1t, w1, wmt, wm, smt, sm, eo, table_energy,
                 force_out, moved_out, energy_out, pairs_ref, counts_ref,
                 rows_ref, table, off_ref, end_ref, pos_t, own_ref, *scratch):
    load_rows(rows_ref, low, own, high)
    turned = position_rows(rows_ref, pos_t)
    front, every = build_pairs(
        rows_ref, table, off_ref, end_ref, pairs_ref, turned[NEIGH:MISC].astype(BF16)
    )
    counts_ref[0] = front
    counts_ref[1] = every
    refs = (pos_t, pairs_ref, w1t, w1, wmt, wm, smt, sm, eo)
    evaluate(refs, scratch, (front, every), own_ref)
    mine = own_rows(rows_ref)
    lane = iota((72, LANES), 1)
    row = iota((72, LANES), 0)
    z = row - 8.0 * jnp.floor(row * 0.125)
    inside = (z > 1.5) & (z < 4.5)
    live3 = pltpu.roll(mine, LANES - LIVE3, 1)
    kind3 = pltpu.roll(mine, LANES - KIND3, 1)
    speed = pltpu.roll(mine, LANES - VEL, 1)
    force = own_ref[0:72] * live3
    force = jnp.where(inside & (lane < 6.0), force, 0.0)
    force_out[...] = force
    inverse_mass = jnp.zeros((72, LANES), F32)
    for k, mass in enumerate(atom_masses):
        inverse_mass = jnp.where(kind3 == float(k), 1.0 / mass, inverse_mass)
    moved = mine + time_step * speed + 0.5 * time_step * time_step * inverse_mass * force
    moved_out[...] = jnp.where(lane < 6.0, moved, jnp.where(lane < 8.0, mine, 0.0))
    live = pltpu.roll(mine, LANES - LIVE + KIND, 1)
    here = inside & (lane > 5.5) & (lane < 7.5)
    live = jnp.where(here, live, 0.0)
    atom = jnp.zeros((72, LANES), F32)
    for k in range(NSPEC):
        atom = jnp.where(mine == float(k), table_energy[k], atom)
    energy_out[...] = energy_rows(
        jnp.sum(scratch[-1][0:1]), jnp.sum(atom * live), jnp.sum(live)
    )


def second_kernel(low, own, high, w1t, w1, wmt, wm, smt, sm, eo, pairs_in, counts_ref, kept_in,
                  force_out, energy_out,
                  rows_ref, pos_t, own_ref, pairs_ref, *scratch):
    load_rows(rows_ref, low, own, high)
    position_rows(rows_ref, pos_t)
    front, every = counts_ref[0], counts_ref[1]
    pairs_ref[...] = pairs_in[...]
    refs = (pos_t, pairs_ref, w1t, w1, wmt, wm, smt, sm, eo)
    evaluate(refs, scratch, (front, every), own_ref)
    lane = iota((72, LANES), 1)
    row = iota((72, LANES), 0)
    z = row - 8.0 * jnp.floor(row * 0.125)
    force = own_ref[0:72] * kept_in[...]
    force_out[...] = jnp.where((z > 1.5) & (z < 4.5) & (lane < 6.0), force, 0.0)
    energy_out[...] = energy_rows(jnp.sum(scratch[-1][0:1]), 0.0, 0.0)


EVAL_SCRATCH = (
    pltpu.VMEM((4 * CH, INNER), F32),
    pltpu.VMEM((4 * CH, 2 * INNER), BF16),
    pltpu.VMEM((4 * CH, INNER), F32),
    pltpu.VMEM((TILES, 16, LANES), F32),
    pltpu.VMEM((TILES, LAT, LANES), BF16),
    pltpu.VMEM((TILES, LAT, LANES), F32),
    pltpu.VMEM((TILES, CH, LANES), F32),
    pltpu.VMEM((TILES, CH, LANES), F32),
    pltpu.VMEM((TILES, LAT, LANES), BF16),
    pltpu.VMEM((8, LANES), F32),
)
PARAMS = pltpu.CompilerParams(vmem_limit_bytes=20 * 2**20)
VM = pl.BlockSpec(memory_space=pltpu.VMEM)
SM = pl.BlockSpec(memory_space=pltpu.SMEM)


def first_call(pieces, weights, table_energy):
    return pl.pallas_call(
        first_kernel,
        name="first",
        out_shape=(
            jax.ShapeDtypeStruct((72, LANES), F32),
            jax.ShapeDtypeStruct((72, LANES), F32),
            jax.ShapeDtypeStruct((8, LANES), F32),
            jax.ShapeDtypeStruct((TILES, 16, LANES), F32),
            jax.ShapeDtypeStruct((2,), jnp.int32),
        ),
        in_specs=[VM] * (len(pieces) + len(weights)) + [SM],
        out_specs=(VM, VM, VM, VM, SM),
        scratch_shapes=(
            pltpu.VMEM((ROWS, LANES), F32),
            pltpu.VMEM((4 * LIST + 16, DEPTH), BF16),
            pltpu.VMEM((ROWS, LANES), F32),
            pltpu.VMEM((ROWS, LANES), F32),
            pltpu.VMEM((32, DEPTH), BF16),
            pltpu.VMEM((OWN, LANES), F32),
            *EVAL_SCRATCH,
        ),
        compiler_params=PARAMS,
    )(*pieces, *weights, table_energy)


def second_call(pieces, weights, pairs, counts, live3):
    return pl.pallas_call(
        second_kernel,
        name="second",
        out_shape=(
            jax.ShapeDtypeStruct((72, LANES), F32),
            jax.ShapeDtypeStruct((8, LANES), F32),
        ),
        in_specs=[VM] * (len(pieces) + len(weights) + 1) + [SM, VM],
        out_specs=(VM, VM),
        scratch_shapes=(
            pltpu.VMEM((ROWS, LANES), F32),
            pltpu.VMEM((32, DEPTH), BF16),
            pltpu.VMEM((OWN, LANES), F32),
            pltpu.VMEM((TILES, 16, LANES), F32),
            *EVAL_SCRATCH,
        ),
        compiler_params=PARAMS,
    )(*pieces, *weights, pairs, counts, live3)


def swap(low_part, high_part, axis):
    count = lax.axis_size(axis)
    forward = [(i, (i + 1) % count) for i in range(count)]
    backward = [(target, source) for source, target in forward]
    return lax.ppermute(high_part, axis, forward), lax.ppermute(low_part, axis, backward)


def spread(rows):
    low, high = swap(rows[:, :, 0:2], rows[:, :, 1:3], "gz")
    rows = jnp.concatenate([low, rows, high, jnp.zeros((3, 3, 1, LANES), F32)], axis=2)
    low, high = swap(rows[0:2], rows[1:3], "gx")
    rows = jnp.concatenate([low, rows, high], axis=0)
    low, high = swap(rows[:, 0:2], rows[:, 1:3], "gy")
    return low, rows, high


def pack(positions, velocity, species, region_count, neighbours):
    slots = lax.broadcasted_iota(jnp.int32, (3, 3, 3, 2), 3)
    live = (slots < region_count[..., None]).astype(F32)
    kind = species.astype(F32)
    lists = neighbours[..., :LIST].astype(F32).reshape(3, 3, 3, 2 * LIST)

    def thrice(v):
        return jnp.broadcast_to(v[..., None], (3, 3, 3, 2, 3)).reshape(3, 3, 3, 6)

    def vectors(v):
        return v.transpose(1, 2, 3, 4, 0).reshape(3, 3, 3, 6)

    def pad(count):
        return jnp.zeros((3, 3, 3, count), F32)

    return jnp.concatenate(
        [vectors(positions), kind, thrice(kind), pad(2), lists, vectors(velocity), pad(2),
         thrice(live), pad(2), live, pad(LANES - LIVE - 2)],
        axis=-1,
    ), thrice(live)


def unpack(force):
    own = force.reshape(3, 3, 8, LANES)[:, :, 2:5, 0:6]
    return own.reshape(3, 3, 3, 2, 3).transpose(4, 0, 1, 2, 3)


def shards(positions, velocity, species, region_count, neighbours,
           basis_weight, species_embed, weight_map, scalar_map, energy_out, species_energy):
    rows, live3 = pack(positions, velocity, species, region_count, neighbours)
    w1 = jnp.concatenate([basis_weight, species_embed, jnp.zeros((3, LAT), BF16)], axis=0)
    weights = (
        w1.T,
        w1,
        weight_map.T,
        weight_map,
        scalar_map.T,
        scalar_map,
        jnp.broadcast_to(energy_out[:, None], (LAT, LANES)),
    )
    live_rows = jnp.pad(live3, ((0, 0), (0, 0), (2, 3), (0, LANES - 6))).reshape(72, LANES)
    force_one, moved, energy_one, pairs, counts = first_call(
        spread(rows), weights, species_energy
    )
    moved = moved.reshape(3, 3, 8, LANES)[:, :, 2:5]
    force_two, energy_two = second_call(spread(moved), weights, pairs, counts, live_rows)
    partial = jnp.concatenate([energy_one[0:3, 0:1], energy_two[0:1, 0:1]], axis=0)
    for axis in ("gz", "gy", "gx"):
        partial = lax.psum(partial, axis)
    energy = jnp.stack([partial[0, 0] + partial[1, 0], partial[3, 0] + partial[1, 0]])
    forces = jnp.stack([unpack(force_one), unpack(force_two)])
    return forces, energy / partial[2, 0]


def solution(mesh):
    placed = (
        P(None, "gx", "gy", "gz", None),
        P(None, "gx", "gy", "gz", None),
        P("gx", "gy", "gz", None),
        P("gx", "gy", "gz"),
        P("gx", "gy", "gz", None, None),
        P(),
        P(),
        P(),
        P(),
        P(),
        P(),
    )
    return jax.shard_map(
        shards,
        mesh=mesh,
        in_specs=placed,
        out_specs=(P(None, None, "gx", "gy", "gz", None), P()),
        check_vma=False,
    )
```

```python
import functools
import math

import jax
import jax.numpy as jnp
from jax import lax
from jax.experimental import pallas as pl
from jax.experimental.pallas import tpu as pltpu
from jax.sharding import PartitionSpec as P

cutoff = 6.0
env_scale = 0.25
domain_side = 18.0
time_step = 0.15
atom_masses = (1.008, 12.011, 14.007, 15.999, 32.06)

CH = 64
LAT = 128
NB = 8
NSPEC = 5
LIST = 24
USED = 392
ROWS = 400
DEPTH = 512
INNER = 256
OWN = 80
TILES = 52
LANES = 128
POS, KIND, KIND3, NEIGH, VEL, LIVE3, LIVE = 0, 6, 8, 16, 64, 72, 80
MISC = NEIGH + 2 * LIST
F32 = jnp.float32
BF16 = jnp.bfloat16


def mm(a, b):
    return lax.dot_general(a, b, (((1,), (0,)), ((), ())), preferred_element_type=F32)


def mm_nt(a, b):
    return lax.dot_general(a, b, (((1,), (1,)), ((), ())), preferred_element_type=F32)


def split2(v):
    high = v.astype(BF16)
    return high, (v - high.astype(F32)).astype(BF16)


def iota(shape, dim):
    return lax.broadcasted_iota(jnp.int32, shape, dim).astype(F32)


def sigmoid(v):
    return 1.0 / (1.0 + jnp.exp(-v))


def row_coords(row):
    xy = jnp.floor(row * 0.125)
    z = row - 8.0 * xy
    x = jnp.floor((xy + 0.5) * (1.0 / 7.0))
    return x, xy - 7.0 * x, z


def away(x, y, z):
    return jnp.maximum(jnp.maximum(jnp.abs(x - 3.0), jnp.abs(y - 3.0)), jnp.abs(z - 3.0))


def far_coords(x, y, z, entry):
    q = jnp.floor(entry * 0.5)
    a = jnp.floor((q + 0.5) * (1.0 / 25.0))
    ab = jnp.floor((q + 0.5) * (1.0 / 5.0))
    steps = (a, ab - 5.0 * a, q - 5.0 * ab)
    far = [3.0 * jnp.floor((v + 1.5) * (1.0 / 3.0)) + s - 2.0 for v, s in zip((x, y, z), steps)]
    shift = [(jnp.floor((s + 2.5) * (1.0 / 3.0)) - 1.0) * domain_side for s in steps]
    return far, shift, entry - 2.0 * q


def one_hot(index, count, depth):
    hit = (iota((count, LANES), 0) == index).astype(F32).astype(BF16)
    if depth > count:
        hit = jnp.concatenate([hit, jnp.zeros((depth - count, LANES), BF16)], axis=0)
    return hit


def build_pairs(rows_ref, table, off_ref, end_ref, pairs_ref, listed_t):
    shape = (ROWS, LANES)
    lane = iota(shape, 1)
    row = iota(shape, 0)
    x, y, z = row_coords(row)
    entry = rows_ref[0:ROWS]
    in_list = (lane >= NEIGH) & (lane < MISC)
    listed = in_list & (entry >= 0.0) & (z < 6.5) & (row < USED)
    far, _, _ = far_coords(x, y, z, entry)
    nearest = jnp.minimum(away(x, y, z), away(*far))
    kept = (listed & (nearest < 1.5), listed & (nearest > 1.5) & (nearest < 2.5))
    upper = (iota((LANES, LANES), 0) <= iota((LANES, LANES), 1)).astype(F32).astype(BF16)
    ones = jnp.ones((LANES, LANES), BF16)
    below = (iota((ROWS, DEPTH), 1) < iota((ROWS, DEPTH), 0)).astype(F32).astype(BF16)
    start = jnp.int32(0)
    counts = []
    for keep in kept:
        keep = keep.astype(F32)
        keep16 = keep.astype(BF16)
        rank = mm(keep16, upper) * keep
        count = mm(keep16, ones)
        padded = jnp.concatenate(
            [count.astype(BF16), jnp.zeros((DEPTH - ROWS, LANES), BF16)], axis=0
        )
        offset = mm(below, padded)
        end = offset + count
        off_ref[...] = offset
        end_ref[...] = end
        total = jnp.max(end)
        high = jnp.floor(offset * (1.0 / 256.0))
        fields = jnp.where(in_list, rank, 0.0)
        for at, value in enumerate((high, offset - 256.0 * high, x, y, z)):
            fields = jnp.where(lane == float(MISC + at), value, fields)
        fields = jnp.concatenate([fields, jnp.zeros((DEPTH - ROWS, LANES), F32)], axis=0)
        fields_t = jnp.transpose(fields)
        table[0 : 2 * LIST] = listed_t
        table[2 * LIST : 4 * LIST + 16] = fields_t[NEIGH : MISC + 16].astype(BF16)
        tiles = (total.astype(jnp.int32) + (LANES - 1)) // LANES

        def body(k, carry, start=start, total=total):
            place = iota((1, LANES), 1) + (k * LANES).astype(F32)
            hit = (off_ref[...] <= place) & (end_ref[...] > place)
            hit = hit.astype(F32).astype(BF16)
            hit = jnp.concatenate([hit, jnp.zeros((DEPTH - ROWS, LANES), BF16)], axis=0)
            got = mm(table[...], hit)
            misc = got[4 * LIST :]
            wanted = place - (256.0 * misc[0:1] + misc[1:2]) + 1.0
            chosen = (got[2 * LIST : 4 * LIST] == wanted).astype(F32)
            entry = jnp.sum(chosen * got[0 : 2 * LIST], axis=0, keepdims=True)
            slot = jnp.sum(chosen[LIST:], axis=0, keepdims=True)
            x, y, z = misc[2:3], misc[3:4], misc[4:5]
            far, shift, far_slot = far_coords(x, y, z, entry)
            valid = place < total
            away_i, away_j = away(x, y, z), away(*far)

            def where(flag, value):
                return jnp.where(flag, value, -1.0)

            def region(c):
                return (c[0] * 7.0 + c[1]) * 8.0 + c[2]

            def inner(c, s):
                return (((c[0] - 1.0) * 5.0 + (c[1] - 1.0)) * 5.0 + (c[2] - 1.0)) * 2.0 + s

            def own(c):
                return ((c[0] - 2.0) * 3.0 + (c[1] - 2.0)) * 8.0 + c[2]

            near = (x, y, z)
            lines = [
                where(valid, region(near)),
                slot,
                where(valid, region(far)),
                far_slot,
                where(valid & (away_i < 2.5), inner(near, slot)),
                where(valid & (away_j < 2.5), inner(far, far_slot)),
                where(valid & (away_i < 1.5), own(near)),
                where(valid & (away_j < 1.5), own(far)),
                valid.astype(F32),
                *shift,
                (valid & (away_i < 1.5)).astype(F32),
                jnp.zeros((3, LANES), F32),
            ]
            pairs_ref[start + k] = jnp.concatenate(lines, axis=0)
            return carry

        lax.fori_loop(0, tiles, body, jnp.int32(0))
        start = start + tiles
        counts.append(start)
    return counts


def turns(radius):
    part = radius * (1.0 / 12.0)
    part = part - jnp.floor(part + 0.5)
    half = part * math.pi
    sq = half * half
    s = jnp.full_like(sq, -1.0 / 39916800.0)
    for c in (1.0 / 362880.0, -1.0 / 5040.0, 1.0 / 120.0, -1.0 / 6.0, 1.0):
        s = s * sq + c
    s = s * half
    c = jnp.full_like(sq, 1.0 / 479001600.0)
    for k in (-1.0 / 3628800.0, 1.0 / 40320.0, -1.0 / 720.0, 1.0 / 24.0, -0.5, 1.0):
        c = c * sq + k
    return 2.0 * s * c, 1.0 - 2.0 * s * s


def evaluate(refs, scratch, counts, own_out):
    pos_t, pairs_ref, w1t, w1, wmt, wm, smt, sm, eo = refs
    env_ref, envs_ref, grad_ref, geo_ref, lat_ref, slope_ref, h_ref, wb_ref, hp_ref, en_ref = (
        scratch
    )
    front, every = counts
    norm = math.sqrt(2.0 / cutoff)

    env_ref[...] = jnp.zeros(env_ref.shape, F32)
    grad_ref[...] = jnp.zeros(grad_ref.shape, F32)
    en_ref[...] = jnp.zeros(en_ref.shape, F32)
    own_out[...] = jnp.zeros(own_out.shape, F32)

    def gathered(index, slot):
        got = mm(pos_t[...], one_hot(index, ROWS, DEPTH))
        full = got[0:8] + got[8:16] + got[16:24]
        second = slot > 0.5
        point = jnp.where(second, full[3:6], full[0:3])
        return point, jnp.where(second, full[7:8], full[6:7])

    def stage_one(t, carry):
        pair = pairs_ref[t]
        valid = pair[8:9]
        near, near_kind = gathered(pair[0:1], pair[1:2])
        far, far_kind = gathered(pair[2:3], pair[3:4])
        d = far - near + pair[9:12]
        square = jnp.sum(d * d, axis=0, keepdims=True)
        square = jnp.where(valid > 0.5, square, 1.0)
        radius = jnp.sqrt(square)
        inverse = 1.0 / radius
        u = d * inverse
        y = jnp.minimum(radius * (1.0 / cutoff), 1.0)
        y2 = y * y
        y5 = y2 * y2 * y
        f = 1.0 + y5 * y * (-28.0 + y * (48.0 - 21.0 * y))
        fd = y5 * (-168.0 + y * (336.0 - 168.0 * y)) * (1.0 / cutoff)
        sin1, cos1 = turns(radius)
        sines, cosines = [jnp.zeros_like(sin1), sin1], [jnp.ones_like(cos1), cos1]
        for _ in range(NB - 1):
            sines.append(2.0 * cos1 * sines[-1] - sines[-2])
            cosines.append(2.0 * cos1 * cosines[-1] - cosines[-2])
        basis = [norm * inverse * s for s in sines[1:]]
        slope = [
            norm * (k * (math.pi / cutoff)) * inverse * c - inverse * b
            for k, (c, b) in enumerate(zip(cosines[1:], basis), 1)
        ]
        kinds = [
            (near_kind == float(k)).astype(F32) + (far_kind == float(k)).astype(F32)
            for k in range(NSPEC)
        ]
        feats = jnp.concatenate(basis + kinds + [jnp.zeros((3, LANES), F32)], axis=0)
        geo_ref[t] = jnp.concatenate(
            [u, inverse, f, fd, jnp.zeros((2, LANES), F32)] + slope, axis=0
        )
        pre = mm(w1t[...], feats.astype(BF16))
        gate = sigmoid(pre)
        lat = (pre * gate).astype(BF16)
        lat_ref[t] = lat
        slope_ref[t] = gate * (1.0 + pre * (1.0 - gate))
        h = mm(wmt[...], lat)
        h_ref[t] = h
        w = h * (f * valid)
        hit_i = one_hot(pair[4:5], INNER, INNER)
        hit_j = one_hot(pair[5:6], INNER, INNER)
        high, low = split2(
            jnp.concatenate([w, w * u[0:1], w * u[1:2], w * u[2:3]], axis=0)
        )
        moments = jnp.concatenate([high, low], axis=1)
        plus, minus = hit_i + hit_j, hit_i - hit_j
        env_ref[0:CH] += mm_nt(moments[0:CH], jnp.concatenate([plus, plus], axis=1))
        env_ref[CH:] += mm_nt(moments[CH:], jnp.concatenate([minus, minus], axis=1))
        return carry

    lax.fori_loop(0, every, stage_one, jnp.int32(0))
    high, low = split2(env_ref[...])
    envs_ref[...] = jnp.concatenate([high, low], axis=1)

    def stage_two(t, carry):
        pair = pairs_ref[t]
        geo = geo_ref[t]
        valid = pair[8:9]
        u = geo[0:3]
        f = geo[4:5]
        hit = one_hot(pair[4:5], INNER, INNER)
        env = mm(envs_ref[...], jnp.concatenate([hit, hit], axis=0))
        aligned = (
            env[0:CH]
            + u[0:1] * env[CH : 2 * CH]
            + u[1:2] * env[2 * CH : 3 * CH]
            + u[2:3] * env[3 * CH :]
        )
        w = h_ref[t] * (f * valid)
        coupling = (env_scale * w * aligned).astype(BF16)
        arg = lat_ref[t].astype(F32) + mm(smt[...], coupling)
        gate = sigmoid(arg)
        hidden = arg * gate
        dotted = jnp.sum(hidden * eo[...], axis=0, keepdims=True)
        en_ref[0:1] += f * dotted * pair[12:13]
        arg_bar = (f * valid) * eo[...] * (gate * (1.0 + arg * (1.0 - gate)))
        arg_bar = arg_bar.astype(BF16)
        hp_ref[t] = arg_bar
        c_bar = mm(sm[...], arg_bar).astype(BF16).astype(F32)
        wb_ref[t] = env_scale * aligned * c_bar
        al_bar = env_scale * w * c_bar
        geo_ref[t, 6:7] = dotted * valid
        u_bar = [
            jnp.sum(al_bar * env[(k + 1) * CH : (k + 2) * CH], axis=0, keepdims=True)
            for k in range(3)
        ]
        pairs_ref[t, 13:16] = jnp.concatenate(u_bar, axis=0)
        high, low = split2(
            jnp.concatenate([al_bar, al_bar * u[0:1], al_bar * u[1:2], al_bar * u[2:3]], axis=0)
        )
        grad_ref[...] += mm_nt(
            jnp.concatenate([high, low], axis=1), jnp.concatenate([hit, hit], axis=1)
        )
        return carry

    lax.fori_loop(0, every, stage_two, jnp.int32(0))
    high, low = split2(grad_ref[...])
    envs_ref[...] = jnp.concatenate([high, low], axis=1)

    def stage_three(t, carry):
        pair = pairs_ref[t]
        geo = geo_ref[t]
        valid = pair[8:9]
        u, inverse, f, fd = geo[0:3], geo[3:4], geo[4:5], geo[5:6]
        hit_i = one_hot(pair[4:5], INNER, INNER)
        hit_j = one_hot(pair[5:6], INNER, INNER)
        plus, minus = hit_i + hit_j, hit_i - hit_j
        grad = envs_ref[...]
        g0 = mm(grad[0:CH], jnp.concatenate([plus, plus], axis=0))
        gv = mm(grad[CH:], jnp.concatenate([minus, minus], axis=0))
        parts = [gv[k * CH : (k + 1) * CH] for k in range(3)]
        h = h_ref[t]
        w = h * (f * valid)
        w_bar = wb_ref[t] + g0 + u[0:1] * parts[0] + u[1:2] * parts[1] + u[2:3] * parts[2]
        u_bar = pair[13:16] + jnp.concatenate(
            [jnp.sum(w * part, axis=0, keepdims=True) for part in parts], axis=0
        )
        f_bar = geo[6:7] + jnp.sum(h * w_bar, axis=0, keepdims=True)
        h_bar = (w_bar * (f * valid)).astype(BF16)
        lat_bar = (mm(wm[...], h_bar).astype(BF16) + hp_ref[t]).astype(F32)
        pre_bar = (lat_bar * slope_ref[t]).astype(BF16)
        basis_bar = mm(w1[...], pre_bar)[0:NB].astype(BF16).astype(F32)
        r_bar = jnp.sum(basis_bar * geo[8:16], axis=0, keepdims=True) + f_bar * fd
        along = jnp.sum(u * u_bar, axis=0, keepdims=True)
        d_bar = (r_bar * u + (u_bar - u * along) * inverse) * valid
        blank = jnp.zeros((2, LANES), F32)

        def slotted(values, slot):
            second = slot > 0.5
            return jnp.concatenate(
                [jnp.where(second, 0.0, values), jnp.where(second, values, 0.0), blank], axis=0
            )

        pulls = jnp.concatenate(
            [slotted(d_bar, pair[1:2]), slotted(-d_bar, pair[3:4])], axis=1
        )
        high, low = split2(jnp.concatenate([pulls, jnp.zeros((120, 2 * LANES), F32)], axis=0))
        where = jnp.concatenate([one_hot(pair[6:7], OWN, OWN), one_hot(pair[7:8], OWN, OWN)], axis=1)
        own_out[...] += mm_nt(where, high) + mm_nt(where, low)
        return carry

    lax.fori_loop(0, front, stage_three, jnp.int32(0))


def load_rows(rows_ref, low, own, high):
    rows_ref[0:ROWS] = jnp.zeros((ROWS, LANES), F32)
    for i in range(7):
        for piece, start, width in ((low, 0, 2), (own, 2, 3), (high, 5, 2)):
            for j in range(width):
                at = (i * 7 + start + j) * 8
                rows_ref[at : at + 8] = piece[i, j]


def own_rows(rows_ref):
    return jnp.concatenate(
        [rows_ref[(i * 7 + 2) * 8 : (i * 7 + 5) * 8] for i in range(2, 5)], axis=0
    )


def position_rows(rows_ref, pos_t):
    rows = jnp.concatenate([rows_ref[0:ROWS], jnp.zeros((DEPTH - ROWS, LANES), F32)], axis=0)
    turned = jnp.transpose(rows)
    top = turned[0:8]
    one = top.astype(BF16)
    rest = top - one.astype(F32)
    two = rest.astype(BF16)
    three = (rest - two.astype(F32)).astype(BF16)
    pos_t[...] = jnp.concatenate(
        [one.astype(F32), two.astype(F32), three.astype(F32), jnp.zeros((8, DEPTH), F32)], axis=0
    ).astype(BF16)
    return turned


def energy_row(first, second, live):
    lane = iota((1, LANES), 1)
    return jnp.where(lane == 0.0, first, 0.0) + jnp.where(lane == 1.0, second, 0.0) + jnp.where(
        lane == 2.0, live, 0.0
    )


def first_kernel(low, own, high, w1t, w1, wmt, wm, smt, sm, eo, table_energy,
                 force_out, moved_out, energy_out, pairs_ref, counts_ref,
                 rows_ref, table, off_ref, end_ref, pos_t, own_ref, *scratch):
    load_rows(rows_ref, low, own, high)
    turned = position_rows(rows_ref, pos_t)
    front, every = build_pairs(
        rows_ref, table, off_ref, end_ref, pairs_ref, turned[NEIGH:MISC].astype(BF16)
    )
    counts_ref[0] = front
    counts_ref[1] = every
    refs = (pos_t, pairs_ref, w1t, w1, wmt, wm, smt, sm, eo)
    evaluate(refs, scratch, (front, every), own_ref)
    mine = own_rows(rows_ref)
    lane = iota((72, LANES), 1)
    row = iota((72, LANES), 0)
    z = row - 8.0 * jnp.floor(row * 0.125)
    inside = (z > 1.5) & (z < 4.5)
    live3 = pltpu.roll(mine, LANES - LIVE3, 1)
    kind3 = pltpu.roll(mine, LANES - KIND3, 1)
    speed = pltpu.roll(mine, LANES - VEL, 1)
    force = own_ref[0:72] * live3
    force = jnp.where(inside & (lane < 6.0), force, 0.0)
    force_out[...] = force
    inverse_mass = jnp.zeros((72, LANES), F32)
    for k, mass in enumerate(atom_masses):
        inverse_mass = jnp.where(kind3 == float(k), 1.0 / mass, inverse_mass)
    moved = mine + time_step * speed + 0.5 * time_step * time_step * inverse_mass * force
    moved_out[...] = jnp.where(lane < 6.0, moved, jnp.where(lane < 8.0, mine, 0.0))
    live = pltpu.roll(mine, LANES - LIVE + KIND, 1)
    here = inside & (lane > 5.5) & (lane < 7.5)
    live = jnp.where(here, live, 0.0)
    atom = jnp.zeros((72, LANES), F32)
    for k in range(NSPEC):
        atom = jnp.where(mine == float(k), table_energy[k], atom)
    atoms = jnp.sum(atom * live)
    energy_out[...] = energy_row(jnp.sum(scratch[-1][0:1]) + atoms, atoms, jnp.sum(live))


def second_kernel(low, own, high, w1t, w1, wmt, wm, smt, sm, eo, pairs_in, counts_ref, kept_in, energy_in,
                  force_out, energy_out,
                  rows_ref, pos_t, own_ref, pairs_ref, *scratch):
    load_rows(rows_ref, low, own, high)
    position_rows(rows_ref, pos_t)
    front, every = counts_ref[0], counts_ref[1]
    pairs_ref[...] = pairs_in[...]
    refs = (pos_t, pairs_ref, w1t, w1, wmt, wm, smt, sm, eo)
    evaluate(refs, scratch, (front, every), own_ref)
    lane = iota((72, LANES), 1)
    row = iota((72, LANES), 0)
    z = row - 8.0 * jnp.floor(row * 0.125)
    force = own_ref[0:72] * kept_in[...]
    force_out[...] = jnp.where((z > 1.5) & (z < 4.5) & (lane < 6.0), force, 0.0)
    energy_out[...] = energy_in[...] + energy_row(0.0, jnp.sum(scratch[-1][0:1]), 0.0)


EVAL_SCRATCH = (
    pltpu.VMEM((4 * CH, INNER), F32),
    pltpu.VMEM((4 * CH, 2 * INNER), BF16),
    pltpu.VMEM((4 * CH, INNER), F32),
    pltpu.VMEM((TILES, 16, LANES), F32),
    pltpu.VMEM((TILES, LAT, LANES), BF16),
    pltpu.VMEM((TILES, LAT, LANES), F32),
    pltpu.VMEM((TILES, CH, LANES), F32),
    pltpu.VMEM((TILES, CH, LANES), F32),
    pltpu.VMEM((TILES, LAT, LANES), BF16),
    pltpu.VMEM((8, LANES), F32),
)
PARAMS = pltpu.CompilerParams(vmem_limit_bytes=20 * 2**20)
VM = pl.BlockSpec(memory_space=pltpu.VMEM)
SM = pl.BlockSpec(memory_space=pltpu.SMEM)


def first_call(pieces, weights, table_energy):
    return pl.pallas_call(
        first_kernel,
        name="first",
        out_shape=(
            jax.ShapeDtypeStruct((72, LANES), F32),
            jax.ShapeDtypeStruct((72, LANES), F32),
            jax.ShapeDtypeStruct((1, LANES), F32),
            jax.ShapeDtypeStruct((TILES, 16, LANES), F32),
            jax.ShapeDtypeStruct((2,), jnp.int32),
        ),
        in_specs=[VM] * (len(pieces) + len(weights)) + [SM],
        out_specs=(VM, VM, VM, VM, SM),
        scratch_shapes=(
            pltpu.VMEM((ROWS, LANES), F32),
            pltpu.VMEM((4 * LIST + 16, DEPTH), BF16),
            pltpu.VMEM((ROWS, LANES), F32),
            pltpu.VMEM((ROWS, LANES), F32),
            pltpu.VMEM((32, DEPTH), BF16),
            pltpu.VMEM((OWN, LANES), F32),
            *EVAL_SCRATCH,
        ),
        compiler_params=PARAMS,
    )(*pieces, *weights, table_energy)


def second_call(pieces, weights, pairs, counts, live3, energy):
    return pl.pallas_call(
        second_kernel,
        name="second",
        out_shape=(
            jax.ShapeDtypeStruct((72, LANES), F32),
            jax.ShapeDtypeStruct((1, LANES), F32),
        ),
        in_specs=[VM] * (len(pieces) + len(weights) + 1) + [SM, VM, VM],
        out_specs=(VM, VM),
        scratch_shapes=(
            pltpu.VMEM((ROWS, LANES), F32),
            pltpu.VMEM((32, DEPTH), BF16),
            pltpu.VMEM((OWN, LANES), F32),
            pltpu.VMEM((TILES, 16, LANES), F32),
            *EVAL_SCRATCH,
        ),
        compiler_params=PARAMS,
    )(*pieces, *weights, pairs, counts, live3, energy)


def swap(low_part, high_part, axis):
    count = lax.axis_size(axis)
    even = lax.axis_index(axis) % 2 == 0
    inner = [(i, i ^ 1) for i in range(count)]
    outer = [(i, (i - 1) % count if i % 2 == 0 else (i + 1) % count) for i in range(count)]
    with jax.named_scope("outer"):
        across = lax.ppermute(jnp.where(even, low_part, high_part), axis, outer)
    with jax.named_scope("inner"):
        within = lax.ppermute(jnp.where(even, high_part, low_part), axis, inner)
    return jnp.where(even, across, within), jnp.where(even, within, across)


def everywhere(row, axes):
    count = math.prod(lax.axis_size(axis) for axis in axes)
    rows = jnp.broadcast_to(row[None], (count, 1, LANES))
    rows = lax.all_to_all(rows, axes, 0, 0, tiled=False)
    return jnp.sum(rows, axis=0)


def spread(rows):
    low, high = swap(rows[:, :, 0:2], rows[:, :, 1:3], "gz")
    rows = jnp.concatenate([low, rows, high, jnp.zeros((3, 3, 1, LANES), F32)], axis=2)
    low, high = swap(rows[0:2], rows[1:3], "gx")
    rows = jnp.concatenate([low, rows, high], axis=0)
    low, high = swap(rows[:, 0:2], rows[:, 1:3], "gy")
    return low, rows, high


def pack(positions, velocity, species, region_count, neighbours):
    slots = lax.broadcasted_iota(jnp.int32, (3, 3, 3, 2), 3)
    live = (slots < region_count[..., None]).astype(F32)
    kind = species.astype(F32)
    lists = neighbours[..., :LIST].astype(F32).reshape(3, 3, 3, 2 * LIST)

    def thrice(v):
        return jnp.broadcast_to(v[..., None], (3, 3, 3, 2, 3)).reshape(3, 3, 3, 6)

    def vectors(v):
        return v.transpose(1, 2, 3, 4, 0).reshape(3, 3, 3, 6)

    def pad(count):
        return jnp.zeros((3, 3, 3, count), F32)

    return jnp.concatenate(
        [vectors(positions), kind, thrice(kind), pad(2), lists, vectors(velocity), pad(2),
         thrice(live), pad(2), live, pad(LANES - LIVE - 2)],
        axis=-1,
    ), thrice(live)


def unpack(force):
    own = force.reshape(3, 3, 8, LANES)[:, :, 2:5, 0:6]
    return own.reshape(3, 3, 3, 2, 3).transpose(4, 0, 1, 2, 3)


def shards(positions, velocity, species, region_count, neighbours,
           basis_weight, species_embed, weight_map, scalar_map, energy_out, species_energy):
    rows, live3 = pack(positions, velocity, species, region_count, neighbours)
    w1 = jnp.concatenate([basis_weight, species_embed, jnp.zeros((3, LAT), BF16)], axis=0)
    weights = (
        w1.T,
        w1,
        weight_map.T,
        weight_map,
        scalar_map.T,
        scalar_map,
        jnp.broadcast_to(energy_out[:, None], (LAT, LANES)),
    )
    live_rows = jnp.pad(live3, ((0, 0), (0, 0), (2, 3), (0, LANES - 6))).reshape(72, LANES)
    force_one, moved, energy_one, pairs, counts = first_call(
        spread(rows), weights, species_energy
    )
    moved = moved.reshape(3, 3, 8, LANES)[:, :, 2:5]
    force_two, energies = second_call(
        spread(moved), weights, pairs, counts, live_rows, energy_one
    )
    totals = everywhere(everywhere(energies, ("gx", "gy")), ("gz",))
    forces = jnp.stack([unpack(force_one), unpack(force_two)])
    return forces, totals[0, 0:2] / totals[0, 2]


def solution(mesh):
    placed = (
        P(None, "gx", "gy", "gz", None),
        P(None, "gx", "gy", "gz", None),
        P("gx", "gy", "gz", None),
        P("gx", "gy", "gz"),
        P("gx", "gy", "gz", None, None),
        P(),
        P(),
        P(),
        P(),
        P(),
        P(),
    )
    return jax.shard_map(
        shards,
        mesh=mesh,
        in_specs=placed,
        out_specs=(P(None, None, "gx", "gy", "gz", None), P()),
        check_vma=False,
    )
```

```python
import math

import jax
import jax.numpy as jnp
from jax import lax
from jax.experimental import pallas as pl
from jax.experimental.pallas import tpu as pltpu
from jax.sharding import PartitionSpec as P


cutoff = 6.0
env_scale = 0.25
domain_side = 18.0
time_step = 0.15
atom_masses = (1.008, 12.011, 14.007, 15.999, 32.06)

CH = 64
LAT = 128
NB = 8
NSPEC = 5
LIST = 24
LISTED = 40
USED = 392
ROWS = 400
DEPTH = 512
INNER = 256
OWN = 80
WIDE = 256
TILES = 26
LANES = 128
POS, KIND, VEL, LIVE, NEIGH = 0, 6, 8, 14, 16
MISC = NEIGH + 2 * LIST
F32 = jnp.float32
BF16 = jnp.bfloat16


def mm(a, b):
    return lax.dot_general(a, b, (((1,), (0,)), ((), ())), preferred_element_type=F32)


def mm_nt(a, b):
    return lax.dot_general(a, b, (((1,), (1,)), ((), ())), preferred_element_type=F32)


def split2(v):
    high = v.astype(BF16)
    return high, (v - high.astype(F32)).astype(BF16)


def iota(shape, dim):
    return lax.broadcasted_iota(jnp.int32, shape, dim).astype(F32)


def sigmoid(v):
    return 1.0 / (1.0 + jnp.exp(-v))


def row_coords(row):
    xy = jnp.floor(row * 0.125)
    z = row - 8.0 * xy
    x = jnp.floor((xy + 0.5) * (1.0 / 7.0))
    return x, xy - 7.0 * x, z


def away(x, y, z):
    return jnp.maximum(jnp.maximum(jnp.abs(x - 3.0), jnp.abs(y - 3.0)), jnp.abs(z - 3.0))


def far_coords(x, y, z, entry):
    q = jnp.floor(entry * 0.5)
    a = jnp.floor((q + 0.5) * (1.0 / 25.0))
    ab = jnp.floor((q + 0.5) * (1.0 / 5.0))
    steps = (a, ab - 5.0 * a, q - 5.0 * ab)
    far = [3.0 * jnp.floor((v + 1.5) * (1.0 / 3.0)) + s - 2.0 for v, s in zip((x, y, z), steps)]
    shift = [(jnp.floor((s + 2.5) * (1.0 / 3.0)) - 1.0) * domain_side for s in steps]
    return far, shift, entry - 2.0 * q


def one_hot(index, count, depth):
    hit = (iota((count, index.shape[1]), 0) == index).astype(F32).astype(BF16)
    return deepen(hit, depth)


def deepen(values, depth):
    more = depth - values.shape[0]
    if more == 0:
        return values
    return jnp.concatenate([values, jnp.zeros((more, values.shape[1]), values.dtype)], axis=0)


def build_pairs(rows_ref, base_ref, below_ref, table, off_ref, end_ref, pairs_ref, listed_t):
    lane = iota((ROWS, LANES), 1)
    entry = rows_ref[0:ROWS]
    listed = (lane >= NEIGH) & (lane < MISC) & (entry >= 0.0)
    q = jnp.floor(entry * 0.5)
    a = jnp.floor((q + 0.5) * (1.0 / 25.0))
    ab = jnp.floor((q + 0.5) * (1.0 / 5.0))
    far = jnp.maximum(jnp.abs(base_ref[0] + a), jnp.abs(base_ref[1] + (ab - 5.0 * a)))
    far = jnp.maximum(far, jnp.abs(base_ref[2] + (q - 5.0 * ab)))
    nearest = jnp.where(listed, jnp.minimum(base_ref[3], far), 9.0)
    kept = (nearest < 1.5, (nearest > 1.5) & (nearest < 2.5))
    upto = iota((2 * LIST, LANES), 0) + NEIGH
    place = iota((2 * LIST, LANES), 1)
    keys = (place <= upto).astype(F32) + (place < upto).astype(F32)
    keys = keys.astype(BF16)
    ones = jnp.ones((LANES, LANES), BF16)
    cx, cy, cz = row_coords(iota((1, DEPTH), 1))
    first = jnp.float32(0.0)
    totals = []
    for keep in kept:
        keep16 = deepen(keep.astype(F32).astype(BF16), DEPTH)
        key_t = mm_nt(keys, keep16)
        count = mm(keep16, ones)
        count_t = mm_nt(ones[0:16], keep16)
        below = below_ref[...]
        offset = mm(below, count.astype(BF16)) + first
        offset_t = mm_nt(count_t.astype(BF16), below)[0:1] + first
        end = offset + count[0:ROWS]
        off_ref[...] = offset
        end_ref[...] = end
        total = jnp.max(end)
        offset_t = jnp.concatenate([offset_t, jnp.zeros((1, DEPTH - ROWS), F32)], axis=1)
        high = jnp.floor(offset_t * (1.0 / 256.0))
        misc = jnp.concatenate(
            [high, offset_t - 256.0 * high, cx, cy, cz, jnp.zeros((11, DEPTH), F32)], axis=0
        )
        table[0 : 2 * LIST] = listed_t
        table[2 * LIST : 4 * LIST] = key_t.astype(BF16)
        table[4 * LIST :] = misc.astype(BF16)

        def body(k, carry, first=first, total=total):
            place = iota((1, WIDE), 1) + (k * WIDE).astype(F32)
            offset = off_ref[...]
            end = end_ref[...]
            hit = jnp.concatenate(
                [
                    ((offset <= part) & (end > part)).astype(F32).astype(BF16)
                    for part in (place[:, 0:LANES], place[:, LANES:])
                ],
                axis=1,
            )
            got = mm(table[...], deepen(hit, DEPTH))
            misc = got[4 * LIST :]
            wanted = 2.0 * (place - (256.0 * misc[0:1] + misc[1:2])) + 1.0
            chosen = (got[2 * LIST : 4 * LIST] == wanted).astype(F32)
            entry = jnp.sum(chosen * got[0 : 2 * LIST], axis=0, keepdims=True)
            slot = jnp.sum(chosen[LIST:], axis=0, keepdims=True)
            x, y, z = misc[2:3], misc[3:4], misc[4:5]
            far, shift, far_slot = far_coords(x, y, z, entry)
            valid = place < total
            away_i, away_j = away(x, y, z), away(*far)

            def where(flag, value):
                return jnp.where(flag, value, -1.0)

            def region(c):
                return (c[0] * 7.0 + c[1]) * 8.0 + c[2]

            def inner(c, s):
                return (((c[0] - 1.0) * 5.0 + (c[1] - 1.0)) * 5.0 + (c[2] - 1.0)) * 2.0 + s

            def own(c):
                return ((c[0] - 2.0) * 3.0 + (c[1] - 2.0)) * 8.0 + c[2]

            near = (x, y, z)
            lines = [
                where(valid, region(near)),
                slot,
                where(valid, region(far)),
                far_slot,
                where(valid & (away_i < 2.5), inner(near, slot)),
                where(valid & (away_j < 2.5), inner(far, far_slot)),
                where(valid & (away_i < 1.5), own(near)),
                where(valid & (away_j < 1.5), own(far)),
                valid.astype(F32),
                *shift,
                (valid & (away_i < 1.5)).astype(F32),
                jnp.zeros((3, WIDE), F32),
            ]
            pairs_ref[k] = jnp.where(place < first, pairs_ref[k], jnp.concatenate(lines, axis=0))
            return carry

        last = total.astype(jnp.int32)
        lax.fori_loop(
            first.astype(jnp.int32) // WIDE, (last + (WIDE - 1)) // WIDE, body, jnp.int32(0)
        )
        totals.append((last + (WIDE - 1)) // WIDE)
        first = total
    return totals


def turns(radius):
    part = radius * (1.0 / 12.0)
    part = part - jnp.floor(part + 0.5)
    half = part * math.pi
    sq = half * half
    s = jnp.full_like(sq, -1.0 / 39916800.0)
    for c in (1.0 / 362880.0, -1.0 / 5040.0, 1.0 / 120.0, -1.0 / 6.0, 1.0):
        s = s * sq + c
    s = s * half
    c = jnp.full_like(sq, 1.0 / 479001600.0)
    for k in (-1.0 / 3628800.0, 1.0 / 40320.0, -1.0 / 720.0, 1.0 / 24.0, -0.5, 1.0):
        c = c * sq + k
    return 2.0 * s * c, 1.0 - 2.0 * s * s


def evaluate(refs, scratch, counts, own_out):
    pos_t, pairs_ref, w1t, w1, wmt, wm, smt, sm, eo_ref = refs
    env_ref, envs_ref, grad_ref, geo_ref, lat_ref, slope_ref, h_ref, wb_ref, hp_ref, en_ref = (
        scratch
    )
    front, every = counts
    norm = math.sqrt(2.0 / cutoff)

    def eo():
        return jnp.concatenate([eo_ref[...], eo_ref[...]], axis=1)

    env_ref[...] = jnp.zeros(env_ref.shape, F32)
    grad_ref[...] = jnp.zeros(grad_ref.shape, F32)
    en_ref[...] = jnp.zeros(en_ref.shape, F32)
    own_out[...] = jnp.zeros(own_out.shape, F32)

    def gathered(index, slot):
        got = mm(pos_t[...], one_hot(index, ROWS, DEPTH))
        full = got[0:8] + got[8:16] + got[16:24]
        second = slot > 0.5
        point = jnp.where(second, full[3:6], full[0:3])
        return point, jnp.where(second, full[7:8], full[6:7])

    def stage_one(t, carry):
        pair = pairs_ref[t]
        valid = pair[8:9]
        near, near_kind = gathered(pair[0:1], pair[1:2])
        far, far_kind = gathered(pair[2:3], pair[3:4])
        d = far - near + pair[9:12]
        square = jnp.sum(d * d, axis=0, keepdims=True)
        square = jnp.where(valid > 0.5, square, 1.0)
        radius = jnp.sqrt(square)
        inverse = 1.0 / radius
        u = d * inverse
        y = jnp.minimum(radius * (1.0 / cutoff), 1.0)
        y2 = y * y
        y5 = y2 * y2 * y
        f = 1.0 + y5 * y * (-28.0 + y * (48.0 - 21.0 * y))
        fd = y5 * (-168.0 + y * (336.0 - 168.0 * y)) * (1.0 / cutoff)
        sin1, cos1 = turns(radius)
        sines, cosines = [jnp.zeros_like(sin1), sin1], [jnp.ones_like(cos1), cos1]
        for _ in range(NB - 1):
            sines.append(2.0 * cos1 * sines[-1] - sines[-2])
            cosines.append(2.0 * cos1 * cosines[-1] - cosines[-2])
        basis = [norm * inverse * s for s in sines[1:]]
        slope = [
            norm * (k * (math.pi / cutoff)) * inverse * c - inverse * b
            for k, (c, b) in enumerate(zip(cosines[1:], basis), 1)
        ]
        kinds = [
            (near_kind == float(k)).astype(F32) + (far_kind == float(k)).astype(F32)
            for k in range(NSPEC)
        ]
        feats = jnp.concatenate(basis + kinds + [jnp.zeros((3, WIDE), F32)], axis=0)
        geo_ref[t, 0:16] = jnp.concatenate(
            [u, inverse, f, fd, jnp.zeros((2, WIDE), F32)] + slope, axis=0
        )
        pre = mm(w1t[...], feats.astype(BF16))
        gate = sigmoid(pre)
        lat = (pre * gate).astype(BF16)
        lat_ref[t] = lat
        slope_ref[t] = gate * (1.0 + pre * (1.0 - gate))
        h = mm(wmt[...], lat)
        h_ref[t] = h
        w = h * (f * valid)
        hit_i = one_hot(pair[4:5], INNER, INNER)
        hit_j = one_hot(pair[5:6], INNER, INNER)
        high, low = split2(
            jnp.concatenate([w, w * u[0:1], w * u[1:2], w * u[2:3]], axis=0)
        )
        moments = jnp.concatenate([high, low], axis=1)
        plus, minus = hit_i + hit_j, hit_i - hit_j
        env_ref[0:CH] += mm_nt(moments[0:CH], jnp.concatenate([plus, plus], axis=1))
        env_ref[CH:] += mm_nt(moments[CH:], jnp.concatenate([minus, minus], axis=1))
        return carry

    lax.fori_loop(0, every, stage_one, jnp.int32(0))
    high, low = split2(env_ref[...])
    envs_ref[...] = jnp.concatenate([high, low], axis=1)

    def stage_two(t, carry):
        pair = pairs_ref[t]
        geo = geo_ref[t]
        valid = pair[8:9]
        u = geo[0:3]
        f = geo[4:5]
        hit = one_hot(pair[4:5], INNER, INNER)
        env = mm(envs_ref[...], jnp.concatenate([hit, hit], axis=0))
        aligned = (
            env[0:CH]
            + u[0:1] * env[CH : 2 * CH]
            + u[1:2] * env[2 * CH : 3 * CH]
            + u[2:3] * env[3 * CH :]
        )
        w = h_ref[t] * (f * valid)
        coupling = (env_scale * w * aligned).astype(BF16)
        arg = lat_ref[t].astype(F32) + mm(smt[...], coupling)
        gate = sigmoid(arg)
        hidden = arg * gate
        dotted = jnp.sum(hidden * eo(), axis=0, keepdims=True)
        en_ref[0:1] += f * dotted * pair[12:13]
        arg_bar = (f * valid) * eo() * (gate * (1.0 + arg * (1.0 - gate)))
        arg_bar = arg_bar.astype(BF16)
        hp_ref[t] = arg_bar
        c_bar = mm(sm[...], arg_bar).astype(BF16).astype(F32)
        wb_ref[t] = env_scale * aligned * c_bar
        al_bar = env_scale * w * c_bar
        geo_ref[t, 6:7] = dotted * valid
        u_bar = [
            jnp.sum(al_bar * env[(k + 1) * CH : (k + 2) * CH], axis=0, keepdims=True)
            for k in range(3)
        ]
        geo_ref[t, 16:19] = jnp.concatenate(u_bar, axis=0)
        high, low = split2(
            jnp.concatenate([al_bar, al_bar * u[0:1], al_bar * u[1:2], al_bar * u[2:3]], axis=0)
        )
        grad_ref[...] += mm_nt(
            jnp.concatenate([high, low], axis=1), jnp.concatenate([hit, hit], axis=1)
        )
        return carry

    lax.fori_loop(0, every, stage_two, jnp.int32(0))
    high, low = split2(grad_ref[...])
    envs_ref[...] = jnp.concatenate([high, low], axis=1)

    def stage_three(t, carry):
        pair = pairs_ref[t]
        geo = geo_ref[t]
        valid = pair[8:9]
        u, inverse, f, fd = geo[0:3], geo[3:4], geo[4:5], geo[5:6]
        hit_i = one_hot(pair[4:5], INNER, INNER)
        hit_j = one_hot(pair[5:6], INNER, INNER)
        plus, minus = hit_i + hit_j, hit_i - hit_j
        grad = envs_ref[...]
        g0 = mm(grad[0:CH], jnp.concatenate([plus, plus], axis=0))
        gv = mm(grad[CH:], jnp.concatenate([minus, minus], axis=0))
        parts = [gv[k * CH : (k + 1) * CH] for k in range(3)]
        h = h_ref[t]
        w = h * (f * valid)
        w_bar = wb_ref[t] + g0 + u[0:1] * parts[0] + u[1:2] * parts[1] + u[2:3] * parts[2]
        u_bar = geo[16:19] + jnp.concatenate(
            [jnp.sum(w * part, axis=0, keepdims=True) for part in parts], axis=0
        )
        f_bar = geo[6:7] + jnp.sum(h * w_bar, axis=0, keepdims=True)
        h_bar = (w_bar * (f * valid)).astype(BF16)
        lat_bar = (mm(wm[...], h_bar).astype(BF16) + hp_ref[t]).astype(F32)
        pre_bar = (lat_bar * slope_ref[t]).astype(BF16)
        basis_bar = mm(w1[...], pre_bar)[0:NB].astype(BF16).astype(F32)
        r_bar = jnp.sum(basis_bar * geo[8:16], axis=0, keepdims=True) + f_bar * fd
        along = jnp.sum(u * u_bar, axis=0, keepdims=True)
        d_bar = (r_bar * u + (u_bar - u * along) * inverse) * valid
        blank = jnp.zeros((2, WIDE), F32)

        def slotted(values, slot):
            second = slot > 0.5
            return jnp.concatenate(
                [jnp.where(second, 0.0, values), jnp.where(second, values, 0.0), blank], axis=0
            )

        pulls = jnp.concatenate(
            [slotted(d_bar, pair[1:2]), slotted(-d_bar, pair[3:4])], axis=1
        )
        high, low = split2(jnp.concatenate([pulls, jnp.zeros((120, 2 * WIDE), F32)], axis=0))
        where = jnp.concatenate([one_hot(pair[6:7], OWN, OWN), one_hot(pair[7:8], OWN, OWN)], axis=1)
        own_out[...] += mm_nt(where, high) + mm_nt(where, low)
        return carry

    lax.fori_loop(0, front, stage_three, jnp.int32(0))


def load_rows(rows_ref, low, own, high):
    rows_ref[0:ROWS] = jnp.zeros((ROWS, LANES), F32)
    for i in range(7):
        for piece, start, width in ((low, 0, 2), (own, 2, 3), (high, 5, 2)):
            for j in range(width):
                at = (i * 7 + start + j) * 8
                rows_ref[at : at + 8] = piece[i, j]


def own_rows(rows_ref):
    return jnp.concatenate(
        [rows_ref[(i * 7 + 2) * 8 : (i * 7 + 5) * 8] for i in range(2, 5)], axis=0
    )


def position_rows(rows_ref, pos_t):
    rows = jnp.concatenate([rows_ref[0:ROWS], jnp.zeros((DEPTH - ROWS, LANES), F32)], axis=0)
    turned = jnp.transpose(rows)
    top = turned[0:8]
    one = top.astype(BF16)
    rest = top - one.astype(F32)
    two = rest.astype(BF16)
    three = (rest - two.astype(F32)).astype(BF16)
    pos_t[...] = jnp.concatenate(
        [one.astype(F32), two.astype(F32), three.astype(F32), jnp.zeros((8, DEPTH), F32)], axis=0
    ).astype(BF16)
    return turned


def energy_row(first, second, live):
    lane = iota((1, LANES), 1)
    return jnp.where(lane == 0.0, first, 0.0) + jnp.where(lane == 1.0, second, 0.0) + jnp.where(
        lane == 2.0, live, 0.0
    )


def fetch(copies, sems):
    made = [pltpu.make_async_copy(src, dst, sems.at[i]) for i, (src, dst) in enumerate(copies)]
    for copy in made:
        copy.start()

    def wait():
        for copy in made:
            copy.wait()

    return wait


def pack_kernel(pos_in, vel_in, kind_in, count_in, list_in, out, pos, vel, kind, count, lists, sems,
                grid, first_list, second_list):
    fetch(
        ((pos_in, pos), (vel_in, vel), (kind_in, kind), (count_in, count), (list_in, lists)), sems
    )()
    for x in range(3):
        for y in range(3):
            at = (3 * x + y) * 16
            for s in range(2):
                for c in range(3):
                    grid[at + POS + 3 * s + c : at + POS + 3 * s + c + 1, 2:5] = pos[c, x, y, s : s + 1]
                    grid[at + VEL + 3 * s + c : at + VEL + 3 * s + c + 1, 2:5] = vel[c, x, y, s : s + 1]
                grid[at + KIND + s : at + KIND + s + 1, 2:5] = kind[x, y, s : s + 1].astype(F32)
                grid[at + LIVE + s : at + LIVE + s + 1, 2:5] = (
                    count[x, y : y + 1] > s
                ).astype(F32)
            row = (3 * x + y) * 8 + 2
            first_list[row : row + 3, 0:LISTED] = lists[x, y, :, 0].astype(F32)
            second_list[row : row + 3, 0:LISTED] = lists[x, y, :, 1].astype(F32)
    turned = jnp.concatenate(
        [jnp.transpose(grid[0:128])[0:8], jnp.transpose(grid[128:256])[0:8]], axis=1
    )
    lane = iota((8, LANES), 1)
    row = iota((8, LANES), 0)
    inside = (row > 1.5) & (row < 4.5)
    for xy in range(9):
        half = turned[:, 0:LANES] if xy < 8 else turned[:, LANES:]
        shift = (xy % 8) * 16
        fields = pltpu.roll(half, (LANES - shift) % LANES, 1)
        one = pltpu.roll(first_list[xy * 8 : xy * 8 + 8], NEIGH, 1)
        two = pltpu.roll(second_list[xy * 8 : xy * 8 + 8], NEIGH + LIST, 1)
        merged = jnp.where(lane < NEIGH, fields, jnp.where(lane < NEIGH + LIST, one, two))
        out[xy] = jnp.where(inside & (lane < MISC), merged, 0.0)


def prep_kernel(bw_in, se_in, wmt_in, sm_in, eo_in, table_in,
                w1t, w1, wmt, wm, smt, sm, eo, base, below, levels, bw, se, table, sems):
    fetch(
        (
            (bw_in, bw),
            (se_in, se),
            (wmt_in, wmt),
            (sm_in, sm),
            (eo_in, eo.at[0:1]),
            (table_in, table),
        ),
        sems,
    )()
    for k in range(NSPEC):
        levels[k : k + 1] = jnp.broadcast_to(table[0:1, k : k + 1], (1, LANES))
    both = jnp.concatenate(
        [bw[...].astype(F32), se[...].astype(F32), jnp.zeros((3, LAT), F32)], axis=0
    )
    w1[...] = both.astype(BF16)
    w1t[...] = jnp.transpose(deepen(both, LANES)).astype(BF16)[:, 0:16]
    wm[...] = jnp.transpose(deepen(wmt[...].astype(F32), LANES)).astype(BF16)[:, 0:CH]
    smt[...] = jnp.transpose(deepen(sm[...].astype(F32), LANES)).astype(BF16)[:, 0:CH]
    eo[...] = jnp.transpose(jnp.broadcast_to(eo[0:1], (LAT, LANES)))
    row = iota((ROWS, LANES), 0)
    x, y, z = row_coords(row)
    unused = (z > 6.5) | (row > USED - 0.5)
    for i, v in enumerate((x, y, z)):
        base[i] = jnp.where(unused, 99.0, 3.0 * jnp.floor((v + 1.5) * (1.0 / 3.0)) - 5.0)
    base[3] = jnp.where(unused, 99.0, away(x, y, z))
    below[...] = (iota((ROWS, DEPTH), 1) < iota((ROWS, DEPTH), 0)).astype(F32).astype(BF16)


def lanes_of(values, lane, first, second):
    return jnp.where(lane < 2.5, values[:, first : first + 1], values[:, second : second + 1])


def own_lane_row():
    lane = iota((72, LANES), 1)
    row = iota((72, LANES), 0)
    z = row - 8.0 * jnp.floor(row * 0.125)
    return lane, (z > 1.5) & (z < 4.5)


def first_kernel(low, own, high, w1t, w1, wmt, wm, smt, sm, eo, base, below, levels,
                 force_out, moved_out, energy_out, pairs_ref, counts_ref,
                 rows_ref, table, off_ref, end_ref, pos_t, own_ref, *scratch):
    load_rows(rows_ref, low, own, high)
    turned = position_rows(rows_ref, pos_t)
    front, every = build_pairs(
        rows_ref, base, below, table, off_ref, end_ref, pairs_ref, turned[NEIGH:MISC].astype(BF16)
    )
    counts_ref[0] = front
    counts_ref[1] = every
    refs = (pos_t, pairs_ref, w1t, w1, wmt, wm, smt, sm, eo)
    evaluate(refs, scratch, (front, every), own_ref)
    mine = own_rows(rows_ref)
    lane, inside = own_lane_row()
    kind3 = lanes_of(mine, lane, KIND, KIND + 1)
    speed = pltpu.roll(mine, LANES - VEL, 1)
    force = own_ref[0:72] * lanes_of(mine, lane, LIVE, LIVE + 1)
    force = jnp.where(inside & (lane < 6.0), force, 0.0)
    force_out[...] = force
    inverse_mass = jnp.zeros((72, LANES), F32)
    for k, mass in enumerate(atom_masses):
        inverse_mass = jnp.where(kind3 == float(k), 1.0 / mass, inverse_mass)
    moved = mine + time_step * speed + 0.5 * time_step * time_step * inverse_mass * force
    moved_out[...] = jnp.where(lane < 6.0, moved, jnp.where(lane < float(NEIGH), mine, 0.0))
    live = pltpu.roll(mine, LANES - LIVE + KIND, 1)
    live = jnp.where(inside & (lane > 5.5) & (lane < 7.5), live, 0.0)
    atom = jnp.zeros((72, LANES), F32)
    for k in range(NSPEC):
        atom = jnp.where(mine == float(k), levels[k : k + 1], atom)
    atoms = jnp.sum(atom * live)
    energy_out[...] = energy_row(jnp.sum(scratch[-1][0:1]) + atoms, atoms, jnp.sum(live))


def second_kernel(low, own, high, w1t, w1, wmt, wm, smt, sm, eo, pairs_ref, counts_ref, energy_in,
                  force_out, energy_out, rows_ref, pos_t, own_ref, *scratch):
    load_rows(rows_ref, low, own, high)
    position_rows(rows_ref, pos_t)
    refs = (pos_t, pairs_ref, w1t, w1, wmt, wm, smt, sm, eo)
    evaluate(refs, scratch, (counts_ref[0], counts_ref[1]), own_ref)
    mine = own_rows(rows_ref)
    lane, inside = own_lane_row()
    force = own_ref[0:72] * lanes_of(mine, lane, LIVE, LIVE + 1)
    force_out[...] = jnp.where(inside & (lane < 6.0), force, 0.0)
    energy_out[...] = energy_in[...] + energy_row(0.0, jnp.sum(scratch[-1][0:1]), 0.0)


def energy_row(first, second, live):
    lane = iota((1, LANES), 1)
    return (
        jnp.where(lane == 0.0, first, 0.0)
        + jnp.where(lane == 1.0, second, 0.0)
        + jnp.where((lane == 2.0) | (lane == 3.0), live, 0.0)
    )


EVAL_SCRATCH = (
    pltpu.VMEM((4 * CH, INNER), F32),
    pltpu.VMEM((4 * CH, 2 * INNER), BF16),
    pltpu.VMEM((4 * CH, INNER), F32),
    pltpu.VMEM((TILES, 24, WIDE), F32),
    pltpu.VMEM((TILES, LAT, WIDE), BF16),
    pltpu.VMEM((TILES, LAT, WIDE), F32),
    pltpu.VMEM((TILES, CH, WIDE), F32),
    pltpu.VMEM((TILES, CH, WIDE), F32),
    pltpu.VMEM((TILES, LAT, WIDE), BF16),
    pltpu.VMEM((8, WIDE), F32),
)
VM = pl.BlockSpec(memory_space=pltpu.VMEM)
SM = pl.BlockSpec(memory_space=pltpu.SMEM)
HB = pl.BlockSpec(memory_space=pltpu.HBM)


def limit(mebibytes):
    return pltpu.CompilerParams(vmem_limit_bytes=mebibytes * 2**20)


def shape(*dims, kind=F32):
    return jax.ShapeDtypeStruct(dims, kind)


def pack_call(positions, velocity, species, region_count, neighbours):
    return pl.pallas_call(
        pack_kernel,
        name="pack",
        out_shape=shape(9, 8, LANES),
        in_specs=[HB] * 5,
        out_specs=VM,
        scratch_shapes=(
            pltpu.VMEM((3, 3, 3, 2, 3), F32),
            pltpu.VMEM((3, 3, 3, 2, 3), F32),
            pltpu.VMEM((3, 3, 2, 3), jnp.int32),
            pltpu.VMEM((3, 3, 3), jnp.int32),
            pltpu.VMEM((3, 3, 3, 2, LISTED), jnp.int32),
            pltpu.SemaphoreType.DMA((5,)),
            pltpu.VMEM((256, LANES), F32),
            pltpu.VMEM((72, LANES), F32),
            pltpu.VMEM((72, LANES), F32),
        ),
        compiler_params=limit(4),
    )(
        positions.transpose(0, 1, 2, 4, 3),
        velocity.transpose(0, 1, 2, 4, 3),
        species.transpose(0, 1, 3, 2),
        region_count,
        neighbours,
    )


def prep_call(basis_weight, species_embed, weight_map, scalar_map, energy_out, species_energy):
    return pl.pallas_call(
        prep_kernel,
        name="prep",
        out_shape=(
            shape(LAT, 16, kind=BF16),
            shape(16, LAT, kind=BF16),
            shape(CH, LAT, kind=BF16),
            shape(LAT, CH, kind=BF16),
            shape(LAT, CH, kind=BF16),
            shape(CH, LAT, kind=BF16),
            shape(LAT, LANES),
            shape(4, ROWS, LANES),
            shape(ROWS, DEPTH, kind=BF16),
            shape(8, LANES),
        ),
        in_specs=[HB] * 6,
        out_specs=(VM,) * 10,
        scratch_shapes=(
            pltpu.VMEM((NB, LAT), BF16),
            pltpu.VMEM((NSPEC, LAT), BF16),
            pltpu.VMEM((1, NSPEC), F32),
            pltpu.SemaphoreType.DMA((6,)),
        ),
        compiler_params=limit(4),
        cost_estimate=pl.CostEstimate(flops=1000000, transcendentals=0, bytes_accessed=2000000),
    )(
        basis_weight,
        species_embed,
        weight_map.T,
        scalar_map,
        energy_out[None, :],
        species_energy[None, :],
    )


def first_call(pieces, prepared):
    return pl.pallas_call(
        first_kernel,
        name="first",
        out_shape=(
            shape(72, LANES),
            shape(72, LANES),
            shape(1, LANES),
            shape(TILES, 16, WIDE),
            shape(2, kind=jnp.int32),
        ),
        in_specs=[VM] * (len(pieces) + len(prepared)),
        out_specs=(VM, VM, VM, VM, SM),
        scratch_shapes=(
            pltpu.VMEM((ROWS, LANES), F32),
            pltpu.VMEM((4 * LIST + 16, DEPTH), BF16),
            pltpu.VMEM((ROWS, LANES), F32),
            pltpu.VMEM((ROWS, LANES), F32),
            pltpu.VMEM((32, DEPTH), BF16),
            pltpu.VMEM((OWN, LANES), F32),
            *EVAL_SCRATCH,
        ),
        compiler_params=limit(20),
    )(*pieces, *prepared)


def second_call(pieces, weights, pairs, counts, energy):
    return pl.pallas_call(
        second_kernel,
        name="second",
        out_shape=(shape(72, LANES), shape(1, LANES)),
        in_specs=[VM] * (len(pieces) + len(weights) + 1) + [SM, VM],
        out_specs=(VM, VM),
        scratch_shapes=(
            pltpu.VMEM((ROWS, LANES), F32),
            pltpu.VMEM((32, DEPTH), BF16),
            pltpu.VMEM((OWN, LANES), F32),
            *EVAL_SCRATCH,
        ),
        compiler_params=limit(20),
    )(*pieces, *weights, pairs, counts, energy)


def swap(low_part, high_part, axis):
    count = lax.axis_size(axis)
    even = lax.axis_index(axis) % 2 == 0
    across, within = jnp.where(even, low_part, high_part), jnp.where(even, high_part, low_part)
    inner = [(i, i ^ 1) for i in range(count)]
    outer = [(i, (i - 1) % count if i % 2 == 0 else (i + 1) % count) for i in range(count)]
    across = lax.ppermute(across, axis, outer)
    within = lax.ppermute(within, axis, inner)
    return jnp.where(even, across, within), jnp.where(even, within, across)


def everywhere(row, axes):
    count = math.prod(lax.axis_size(axis) for axis in axes)
    rows = jnp.broadcast_to(row[None], (count, 1, LANES))
    rows = lax.all_to_all(rows, axes, 0, 0, tiled=False)
    return jnp.sum(rows, axis=0)


def spread(rows, beside):
    rows = rows.reshape(3, 3, 8, LANES)
    low, high = swap(rows[:, :, 2:4], rows[:, :, 3:5], "gz")
    rows = jnp.concatenate(
        [low, rows[:, :, 2:5], high, jnp.zeros((3, 3, 1, LANES), F32)], axis=2
    )
    low, high = swap(rows[0:2], rows[1:3], "gx")
    rows = jnp.concatenate([low, rows, high], axis=0)
    rows, beside = lax.optimization_barrier((rows, beside))
    low, high = swap(rows[:, 0:2], rows[:, 1:3], "gy")
    return (low, rows, high), beside


def unpack(force):
    own = force.reshape(3, 3, 8, LANES)[:, :, 2:5, 0:6]
    return own.reshape(3, 3, 3, 2, 3).transpose(4, 0, 1, 2, 3)


def shards(positions, velocity, species, region_count, neighbours,
           basis_weight, species_embed, weight_map, scalar_map, energy_out, species_energy):
    rows = pack_call(positions, velocity, species, region_count, neighbours)
    prepared = prep_call(
        basis_weight, species_embed, weight_map, scalar_map, energy_out, species_energy
    )
    pieces, prepared = spread(rows, prepared)
    force_one, moved, energy_one, pairs, counts = first_call(pieces, prepared)
    pieces, _ = spread(moved, ())
    force_two, energies = second_call(pieces, prepared[0:7], pairs, counts, energy_one)
    totals = everywhere(everywhere(energies, ("gx", "gy")), ("gz",))
    forces = jnp.stack([unpack(force_one), unpack(force_two)])
    return forces, totals[0, 0:2] / totals[0, 2:4]


def solution(mesh):
    placed = (
        P(None, "gx", "gy", "gz", None),
        P(None, "gx", "gy", "gz", None),
        P("gx", "gy", "gz", None),
        P("gx", "gy", "gz"),
        P("gx", "gy", "gz", None, None),
        P(),
        P(),
        P(),
        P(),
        P(),
        P(),
    )
    return jax.shard_map(
        shards,
        mesh=mesh,
        in_specs=placed,
        out_specs=(P(None, None, "gx", "gy", "gz", None), P()),
        check_vma=False,
    )
```

```python
import math

import jax
import jax.numpy as jnp
from jax import lax
from jax.experimental import pallas as pl
from jax.experimental.pallas import tpu as pltpu
from jax.sharding import PartitionSpec as P


cutoff = 6.0
env_scale = 0.25
domain_side = 18.0
time_step = 0.15
atom_masses = (1.008, 12.011, 14.007, 15.999, 32.06)

CH = 64
LAT = 128
NB = 8
NSPEC = 5
LIST = 24
LISTED = 40
USED = 392
ROWS = 400
SPARSE = 448
DEPTH = 512
INNER = 256
OWN = 80
WIDE = 256
TILES = 26
LANES = 128
HALF = 64
POS, KIND, VEL, LIVE, NEIGH = 0, 6, 8, 14, 16
MISC = NEIGH + 2 * LIST
F32 = jnp.float32
BF16 = jnp.bfloat16


def mm(a, b):
    return lax.dot_general(a, b, (((1,), (0,)), ((), ())), preferred_element_type=F32)


def mm_nt(a, b):
    return lax.dot_general(a, b, (((1,), (1,)), ((), ())), preferred_element_type=F32)


def split2(v):
    high = v.astype(BF16)
    return high, (v - high.astype(F32)).astype(BF16)


def iota(shape, dim):
    return lax.broadcasted_iota(jnp.int32, shape, dim).astype(F32)


def sigmoid(v):
    return 1.0 / (1.0 + jnp.exp(-v))


def row_coords(row):
    xy = jnp.floor(row * 0.125)
    z = row - 8.0 * xy
    x = jnp.floor((xy + 0.5) * (1.0 / 7.0))
    return x, xy - 7.0 * x, z


def away(x, y, z):
    return jnp.maximum(jnp.maximum(jnp.abs(x - 3.0), jnp.abs(y - 3.0)), jnp.abs(z - 3.0))


def far_coords(x, y, z, entry):
    q = jnp.floor(entry * 0.5)
    a = jnp.floor((q + 0.5) * (1.0 / 25.0))
    ab = jnp.floor((q + 0.5) * (1.0 / 5.0))
    steps = (a, ab - 5.0 * a, q - 5.0 * ab)
    far = [3.0 * jnp.floor((v + 1.5) * (1.0 / 3.0)) + s - 2.0 for v, s in zip((x, y, z), steps)]
    shift = [(jnp.floor((s + 2.5) * (1.0 / 3.0)) - 1.0) * domain_side for s in steps]
    return far, shift, entry - 2.0 * q


def one_hot(index, count, depth):
    hit = (iota((count, index.shape[1]), 0) == index).astype(F32).astype(BF16)
    return deepen(hit, depth)


def deepen(values, depth):
    more = depth - values.shape[0]
    if more == 0:
        return values
    return jnp.concatenate([values, jnp.zeros((more, values.shape[1]), values.dtype)], axis=0)


def build_pairs(rows_ref, base_ref, below_ref, table, off_ref, end_ref, pairs_ref, listed_t):
    lane = iota((ROWS, LANES), 1)
    entry = rows_ref[0:ROWS]
    listed = (lane >= NEIGH) & (lane < MISC) & (entry >= 0.0)
    q = jnp.floor(entry * 0.5)
    a = jnp.floor((q + 0.5) * (1.0 / 25.0))
    ab = jnp.floor((q + 0.5) * (1.0 / 5.0))
    far = jnp.maximum(jnp.abs(base_ref[0] + a), jnp.abs(base_ref[1] + (ab - 5.0 * a)))
    far = jnp.maximum(far, jnp.abs(base_ref[2] + (q - 5.0 * ab)))
    nearest = jnp.where(listed, jnp.minimum(base_ref[3], far), 9.0)
    kept = (nearest < 1.5, (nearest > 1.5) & (nearest < 2.5))
    upto = iota((2 * LIST, LANES), 0) + NEIGH
    place = iota((2 * LIST, LANES), 1)
    keys = (place <= upto).astype(F32) + (place < upto).astype(F32)
    keys = keys.astype(BF16)
    ones = jnp.ones((LANES, LANES), BF16)
    cx, cy, cz = row_coords(iota((1, DEPTH), 1))
    keeps = [deepen(keep.astype(F32).astype(BF16), DEPTH) for keep in kept]
    counts = [mm(keep, ones) for keep in keeps]
    counts_t = [mm_nt(ones[0:16], keep).astype(BF16) for keep in keeps]
    below = below_ref[...]
    offsets = mm(below, jnp.concatenate(counts, axis=1).astype(BF16))
    offsets_t = mm_nt(jnp.concatenate(counts_t, axis=0), below)
    first = jnp.zeros((1, 1), F32)
    ends = []
    for which, keep in enumerate(keeps):
        offset = offsets[:, which * LANES : (which + 1) * LANES] + first
        end = offset + counts[which][0:ROWS]
        off_ref[which] = offset
        end_ref[which] = end
        offset_t = offsets_t[16 * which : 16 * which + 1] + first
        offset_t = jnp.concatenate([offset_t, jnp.zeros((1, DEPTH - ROWS), F32)], axis=1)
        high = jnp.floor(offset_t * (1.0 / 256.0))
        misc = jnp.concatenate(
            [high, offset_t - 256.0 * high, cx, cy, cz, jnp.zeros((11, DEPTH), F32)], axis=0
        )
        table[which, 0 : 2 * LIST] = listed_t
        table[which, 2 * LIST : 4 * LIST] = mm_nt(keys, keep).astype(BF16)
        table[which, 4 * LIST :] = misc.astype(BF16)
        first = jnp.max(jnp.max(end, axis=0, keepdims=True), axis=1, keepdims=True)
        ends.append(jnp.max(first))
    first = jnp.float32(0.0)
    totals = []
    for which, total in enumerate(ends):

        def body(k, carry, which=which, first=first, total=total):
            place = iota((1, WIDE), 1) + (k * WIDE).astype(F32)
            offset = off_ref[which]
            end = end_ref[which]
            hit = jnp.concatenate(
                [
                    ((offset <= part) & (end > part)).astype(F32).astype(BF16)
                    for part in (place[:, 0:LANES], place[:, LANES:])
                ],
                axis=1,
            )
            got = mm(table[which], deepen(hit, DEPTH))
            misc = got[4 * LIST :]
            wanted = 2.0 * (place - (256.0 * misc[0:1] + misc[1:2])) + 1.0
            chosen = (got[2 * LIST : 4 * LIST] == wanted).astype(F32)
            entry = jnp.sum(chosen * got[0 : 2 * LIST], axis=0, keepdims=True)
            slot = jnp.sum(chosen[LIST:], axis=0, keepdims=True)
            x, y, z = misc[2:3], misc[3:4], misc[4:5]
            far, shift, far_slot = far_coords(x, y, z, entry)
            valid = place < total
            away_i, away_j = away(x, y, z), away(*far)

            def where(flag, value):
                return jnp.where(flag, value, -1.0)

            def region(c, layers):
                return (c[0] * layers + c[1]) * 8.0 + c[2]

            def inner(c, s):
                return (((c[0] - 1.0) * 5.0 + (c[1] - 1.0)) * 5.0 + (c[2] - 1.0)) * 2.0 + s

            def own(c):
                return ((c[0] - 2.0) * 3.0 + (c[1] - 2.0)) * 8.0 + c[2]

            near = (x, y, z)
            lines = [
                where(valid, region(near, 7.0)),
                slot,
                where(valid, region(far, 7.0)),
                far_slot,
                where(valid & (away_i < 2.5), inner(near, slot)),
                where(valid & (away_j < 2.5), inner(far, far_slot)),
                where(valid & (away_i < 1.5), own(near)),
                where(valid & (away_j < 1.5), own(far)),
                valid.astype(F32),
                *shift,
                (valid & (away_i < 1.5)).astype(F32),
                where(valid, region(near, 8.0)),
                where(valid, region(far, 8.0)),
                jnp.zeros((9, WIDE), F32),
            ]
            pairs_ref[k] = jnp.where(place < first, pairs_ref[k], jnp.concatenate(lines, axis=0))
            return carry

        last = total.astype(jnp.int32)
        lax.fori_loop(
            first.astype(jnp.int32) // WIDE, (last + (WIDE - 1)) // WIDE, body, jnp.int32(0)
        )
        totals.append((last + (WIDE - 1)) // WIDE)
        first = total
    return totals


def turns(radius):
    part = radius * (1.0 / 12.0)
    part = part - jnp.floor(part + 0.5)
    half = part * math.pi
    sq = half * half
    s = jnp.full_like(sq, -1.0 / 39916800.0)
    for c in (1.0 / 362880.0, -1.0 / 5040.0, 1.0 / 120.0, -1.0 / 6.0, 1.0):
        s = s * sq + c
    s = s * half
    c = jnp.full_like(sq, 1.0 / 479001600.0)
    for k in (-1.0 / 3628800.0, 1.0 / 40320.0, -1.0 / 720.0, 1.0 / 24.0, -0.5, 1.0):
        c = c * sq + k
    return 2.0 * s * c, 1.0 - 2.0 * s * s


def evaluate(refs, scratch, counts, own_out, moved):
    pos_t, pairs_ref, w1t, w1, wmt, wm, smt, sm, eo_ref = refs
    env_ref, envs_ref, grad_ref, geo_ref, lat_ref, slope_ref, h_ref, wb_ref, hp_ref, en_ref = (
        scratch
    )
    front, every = counts
    norm = math.sqrt(2.0 / cutoff)

    def eo():
        return jnp.concatenate([eo_ref[...], eo_ref[...]], axis=1)

    env_ref[...] = jnp.zeros(env_ref.shape, F32)
    grad_ref[...] = jnp.zeros(grad_ref.shape, F32)
    en_ref[...] = jnp.zeros(en_ref.shape, F32)
    own_out[...] = jnp.zeros(own_out.shape, F32)

    def gathered(index, slot):
        got = mm(pos_t[...], one_hot(index, SPARSE if moved else ROWS, DEPTH))
        full = got[0:8] + got[8:16] + got[16:24]
        second = slot > 0.5
        point = jnp.where(second, full[3:6], full[0:3])
        return point, jnp.where(second, full[7:8], full[6:7])

    def stage_one(t, carry):
        pair = pairs_ref[t]
        valid = pair[8:9]
        if moved:
            near, _ = gathered(pair[13:14], pair[1:2])
            far, _ = gathered(pair[14:15], pair[3:4])
            near_kind, far_kind = pair[15:16], pair[16:17]
        else:
            near, near_kind = gathered(pair[0:1], pair[1:2])
            far, far_kind = gathered(pair[2:3], pair[3:4])
            pairs_ref[t, 15:17] = jnp.concatenate([near_kind, far_kind], axis=0)
        d = far - near + pair[9:12]
        square = jnp.sum(d * d, axis=0, keepdims=True)
        square = jnp.where(valid > 0.5, square, 1.0)
        radius = jnp.sqrt(square)
        inverse = 1.0 / radius
        u = d * inverse
        y = jnp.minimum(radius * (1.0 / cutoff), 1.0)
        y2 = y * y
        y5 = y2 * y2 * y
        f = 1.0 + y5 * y * (-28.0 + y * (48.0 - 21.0 * y))
        fd = y5 * (-168.0 + y * (336.0 - 168.0 * y)) * (1.0 / cutoff)
        sin1, cos1 = turns(radius)
        sines, cosines = [jnp.zeros_like(sin1), sin1], [jnp.ones_like(cos1), cos1]
        for _ in range(NB - 1):
            sines.append(2.0 * cos1 * sines[-1] - sines[-2])
            cosines.append(2.0 * cos1 * cosines[-1] - cosines[-2])
        basis = [norm * inverse * s for s in sines[1:]]
        slope = [
            norm * (k * (math.pi / cutoff)) * inverse * c - inverse * b
            for k, (c, b) in enumerate(zip(cosines[1:], basis), 1)
        ]
        kinds = [
            (near_kind == float(k)).astype(F32) + (far_kind == float(k)).astype(F32)
            for k in range(NSPEC)
        ]
        feats = jnp.concatenate(basis + kinds + [jnp.zeros((3, WIDE), F32)], axis=0)
        geo_ref[t, 0:16] = jnp.concatenate(
            [u, inverse, f, fd, jnp.zeros((2, WIDE), F32)] + slope, axis=0
        )
        pre = mm(w1t[...], feats.astype(BF16))
        gate = sigmoid(pre)
        lat = (pre * gate).astype(BF16)
        lat_ref[t] = lat
        slope_ref[t] = gate * (1.0 + pre * (1.0 - gate))
        h = mm(wmt[...], lat)
        h_ref[t] = h
        w = h * (f * valid)
        hit_i = one_hot(pair[4:5], INNER, INNER)
        hit_j = one_hot(pair[5:6], INNER, INNER)
        high, low = split2(
            jnp.concatenate([w, w * u[0:1], w * u[1:2], w * u[2:3]], axis=0)
        )
        moments = jnp.concatenate([high, low], axis=1)
        plus, minus = hit_i + hit_j, hit_i - hit_j
        env_ref[0:CH] += mm_nt(moments[0:CH], jnp.concatenate([plus, plus], axis=1))
        env_ref[CH:] += mm_nt(moments[CH:], jnp.concatenate([minus, minus], axis=1))
        return carry

    lax.fori_loop(0, every, stage_one, jnp.int32(0))
    high, low = split2(env_ref[...])
    envs_ref[...] = jnp.concatenate([high, low], axis=1)

    def stage_two(t, carry):
        pair = pairs_ref[t]
        geo = geo_ref[t]
        valid = pair[8:9]
        u = geo[0:3]
        f = geo[4:5]
        hit = one_hot(pair[4:5], INNER, INNER)
        env = mm(envs_ref[...], jnp.concatenate([hit, hit], axis=0))
        aligned = (
            env[0:CH]
            + u[0:1] * env[CH : 2 * CH]
            + u[1:2] * env[2 * CH : 3 * CH]
            + u[2:3] * env[3 * CH :]
        )
        w = h_ref[t] * (f * valid)
        coupling = (env_scale * w * aligned).astype(BF16)
        arg = lat_ref[t].astype(F32) + mm(smt[...], coupling)
        gate = sigmoid(arg)
        hidden = arg * gate
        dotted = jnp.sum(hidden * eo(), axis=0, keepdims=True)
        en_ref[0:1] += f * dotted * pair[12:13]
        arg_bar = (f * valid) * eo() * (gate * (1.0 + arg * (1.0 - gate)))
        arg_bar = arg_bar.astype(BF16)
        hp_ref[t] = arg_bar
        c_bar = mm(sm[...], arg_bar).astype(BF16).astype(F32)
        wb_ref[t] = env_scale * aligned * c_bar
        al_bar = env_scale * w * c_bar
        geo_ref[t, 6:7] = dotted * valid
        u_bar = [
            jnp.sum(al_bar * env[(k + 1) * CH : (k + 2) * CH], axis=0, keepdims=True)
            for k in range(3)
        ]
        geo_ref[t, 16:19] = jnp.concatenate(u_bar, axis=0)
        high, low = split2(
            jnp.concatenate([al_bar, al_bar * u[0:1], al_bar * u[1:2], al_bar * u[2:3]], axis=0)
        )
        grad_ref[...] += mm_nt(
            jnp.concatenate([high, low], axis=1), jnp.concatenate([hit, hit], axis=1)
        )
        return carry

    lax.fori_loop(0, every, stage_two, jnp.int32(0))
    high, low = split2(grad_ref[...])
    envs_ref[...] = jnp.concatenate([high, low], axis=1)

    def stage_three(t, carry):
        pair = pairs_ref[t]
        geo = geo_ref[t]
        valid = pair[8:9]
        u, inverse, f, fd = geo[0:3], geo[3:4], geo[4:5], geo[5:6]
        hit_i = one_hot(pair[4:5], INNER, INNER)
        hit_j = one_hot(pair[5:6], INNER, INNER)
        plus, minus = hit_i + hit_j, hit_i - hit_j
        grad = envs_ref[...]
        g0 = mm(grad[0:CH], jnp.concatenate([plus, plus], axis=0))
        gv = mm(grad[CH:], jnp.concatenate([minus, minus], axis=0))
        parts = [gv[k * CH : (k + 1) * CH] for k in range(3)]
        h = h_ref[t]
        w = h * (f * valid)
        w_bar = wb_ref[t] + g0 + u[0:1] * parts[0] + u[1:2] * parts[1] + u[2:3] * parts[2]
        u_bar = geo[16:19] + jnp.concatenate(
            [jnp.sum(w * part, axis=0, keepdims=True) for part in parts], axis=0
        )
        f_bar = geo[6:7] + jnp.sum(h * w_bar, axis=0, keepdims=True)
        h_bar = (w_bar * (f * valid)).astype(BF16)
        lat_bar = (mm(wm[...], h_bar).astype(BF16) + hp_ref[t]).astype(F32)
        pre_bar = (lat_bar * slope_ref[t]).astype(BF16)
        basis_bar = mm(w1[...], pre_bar)[0:NB].astype(BF16).astype(F32)
        r_bar = jnp.sum(basis_bar * geo[8:16], axis=0, keepdims=True) + f_bar * fd
        along = jnp.sum(u * u_bar, axis=0, keepdims=True)
        d_bar = (r_bar * u + (u_bar - u * along) * inverse) * valid
        blank = jnp.zeros((2, WIDE), F32)

        def slotted(values, slot):
            second = slot > 0.5
            return jnp.concatenate(
                [jnp.where(second, 0.0, values), jnp.where(second, values, 0.0), blank], axis=0
            )

        pulls = jnp.concatenate(
            [slotted(d_bar, pair[1:2]), slotted(-d_bar, pair[3:4])], axis=1
        )
        high, low = split2(jnp.concatenate([pulls, jnp.zeros((120, 2 * WIDE), F32)], axis=0))
        where = jnp.concatenate([one_hot(pair[6:7], OWN, OWN), one_hot(pair[7:8], OWN, OWN)], axis=1)
        own_out[...] += mm_nt(where, high) + mm_nt(where, low)
        return carry

    lax.fori_loop(0, front, stage_three, jnp.int32(0))


def load_rows(rows_ref, low, own, high):
    rows_ref[0:ROWS] = jnp.zeros((ROWS, LANES), F32)
    for i in range(7):
        at = i * 56
        for piece, start in ((low, 0), (high, 40)):
            both = piece[i]
            rows_ref[at + start : at + start + 8] = both
            rows_ref[at + start + 8 : at + start + 16] = pltpu.roll(both, HALF, 1)
        for j in range(3):
            rows_ref[at + 16 + 8 * j : at + 24 + 8 * j, 0:HALF] = own[i, j]


def own_rows(rows_ref):
    return jnp.concatenate(
        [rows_ref[(i * 7 + 2) * 8 : (i * 7 + 5) * 8] for i in range(2, 5)], axis=0
    )


def put_positions(top, pos_t):
    one = top.astype(BF16)
    rest = top - one.astype(F32)
    two = rest.astype(BF16)
    three = (rest - two.astype(F32)).astype(BF16)
    pos_t[...] = jnp.concatenate(
        [one.astype(F32), two.astype(F32), three.astype(F32), jnp.zeros((8, DEPTH), F32)], axis=0
    ).astype(BF16)


def fetch(copies, sems):
    made = [pltpu.make_async_copy(src, dst, sems.at[i]) for i, (src, dst) in enumerate(copies)]
    for copy in made:
        copy.start()

    def wait():
        for copy in made:
            copy.wait()

    return wait


def pack_kernel(pos_in, vel_in, kind_in, count_in, list_in, out, across, within,
                pos, vel, kind, count, lists, sems, grid, first_list, second_list):
    even = lax.axis_index("gz") % 2 == 0
    fetch(
        ((pos_in, pos), (vel_in, vel), (kind_in, kind), (count_in, count), (list_in, lists)), sems
    )()
    for x in range(3):
        for y in range(3):
            at = (3 * x + y) * 16
            for s in range(2):
                for c in range(3):
                    grid[at + POS + 3 * s + c : at + POS + 3 * s + c + 1, 2:5] = pos[c, x, y, s : s + 1]
                    grid[at + VEL + 3 * s + c : at + VEL + 3 * s + c + 1, 2:5] = vel[c, x, y, s : s + 1]
                grid[at + KIND + s : at + KIND + s + 1, 2:5] = kind[x, y, s : s + 1].astype(F32)
                grid[at + LIVE + s : at + LIVE + s + 1, 2:5] = (
                    count[x, y : y + 1] > s
                ).astype(F32)
            row = (3 * x + y) * 8 + 2
            first_list[row : row + 3, 0:LISTED] = lists[x, y, :, 0].astype(F32)
            second_list[row : row + 3, 0:LISTED] = lists[x, y, :, 1].astype(F32)
    turned = jnp.concatenate(
        [jnp.transpose(grid[0:128])[0:8], jnp.transpose(grid[128:256])[0:8]], axis=1
    )
    lane = iota((8, LANES), 1)
    row = iota((8, LANES), 0)
    inside = (row > 1.5) & (row < 4.5)
    for xy in range(9):
        half = turned[:, 0:LANES] if xy < 8 else turned[:, LANES:]
        shift = (xy % 8) * 16
        fields = pltpu.roll(half, (LANES - shift) % LANES, 1)
        one = pltpu.roll(first_list[xy * 8 : xy * 8 + 8], NEIGH, 1)
        two = pltpu.roll(second_list[xy * 8 : xy * 8 + 8], NEIGH + LIST, 1)
        merged = jnp.where(lane < NEIGH, fields, jnp.where(lane < NEIGH + LIST, one, two))
        merged = jnp.where(inside & (lane < MISC), merged, 0.0)
        out[xy] = merged
        across[xy] = jnp.where(even, merged[2:4], merged[3:5])
        within[xy] = jnp.where(even, merged[3:5], merged[2:4])


def prep_kernel(bw_in, se_in, wmt_in, sm_in, eo_in, table_in,
                w1t, w1, wmt, wm, smt, sm, eo, base, below, levels, bw, se, table, sems):
    fetch(
        (
            (bw_in, bw),
            (se_in, se),
            (wmt_in, wmt),
            (sm_in, sm),
            (eo_in, eo.at[0:1]),
            (table_in, table),
        ),
        sems,
    )()
    for k in range(NSPEC):
        levels[k : k + 1] = jnp.broadcast_to(table[0:1, k : k + 1], (1, LANES))
    both = jnp.concatenate(
        [bw[...].astype(F32), se[...].astype(F32), jnp.zeros((3, LAT), F32)], axis=0
    )
    w1[...] = both.astype(BF16)
    w1t[...] = jnp.transpose(deepen(both, LANES)).astype(BF16)[:, 0:16]
    wm[...] = jnp.transpose(deepen(wmt[...].astype(F32), LANES)).astype(BF16)[:, 0:CH]
    smt[...] = jnp.transpose(deepen(sm[...].astype(F32), LANES)).astype(BF16)[:, 0:CH]
    eo[...] = jnp.transpose(jnp.broadcast_to(eo[0:1], (LAT, LANES)))
    row = iota((ROWS, LANES), 0)
    x, y, z = row_coords(row)
    unused = (z > 6.5) | (row > USED - 0.5)
    for i, v in enumerate((x, y, z)):
        base[i] = jnp.where(unused, 99.0, 3.0 * jnp.floor((v + 1.5) * (1.0 / 3.0)) - 5.0)
    base[3] = jnp.where(unused, 99.0, away(x, y, z))
    below[...] = (iota((ROWS, DEPTH), 1) < iota((ROWS, DEPTH), 0)).astype(F32).astype(BF16)


def lanes_of(values, lane, first, second):
    return jnp.where(lane < 2.5, values[:, first : first + 1], values[:, second : second + 1])


def own_lane_row():
    lane = iota((72, LANES), 1)
    row = iota((72, LANES), 0)
    z = row - 8.0 * jnp.floor(row * 0.125)
    return lane, (z > 1.5) & (z < 4.5)


def first_kernel(low, own, high, w1t, w1, wmt, wm, smt, sm, eo, base, below, levels,
                 force_out, moved_out, live_out, energy_out, pairs_ref, counts_ref,
                 rows_ref, table, off_ref, end_ref, pos_t, own_ref, *scratch):
    load_rows(rows_ref, low, own, high)
    turned = jnp.transpose(deepen(rows_ref[0:ROWS], DEPTH))
    put_positions(turned[0:8], pos_t)
    front, every = build_pairs(
        rows_ref, base, below, table, off_ref, end_ref, pairs_ref, turned[NEIGH:MISC].astype(BF16)
    )
    counts_ref[0] = front
    counts_ref[1] = every
    refs = (pos_t, pairs_ref, w1t, w1, wmt, wm, smt, sm, eo)
    evaluate(refs, scratch, (front, every), own_ref, False)
    mine = own_rows(rows_ref)
    lane, inside = own_lane_row()
    kind3 = lanes_of(mine, lane, KIND, KIND + 1)
    speed = pltpu.roll(mine, LANES - VEL, 1)
    live3 = jnp.where(inside & (lane < 6.0), lanes_of(mine, lane, LIVE, LIVE + 1), 0.0)
    live_out[...] = live3
    force = jnp.where(inside & (lane < 6.0), own_ref[0:72] * live3, 0.0)
    force_out[...] = force
    inverse_mass = jnp.zeros((72, LANES), F32)
    for k, mass in enumerate(atom_masses):
        inverse_mass = jnp.where(kind3 == float(k), 1.0 / mass, inverse_mass)
    moved = mine + time_step * speed + 0.5 * time_step * time_step * inverse_mass * force
    moved = jnp.where(lane < 6.0, moved, 0.0)
    for y in range(3):
        moved_out[y] = sum(
            pltpu.roll(moved[(x * 3 + y) * 8 : (x * 3 + y) * 8 + 8], (x + 2) * 16, 1)
            for x in range(3)
        )
    live = pltpu.roll(mine, LANES - LIVE + KIND, 1)
    live = jnp.where(inside & (lane > 5.5) & (lane < 7.5), live, 0.0)
    atom = jnp.zeros((72, LANES), F32)
    for k in range(NSPEC):
        atom = jnp.where(mine == float(k), levels[k : k + 1], atom)
    atoms = jnp.sum(atom * live)
    energy_out[...] = energy_row(jnp.sum(scratch[-1][0:1]) + atoms, atoms, jnp.sum(live))


def second_kernel(low, own, high, w1t, w1, wmt, wm, smt, sm, eo, pairs_ref, counts_ref, energy_in,
                  live, force_out, energy_out, pos_t, own_ref, *scratch):
    layers = [piece[i] for piece, width in ((low, 2), (own, 3), (high, 2)) for i in range(width)]
    turned = jnp.transpose(deepen(jnp.concatenate(layers, axis=0), LANES))
    blocks = [turned[x * 16 : x * 16 + 8] for x in range(7)] + [jnp.zeros((8, LANES), F32)]
    top = [blocks[x] + pltpu.roll(blocks[x + 1], HALF, 1) for x in range(0, 8, 2)]
    put_positions(jnp.concatenate(top, axis=1), pos_t)
    refs = (pos_t, pairs_ref, w1t, w1, wmt, wm, smt, sm, eo)
    evaluate(refs, scratch, (counts_ref[0], counts_ref[1]), own_ref, True)
    lane, inside = own_lane_row()
    force_out[...] = jnp.where(inside & (lane < 6.0), own_ref[0:72] * live[...], 0.0)
    energy_out[...] = energy_in[...] + energy_row(0.0, jnp.sum(scratch[-1][0:1]), 0.0)


def energy_row(first, second, live):
    lane = iota((1, LANES), 1)
    return (
        jnp.where(lane == 0.0, first, 0.0)
        + jnp.where(lane == 1.0, second, 0.0)
        + jnp.where((lane == 2.0) | (lane == 3.0), live, 0.0)
    )


EVAL_SCRATCH = (
    pltpu.VMEM((4 * CH, INNER), F32),
    pltpu.VMEM((4 * CH, 2 * INNER), BF16),
    pltpu.VMEM((4 * CH, INNER), F32),
    pltpu.VMEM((TILES, 24, WIDE), F32),
    pltpu.VMEM((TILES, LAT, WIDE), BF16),
    pltpu.VMEM((TILES, LAT, WIDE), F32),
    pltpu.VMEM((TILES, CH, WIDE), F32),
    pltpu.VMEM((TILES, CH, WIDE), F32),
    pltpu.VMEM((TILES, LAT, WIDE), BF16),
    pltpu.VMEM((8, WIDE), F32),
)
VM = pl.BlockSpec(memory_space=pltpu.VMEM)
SM = pl.BlockSpec(memory_space=pltpu.SMEM)
HB = pl.BlockSpec(memory_space=pltpu.HBM)


def limit(mebibytes):
    return pltpu.CompilerParams(vmem_limit_bytes=mebibytes * 2**20)


def shape(*dims, kind=F32):
    return jax.ShapeDtypeStruct(dims, kind)


def pack_call(positions, velocity, species, region_count, neighbours):
    return pl.pallas_call(
        pack_kernel,
        name="pack",
        out_shape=(shape(9, 8, LANES), shape(9, 2, LANES), shape(9, 2, LANES)),
        in_specs=[HB] * 5,
        out_specs=(VM, VM, VM),
        scratch_shapes=(
            pltpu.VMEM((3, 3, 3, 2, 3), F32),
            pltpu.VMEM((3, 3, 3, 2, 3), F32),
            pltpu.VMEM((3, 3, 2, 3), jnp.int32),
            pltpu.VMEM((3, 3, 3), jnp.int32),
            pltpu.VMEM((3, 3, 3, 2, LISTED), jnp.int32),
            pltpu.SemaphoreType.DMA((5,)),
            pltpu.VMEM((256, LANES), F32),
            pltpu.VMEM((72, LANES), F32),
            pltpu.VMEM((72, LANES), F32),
        ),
    )(
        positions.transpose(0, 1, 2, 4, 3),
        velocity.transpose(0, 1, 2, 4, 3),
        species.transpose(0, 1, 3, 2),
        region_count,
        neighbours,
    )


def prep_call(basis_weight, species_embed, weight_map, scalar_map, energy_out, species_energy):
    return pl.pallas_call(
        prep_kernel,
        name="prep",
        out_shape=(
            shape(LAT, 16, kind=BF16),
            shape(16, LAT, kind=BF16),
            shape(CH, LAT, kind=BF16),
            shape(LAT, CH, kind=BF16),
            shape(LAT, CH, kind=BF16),
            shape(CH, LAT, kind=BF16),
            shape(LAT, LANES),
            shape(4, ROWS, LANES),
            shape(ROWS, DEPTH, kind=BF16),
            shape(8, LANES),
        ),
        in_specs=[HB] * 6,
        out_specs=(VM,) * 10,
        scratch_shapes=(
            pltpu.VMEM((NB, LAT), BF16),
            pltpu.VMEM((NSPEC, LAT), BF16),
            pltpu.VMEM((1, NSPEC), F32),
            pltpu.SemaphoreType.DMA((6,)),
        ),
        compiler_params=limit(4),
        cost_estimate=pl.CostEstimate(flops=1000000, transcendentals=0, bytes_accessed=2000000),
    )(
        basis_weight,
        species_embed,
        weight_map.T,
        scalar_map,
        energy_out[None, :],
        species_energy[None, :],
    )


def first_call(pieces, prepared):
    return pl.pallas_call(
        first_kernel,
        name="first",
        out_shape=(
            shape(72, LANES),
            shape(3, 8, LANES),
            shape(72, LANES),
            shape(1, LANES),
            shape(TILES, 24, WIDE),
            shape(2, kind=jnp.int32),
        ),
        in_specs=[VM] * (len(pieces) + len(prepared)),
        out_specs=(VM, VM, VM, VM, VM, SM),
        scratch_shapes=(
            pltpu.VMEM((ROWS, LANES), F32),
            pltpu.VMEM((2, 4 * LIST + 16, DEPTH), BF16),
            pltpu.VMEM((2, ROWS, LANES), F32),
            pltpu.VMEM((2, ROWS, LANES), F32),
            pltpu.VMEM((32, DEPTH), BF16),
            pltpu.VMEM((OWN, LANES), F32),
            *EVAL_SCRATCH,
        ),
        compiler_params=limit(20),
    )(*pieces, *prepared)


def second_call(pieces, weights, pairs, counts, energy, live):
    return pl.pallas_call(
        second_kernel,
        name="second",
        out_shape=(shape(72, LANES), shape(1, LANES)),
        in_specs=[VM] * (len(pieces) + len(weights) + 1) + [SM, VM, VM],
        out_specs=(VM, VM),
        scratch_shapes=(
            pltpu.VMEM((32, DEPTH), BF16),
            pltpu.VMEM((OWN, LANES), F32),
            *EVAL_SCRATCH,
        ),
        compiler_params=limit(20),
    )(*pieces, *weights, pairs, counts, energy, live)


def is_even(axis):
    return lax.axis_index(axis) % 2 == 0


def trade(across, within, axis):
    count = lax.axis_size(axis)
    inner = [(i, i ^ 1) for i in range(count)]
    outer = [(i, (i - 1) % count if i % 2 == 0 else (i + 1) % count) for i in range(count)]
    across = lax.ppermute(across, axis, outer)
    within = lax.ppermute(within, axis, inner)
    even = is_even(axis)
    return jnp.where(even, across, within), jnp.where(even, within, across)


def swap(low_part, high_part, axis):
    even = is_even(axis)
    return trade(jnp.where(even, low_part, high_part), jnp.where(even, high_part, low_part), axis)


def everywhere(row, axes):
    count = math.prod(lax.axis_size(axis) for axis in axes)
    rows = jnp.broadcast_to(row[None], (count, 1, LANES))
    rows = lax.all_to_all(rows, axes, 0, 0, tiled=False)
    return jnp.sum(rows, axis=0)


def spread_rows(rows, across, within, beside):
    low, high = trade(across, within, "gz")
    low, high = (v.reshape(3, 3, 2, LANES)[..., 0:HALF] for v in (low, high))
    rows = rows.reshape(3, 3, 8, LANES)[:, :, 2:5, 0:HALF]
    rows = jnp.concatenate([low, rows, high, jnp.zeros((3, 3, 1, HALF), F32)], axis=2)

    def joined(one, two):
        return jnp.concatenate([one, two], axis=-1)

    def parted(both):
        return jnp.stack([both[..., 0:HALF], both[..., HALF:]])

    low, high = swap(joined(rows[0], rows[1]), joined(rows[1], rows[2]), "gx")
    rows = jnp.concatenate([parted(low), rows, parted(high)], axis=0)
    rows, beside = lax.optimization_barrier((rows, beside))
    low, high = swap(joined(rows[:, 0], rows[:, 1]), joined(rows[:, 1], rows[:, 2]), "gy")
    return (low, rows, high), beside


def spread_moved(rows):
    low, high = swap(rows[:, 2:4], rows[:, 3:5], "gz")
    rows = jnp.concatenate([low, rows[:, 2:5], high, jnp.zeros((3, 1, LANES), F32)], axis=1)
    low, high = trade(rows, rows, "gx")
    rows = jnp.concatenate(
        [low[..., 48:80], rows[..., 32:80], high[..., 32:64], jnp.zeros((3, 8, 16), F32)], axis=-1
    )
    low, high = swap(rows[0:2], rows[1:3], "gy")
    return low, rows, high


def unpack(force):
    own = force.reshape(3, 3, 8, LANES)[:, :, 2:5, 0:6]
    return own.reshape(3, 3, 3, 2, 3).transpose(4, 0, 1, 2, 3)


def shards(positions, velocity, species, region_count, neighbours,
           basis_weight, species_embed, weight_map, scalar_map, energy_out, species_energy):
    sent = pack_call(positions, velocity, species, region_count, neighbours)
    prepared = prep_call(
        basis_weight, species_embed, weight_map, scalar_map, energy_out, species_energy
    )
    pieces, prepared = spread_rows(*sent, prepared)
    force_one, moved, live, energy_one, pairs, counts = first_call(pieces, prepared)
    force_two, energies = second_call(
        spread_moved(moved), prepared[0:7], pairs, counts, energy_one, live
    )
    totals = everywhere(everywhere(energies, ("gx", "gy")), ("gz",))
    forces = jnp.stack([unpack(force_one), unpack(force_two)])
    return forces, totals[0, 0:2] / totals[0, 2:4]


def solution(mesh):
    placed = (
        P(None, "gx", "gy", "gz", None),
        P(None, "gx", "gy", "gz", None),
        P("gx", "gy", "gz", None),
        P("gx", "gy", "gz"),
        P("gx", "gy", "gz", None, None),
        P(),
        P(),
        P(),
        P(),
        P(),
        P(),
    )
    return jax.shard_map(
        shards,
        mesh=mesh,
        in_specs=placed,
        out_specs=(P(None, None, "gx", "gy", "gz", None), P()),
        check_vma=False,
    )
```

```python
import math

import jax
import jax.numpy as jnp
from jax import lax
from jax.experimental import pallas as pl
from jax.experimental.pallas import tpu as pltpu
from jax.sharding import PartitionSpec as P


cutoff = 6.0
env_scale = 0.25
domain_side = 18.0
time_step = 0.15
atom_masses = (1.008, 12.011, 14.007, 15.999, 32.06)

CH = 64
LAT = 128
NB = 8
NSPEC = 5
LIST = 24
LISTED = 40
USED = 392
ROWS = 400
LAYER = 64
DEPTH = 512
INNER = 256
OWN = 80
WIDE = 256
TILES = 26
LANES = 128
HALF = 64
POS, KIND, VEL, LIVE, NEIGH = 0, 6, 8, 14, 16
MISC = NEIGH + 2 * LIST
F32 = jnp.float32
BF16 = jnp.bfloat16


def mm(a, b):
    return lax.dot_general(a, b, (((1,), (0,)), ((), ())), preferred_element_type=F32)


def mm_nt(a, b):
    return lax.dot_general(a, b, (((1,), (1,)), ((), ())), preferred_element_type=F32)


def split2(v):
    high = v.astype(BF16)
    return high, (v - high.astype(F32)).astype(BF16)


def iota(shape, dim):
    return lax.broadcasted_iota(jnp.int32, shape, dim).astype(F32)


def sigmoid(v):
    return 1.0 / (1.0 + jnp.exp(-v))


def row_coords(row):
    xy = jnp.floor(row * 0.125)
    z = row - 8.0 * xy
    x = jnp.floor((xy + 0.5) * (1.0 / 7.0))
    return x, xy - 7.0 * x, z


def away(x, y, z):
    return jnp.maximum(jnp.maximum(jnp.abs(x - 3.0), jnp.abs(y - 3.0)), jnp.abs(z - 3.0))


def far_coords(x, y, z, entry):
    q = jnp.floor(entry * 0.5)
    a = jnp.floor((q + 0.5) * (1.0 / 25.0))
    ab = jnp.floor((q + 0.5) * (1.0 / 5.0))
    steps = (a, ab - 5.0 * a, q - 5.0 * ab)
    far = [3.0 * jnp.floor((v + 1.5) * (1.0 / 3.0)) + s - 2.0 for v, s in zip((x, y, z), steps)]
    shift = [(jnp.floor((s + 2.5) * (1.0 / 3.0)) - 1.0) * domain_side for s in steps]
    return far, shift, entry - 2.0 * q


def one_hot(index, count, depth):
    hit = (iota((count, index.shape[1]), 0) == index).astype(F32).astype(BF16)
    return deepen(hit, depth)


def deepen(values, depth):
    more = depth - values.shape[0]
    if more == 0:
        return values
    return jnp.concatenate([values, jnp.zeros((more, values.shape[1]), values.dtype)], axis=0)


def build_pairs(rows_ref, base_ref, below_ref, table, off_ref, end_ref, pairs_ref, listed_t):
    lane = iota((ROWS, LANES), 1)
    entry = rows_ref[0:ROWS]
    listed = (lane >= NEIGH) & (lane < MISC) & (entry >= 0.0)
    q = jnp.floor(entry * 0.5)
    a = jnp.floor((q + 0.5) * (1.0 / 25.0))
    ab = jnp.floor((q + 0.5) * (1.0 / 5.0))
    far = jnp.maximum(jnp.abs(base_ref[0] + a), jnp.abs(base_ref[1] + (ab - 5.0 * a)))
    far = jnp.maximum(far, jnp.abs(base_ref[2] + (q - 5.0 * ab)))
    nearest = jnp.where(listed, jnp.minimum(base_ref[3], far), 9.0)
    kept = (nearest < 1.5, (nearest > 1.5) & (nearest < 2.5))
    upto = iota((2 * LIST, LANES), 0) + NEIGH
    place = iota((2 * LIST, LANES), 1)
    keys = (place <= upto).astype(F32) + (place < upto).astype(F32)
    keys = keys.astype(BF16)
    ones = jnp.ones((LANES, LANES), BF16)
    cx, cy, cz = row_coords(iota((1, DEPTH), 1))
    keeps = [deepen(keep.astype(F32).astype(BF16), DEPTH) for keep in kept]
    counts = [mm(keep, ones) for keep in keeps]
    counts_t = [mm_nt(ones[0:16], keep).astype(BF16) for keep in keeps]
    below = below_ref[...]
    offsets = mm(below, jnp.concatenate(counts, axis=1).astype(BF16))
    offsets_t = mm_nt(jnp.concatenate(counts_t, axis=0), below)
    first = jnp.zeros((1, 1), F32)
    ends = []
    for which, keep in enumerate(keeps):
        offset = offsets[:, which * LANES : (which + 1) * LANES] + first
        end = offset + counts[which][0:ROWS]
        off_ref[which] = offset
        end_ref[which] = end
        offset_t = offsets_t[16 * which : 16 * which + 1] + first
        offset_t = jnp.concatenate([offset_t, jnp.zeros((1, DEPTH - ROWS), F32)], axis=1)
        high = jnp.floor(offset_t * (1.0 / 256.0))
        misc = jnp.concatenate(
            [high, offset_t - 256.0 * high, cx, cy, cz, jnp.zeros((11, DEPTH), F32)], axis=0
        )
        table[which, 0 : 2 * LIST] = listed_t
        table[which, 2 * LIST : 4 * LIST] = mm_nt(keys, keep).astype(BF16)
        table[which, 4 * LIST :] = misc.astype(BF16)
        first = jnp.max(jnp.max(end, axis=0, keepdims=True), axis=1, keepdims=True)
        ends.append(jnp.max(first))
    first = jnp.float32(0.0)
    totals = []
    for which, total in enumerate(ends):

        def body(k, carry, which=which, first=first, total=total):
            place = iota((1, WIDE), 1) + (k * WIDE).astype(F32)
            offset = off_ref[which]
            end = end_ref[which]
            hit = jnp.concatenate(
                [
                    ((offset <= part) & (end > part)).astype(F32).astype(BF16)
                    for part in (place[:, 0:LANES], place[:, LANES:])
                ],
                axis=1,
            )
            got = mm(table[which], deepen(hit, DEPTH))
            misc = got[4 * LIST :]
            wanted = 2.0 * (place - (256.0 * misc[0:1] + misc[1:2])) + 1.0
            chosen = (got[2 * LIST : 4 * LIST] == wanted).astype(F32)
            entry = jnp.sum(chosen * got[0 : 2 * LIST], axis=0, keepdims=True)
            slot = jnp.sum(chosen[LIST:], axis=0, keepdims=True)
            x, y, z = misc[2:3], misc[3:4], misc[4:5]
            far, shift, far_slot = far_coords(x, y, z, entry)
            valid = place < total
            away_i, away_j = away(x, y, z), away(*far)

            def where(flag, value):
                return jnp.where(flag, value, -1.0)

            def region(c):
                return c[1] * 8.0 + c[2]

            def inner(c, s):
                return (((c[0] - 1.0) * 5.0 + (c[1] - 1.0)) * 5.0 + (c[2] - 1.0)) * 2.0 + s

            def own(c):
                return ((c[0] - 2.0) * 3.0 + (c[1] - 2.0)) * 8.0 + c[2]

            near = (x, y, z)
            lines = [
                where(valid, region(near)),
                slot,
                where(valid, region(far)),
                far_slot,
                where(valid & (away_i < 2.5), inner(near, slot)),
                where(valid & (away_j < 2.5), inner(far, far_slot)),
                where(valid & (away_i < 1.5), own(near)),
                where(valid & (away_j < 1.5), own(far)),
                valid.astype(F32),
                *shift,
                (valid & (away_i < 1.5)).astype(F32),
                near[0],
                far[0],
                jnp.zeros((9, WIDE), F32),
            ]
            pairs_ref[k] = jnp.where(place < first, pairs_ref[k], jnp.concatenate(lines, axis=0))
            return carry

        last = total.astype(jnp.int32)
        lax.fori_loop(
            first.astype(jnp.int32) // WIDE, (last + (WIDE - 1)) // WIDE, body, jnp.int32(0)
        )
        totals.append((last + (WIDE - 1)) // WIDE)
        first = total
    return totals


def turns(radius):
    part = radius * (1.0 / 12.0)
    part = part - jnp.floor(part + 0.5)
    half = part * math.pi
    sq = half * half
    s = jnp.full_like(sq, -1.0 / 39916800.0)
    for c in (1.0 / 362880.0, -1.0 / 5040.0, 1.0 / 120.0, -1.0 / 6.0, 1.0):
        s = s * sq + c
    s = s * half
    c = jnp.full_like(sq, 1.0 / 479001600.0)
    for k in (-1.0 / 3628800.0, 1.0 / 40320.0, -1.0 / 720.0, 1.0 / 24.0, -0.5, 1.0):
        c = c * sq + k
    return 2.0 * s * c, 1.0 - 2.0 * s * s


def evaluate(refs, scratch, counts, own_out, moved):
    pos_t, pairs_ref, w1t, w1, wmt, wm, smt, sm, eo_ref = refs
    env_ref, envs_ref, grad_ref, geo_ref, feat_ref, lat_ref, slope_ref, h_ref, wb_ref, hp_ref = (
        scratch[:-1]
    )
    en_ref = scratch[-1]
    front, every = counts
    norm = math.sqrt(2.0 / cutoff)

    def eo():
        return jnp.concatenate([eo_ref[...], eo_ref[...]], axis=1)

    env_ref[...] = jnp.zeros(env_ref.shape, F32)
    grad_ref[...] = jnp.zeros(grad_ref.shape, F32)
    en_ref[...] = jnp.zeros(en_ref.shape, F32)
    own_out[...] = jnp.zeros(own_out.shape, F32)

    def gathered(place, layer, slot):
        got = mm(pos_t[...], one_hot(place, LAYER, LAYER))
        full = jnp.zeros((8, WIDE), F32)
        for x in range(7):
            at = 8 * x
            part = got[at : at + 8] + got[LAYER + at : LAYER + at + 8]
            part = part + got[2 * LAYER + at : 2 * LAYER + at + 8]
            full = full + jnp.where(layer == float(x), part, 0.0)
        second = slot > 0.5
        point = jnp.where(second, full[3:6], full[0:3])
        return point, jnp.where(second, full[7:8], full[6:7])

    def shape_pairs(t):
        pair = pairs_ref[t]
        valid = pair[8:9]
        near, near_kind = gathered(pair[0:1], pair[13:14], pair[1:2])
        far, far_kind = gathered(pair[2:3], pair[14:15], pair[3:4])
        if moved:
            near_kind, far_kind = pair[15:16], pair[16:17]
        else:
            pairs_ref[t, 15:17] = jnp.concatenate([near_kind, far_kind], axis=0)
        d = far - near + pair[9:12]
        square = jnp.sum(d * d, axis=0, keepdims=True)
        square = jnp.where(valid > 0.5, square, 1.0)
        radius = jnp.sqrt(square)
        inverse = 1.0 / radius
        u = d * inverse
        y = jnp.minimum(radius * (1.0 / cutoff), 1.0)
        y2 = y * y
        y5 = y2 * y2 * y
        f = 1.0 + y5 * y * (-28.0 + y * (48.0 - 21.0 * y))
        fd = y5 * (-168.0 + y * (336.0 - 168.0 * y)) * (1.0 / cutoff)
        sin1, cos1 = turns(radius)
        sines, cosines = [jnp.zeros_like(sin1), sin1], [jnp.ones_like(cos1), cos1]
        for _ in range(NB - 1):
            sines.append(2.0 * cos1 * sines[-1] - sines[-2])
            cosines.append(2.0 * cos1 * cosines[-1] - cosines[-2])
        basis = [norm * inverse * s for s in sines[1:]]
        slope = [
            norm * (k * (math.pi / cutoff)) * inverse * c - inverse * b
            for k, (c, b) in enumerate(zip(cosines[1:], basis), 1)
        ]
        kinds = [
            (near_kind == float(k)).astype(F32) + (far_kind == float(k)).astype(F32)
            for k in range(NSPEC)
        ]
        feats = jnp.concatenate(basis + kinds + [jnp.zeros((3, WIDE), F32)], axis=0)
        geo_ref[t, 0:16] = jnp.concatenate(
            [u, inverse, f, fd, jnp.zeros((2, WIDE), F32)] + slope, axis=0
        )
        feat_ref[t] = feats.astype(BF16)

    def stage_one(t, carry):
        shape_pairs(t)
        pair = pairs_ref[t]
        geo = geo_ref[t]
        valid, u, f = pair[8:9], geo[0:3], geo[4:5]
        pre = mm(w1t[...], feat_ref[t])
        gate = sigmoid(pre)
        lat = (pre * gate).astype(BF16)
        lat_ref[t] = lat
        slope_ref[t] = gate * (1.0 + pre * (1.0 - gate))
        h = mm(wmt[...], lat)
        h_ref[t] = h
        w = h * (f * valid)
        hit_i = one_hot(pair[4:5], INNER, INNER)
        hit_j = one_hot(pair[5:6], INNER, INNER)
        moments = jnp.concatenate([w, w * u[0:1], w * u[1:2], w * u[2:3]], axis=0).astype(BF16)
        env_ref[0:CH] += mm_nt(moments[0:CH], hit_i + hit_j)
        env_ref[CH:] += mm_nt(moments[CH:], hit_i - hit_j)
        return carry

    lax.fori_loop(0, every, stage_one, jnp.int32(0))
    envs_ref[...] = env_ref[...].astype(BF16)

    def stage_two(t, carry):
        pair = pairs_ref[t]
        geo = geo_ref[t]
        valid = pair[8:9]
        u = geo[0:3]
        f = geo[4:5]
        hit = one_hot(pair[4:5], INNER, INNER)
        env = mm(envs_ref[...], hit)
        aligned = (
            env[0:CH]
            + u[0:1] * env[CH : 2 * CH]
            + u[1:2] * env[2 * CH : 3 * CH]
            + u[2:3] * env[3 * CH :]
        )
        w = h_ref[t] * (f * valid)
        coupling = (env_scale * w * aligned).astype(BF16)
        arg = lat_ref[t].astype(F32) + mm(smt[...], coupling)
        gate = sigmoid(arg)
        hidden = arg * gate
        dotted = jnp.sum(hidden * eo(), axis=0, keepdims=True)
        en_ref[0:1] += f * dotted * pair[12:13]
        arg_bar = (f * valid) * eo() * (gate * (1.0 + arg * (1.0 - gate)))
        arg_bar = arg_bar.astype(BF16)
        hp_ref[t] = arg_bar
        c_bar = mm(sm[...], arg_bar).astype(BF16).astype(F32)
        wb_ref[t] = env_scale * aligned * c_bar
        al_bar = env_scale * w * c_bar
        geo_ref[t, 6:7] = dotted * valid
        u_bar = [
            jnp.sum(al_bar * env[(k + 1) * CH : (k + 2) * CH], axis=0, keepdims=True)
            for k in range(3)
        ]
        geo_ref[t, 16:19] = jnp.concatenate(u_bar, axis=0)
        pulls = jnp.concatenate(
            [al_bar, al_bar * u[0:1], al_bar * u[1:2], al_bar * u[2:3]], axis=0
        )
        grad_ref[...] += mm_nt(pulls.astype(BF16), hit)
        return carry

    lax.fori_loop(0, every, stage_two, jnp.int32(0))
    envs_ref[...] = grad_ref[...].astype(BF16)

    def stage_three(t, carry):
        pair = pairs_ref[t]
        geo = geo_ref[t]
        valid = pair[8:9]
        u, inverse, f, fd = geo[0:3], geo[3:4], geo[4:5], geo[5:6]
        hit_i = one_hot(pair[4:5], INNER, INNER)
        hit_j = one_hot(pair[5:6], INNER, INNER)
        grad = envs_ref[...]
        g0 = mm(grad[0:CH], hit_i + hit_j)
        gv = mm(grad[CH:], hit_i - hit_j)
        parts = [gv[k * CH : (k + 1) * CH] for k in range(3)]
        h = h_ref[t]
        w = h * (f * valid)
        w_bar = wb_ref[t] + g0 + u[0:1] * parts[0] + u[1:2] * parts[1] + u[2:3] * parts[2]
        u_bar = geo[16:19] + jnp.concatenate(
            [jnp.sum(w * part, axis=0, keepdims=True) for part in parts], axis=0
        )
        f_bar = geo[6:7] + jnp.sum(h * w_bar, axis=0, keepdims=True)
        h_bar = (w_bar * (f * valid)).astype(BF16)
        lat_bar = (mm(wm[...], h_bar).astype(BF16) + hp_ref[t]).astype(F32)
        pre_bar = (lat_bar * slope_ref[t]).astype(BF16)
        basis_bar = mm(w1[...], pre_bar)[0:NB].astype(BF16).astype(F32)
        r_bar = jnp.sum(basis_bar * geo[8:16], axis=0, keepdims=True) + f_bar * fd
        along = jnp.sum(u * u_bar, axis=0, keepdims=True)
        d_bar = (r_bar * u + (u_bar - u * along) * inverse) * valid
        blank = jnp.zeros((2, WIDE), F32)

        def slotted(values, slot):
            second = slot > 0.5
            return jnp.concatenate(
                [jnp.where(second, 0.0, values), jnp.where(second, values, 0.0), blank], axis=0
            )

        pulls = jnp.concatenate(
            [slotted(d_bar, pair[1:2]), slotted(-d_bar, pair[3:4])], axis=1
        )
        high, low = split2(jnp.concatenate([pulls, jnp.zeros((120, 2 * WIDE), F32)], axis=0))
        where = jnp.concatenate([one_hot(pair[6:7], OWN, OWN), one_hot(pair[7:8], OWN, OWN)], axis=1)
        own_out[...] += mm_nt(where, high) + mm_nt(where, low)
        return carry

    lax.fori_loop(0, front, stage_three, jnp.int32(0))


def load_rows(rows_ref, low, own, high):
    rows_ref[0:ROWS] = jnp.zeros((ROWS, LANES), F32)
    for i in range(7):
        at = i * 56
        for piece, start in ((low, 0), (high, 40)):
            both = piece[i]
            rows_ref[at + start : at + start + 8] = both
            rows_ref[at + start + 8 : at + start + 16] = pltpu.roll(both, HALF, 1)
        for j in range(3):
            rows_ref[at + 16 + 8 * j : at + 24 + 8 * j, 0:HALF] = own[i, j]


def own_rows(rows_ref):
    return jnp.concatenate(
        [rows_ref[(i * 7 + 2) * 8 : (i * 7 + 5) * 8] for i in range(2, 5)], axis=0
    )


def put_positions(turned, pos_t):
    one = turned.astype(BF16)
    rest = turned - one.astype(F32)
    two = rest.astype(BF16)
    three = (rest - two.astype(F32)).astype(BF16)
    for i, part in enumerate((one, two, three)):
        pos_t[i * LAYER : (i + 1) * LAYER] = part[:, 0:LAYER]


def fetch(copies, sems):
    made = [pltpu.make_async_copy(src, dst, sems.at[i]) for i, (src, dst) in enumerate(copies)]
    for copy in made:
        copy.start()

    def wait():
        for copy in made:
            copy.wait()

    return wait


def pack_kernel(pos_in, vel_in, kind_in, count_in, list_in, out, across, within,
                pos, vel, kind, count, lists, sems, grid, first_list, second_list):
    even = lax.axis_index("gz") % 2 == 0
    fetch(
        ((pos_in, pos), (vel_in, vel), (kind_in, kind), (count_in, count), (list_in, lists)), sems
    )()
    for x in range(3):
        for y in range(3):
            at = (3 * x + y) * 16
            for s in range(2):
                for c in range(3):
                    grid[at + POS + 3 * s + c : at + POS + 3 * s + c + 1, 2:5] = pos[c, x, y, s : s + 1]
                    grid[at + VEL + 3 * s + c : at + VEL + 3 * s + c + 1, 2:5] = vel[c, x, y, s : s + 1]
                grid[at + KIND + s : at + KIND + s + 1, 2:5] = kind[x, y, s : s + 1].astype(F32)
                grid[at + LIVE + s : at + LIVE + s + 1, 2:5] = (
                    count[x, y : y + 1] > s
                ).astype(F32)
            row = (3 * x + y) * 8 + 2
            first_list[row : row + 3, 0:LISTED] = lists[x, y, :, 0].astype(F32)
            second_list[row : row + 3, 0:LISTED] = lists[x, y, :, 1].astype(F32)
    turned = jnp.concatenate(
        [jnp.transpose(grid[0:128])[0:8], jnp.transpose(grid[128:256])[0:8]], axis=1
    )
    lane = iota((8, LANES), 1)
    row = iota((8, LANES), 0)
    inside = (row > 1.5) & (row < 4.5)
    for xy in range(9):
        half = turned[:, 0:LANES] if xy < 8 else turned[:, LANES:]
        shift = (xy % 8) * 16
        fields = pltpu.roll(half, (LANES - shift) % LANES, 1)
        one = pltpu.roll(first_list[xy * 8 : xy * 8 + 8], NEIGH, 1)
        two = pltpu.roll(second_list[xy * 8 : xy * 8 + 8], NEIGH + LIST, 1)
        merged = jnp.where(lane < NEIGH, fields, jnp.where(lane < NEIGH + LIST, one, two))
        merged = jnp.where(inside & (lane < MISC), merged, 0.0)
        out[xy] = merged
        across[xy] = jnp.where(even, merged[2:4], merged[3:5])
        within[xy] = jnp.where(even, merged[3:5], merged[2:4])


def prep_kernel(bw_in, se_in, wmt_in, sm_in, eo_in, table_in,
                w1t, w1, wmt, wm, smt, sm, eo, base, below, levels, bw, se, table, sems):
    fetch(
        (
            (bw_in, bw),
            (se_in, se),
            (wmt_in, wmt),
            (sm_in, sm),
            (eo_in, eo.at[0:1]),
            (table_in, table),
        ),
        sems,
    )()
    for k in range(NSPEC):
        levels[k : k + 1] = jnp.broadcast_to(table[0:1, k : k + 1], (1, LANES))
    both = jnp.concatenate(
        [bw[...].astype(F32), se[...].astype(F32), jnp.zeros((3, LAT), F32)], axis=0
    )
    w1[...] = both.astype(BF16)
    w1t[...] = jnp.transpose(deepen(both, LANES)).astype(BF16)[:, 0:16]
    wm[...] = jnp.transpose(deepen(wmt[...].astype(F32), LANES)).astype(BF16)[:, 0:CH]
    smt[...] = jnp.transpose(deepen(sm[...].astype(F32), LANES)).astype(BF16)[:, 0:CH]
    eo[...] = jnp.transpose(jnp.broadcast_to(eo[0:1], (LAT, LANES)))
    row = iota((ROWS, LANES), 0)
    x, y, z = row_coords(row)
    unused = (z > 6.5) | (row > USED - 0.5)
    for i, v in enumerate((x, y, z)):
        base[i] = jnp.where(unused, 99.0, 3.0 * jnp.floor((v + 1.5) * (1.0 / 3.0)) - 5.0)
    base[3] = jnp.where(unused, 99.0, away(x, y, z))
    below[...] = (iota((ROWS, DEPTH), 1) < iota((ROWS, DEPTH), 0)).astype(F32).astype(BF16)


def lanes_of(values, lane, first, second):
    return jnp.where(lane < 2.5, values[:, first : first + 1], values[:, second : second + 1])


def own_lane_row():
    lane = iota((72, LANES), 1)
    row = iota((72, LANES), 0)
    z = row - 8.0 * jnp.floor(row * 0.125)
    return lane, (z > 1.5) & (z < 4.5)


def first_kernel(low, own, high, w1t, w1, wmt, wm, smt, sm, eo, base, below, levels,
                 force_out, moved_out, live_out, energy_out, pairs_ref, counts_ref,
                 rows_ref, table, off_ref, end_ref, pos_t, own_ref, *scratch):
    load_rows(rows_ref, low, own, high)
    turned = jnp.transpose(deepen(rows_ref[0:ROWS], DEPTH))
    lane = iota((56, LANES), 1)
    layers = sum(
        pltpu.roll(jnp.where(lane < 8.0, rows_ref[x * 56 : x * 56 + 56], 0.0), 8 * x, 1)
        for x in range(7)
    )
    put_positions(jnp.transpose(deepen(layers, LANES))[0:LAYER], pos_t)
    front, every = build_pairs(
        rows_ref, base, below, table, off_ref, end_ref, pairs_ref, turned[NEIGH:MISC].astype(BF16)
    )
    counts_ref[0] = front
    counts_ref[1] = every
    refs = (pos_t, pairs_ref, w1t, w1, wmt, wm, smt, sm, eo)
    evaluate(refs, scratch, (front, every), own_ref, False)
    mine = own_rows(rows_ref)
    lane, inside = own_lane_row()
    kind3 = lanes_of(mine, lane, KIND, KIND + 1)
    speed = pltpu.roll(mine, LANES - VEL, 1)
    live3 = jnp.where(inside & (lane < 6.0), lanes_of(mine, lane, LIVE, LIVE + 1), 0.0)
    live_out[...] = live3
    force = jnp.where(inside & (lane < 6.0), own_ref[0:72] * live3, 0.0)
    force_out[...] = force
    inverse_mass = jnp.zeros((72, LANES), F32)
    for k, mass in enumerate(atom_masses):
        inverse_mass = jnp.where(kind3 == float(k), 1.0 / mass, inverse_mass)
    moved = mine + time_step * speed + 0.5 * time_step * time_step * inverse_mass * force
    moved = jnp.where(lane < 6.0, moved, 0.0)
    for y in range(3):
        moved_out[y] = sum(
            pltpu.roll(moved[(x * 3 + y) * 8 : (x * 3 + y) * 8 + 8], (x + 2) * 16, 1)
            for x in range(3)
        )
    live = pltpu.roll(mine, LANES - LIVE + KIND, 1)
    live = jnp.where(inside & (lane > 5.5) & (lane < 7.5), live, 0.0)
    atom = jnp.zeros((72, LANES), F32)
    for k in range(NSPEC):
        atom = jnp.where(mine == float(k), levels[k : k + 1], atom)
    atoms = jnp.sum(atom * live)
    energy_out[...] = energy_row(jnp.sum(scratch[-1][0:1]) + atoms, atoms, jnp.sum(live))


def second_kernel(low, own, high, w1t, w1, wmt, wm, smt, sm, eo, pairs_ref, counts_ref, energy_in,
                  live, force_out, energy_out, pos_t, own_ref, *scratch):
    layers = [piece[i] for piece, width in ((low, 2), (own, 3), (high, 2)) for i in range(width)]
    turned = jnp.transpose(deepen(jnp.concatenate(layers, axis=0), LANES))
    blocks = [turned[x * 16 : x * 16 + 8] for x in range(7)] + [jnp.zeros((8, LANES), F32)]
    put_positions(jnp.concatenate(blocks, axis=0), pos_t)
    refs = (pos_t, pairs_ref, w1t, w1, wmt, wm, smt, sm, eo)
    evaluate(refs, scratch, (counts_ref[0], counts_ref[1]), own_ref, True)
    lane, inside = own_lane_row()
    force_out[...] = jnp.where(inside & (lane < 6.0), own_ref[0:72] * live[...], 0.0)
    energy_out[...] = energy_in[...] + energy_row(0.0, jnp.sum(scratch[-1][0:1]), 0.0)


def energy_row(first, second, live):
    lane = iota((1, LANES), 1)
    return (
        jnp.where(lane == 0.0, first, 0.0)
        + jnp.where(lane == 1.0, second, 0.0)
        + jnp.where((lane == 2.0) | (lane == 3.0), live, 0.0)
    )


EVAL_SCRATCH = (
    pltpu.VMEM((4 * CH, INNER), F32),
    pltpu.VMEM((4 * CH, INNER), BF16),
    pltpu.VMEM((4 * CH, INNER), F32),
    pltpu.VMEM((TILES, 24, WIDE), F32),
    pltpu.VMEM((TILES, 16, WIDE), BF16),
    pltpu.VMEM((TILES, LAT, WIDE), BF16),
    pltpu.VMEM((TILES, LAT, WIDE), F32),
    pltpu.VMEM((TILES, CH, WIDE), F32),
    pltpu.VMEM((TILES, CH, WIDE), F32),
    pltpu.VMEM((TILES, LAT, WIDE), BF16),
    pltpu.VMEM((8, WIDE), F32),
)
VM = pl.BlockSpec(memory_space=pltpu.VMEM)
SM = pl.BlockSpec(memory_space=pltpu.SMEM)
HB = pl.BlockSpec(memory_space=pltpu.HBM)


def limit(mebibytes):
    return pltpu.CompilerParams(vmem_limit_bytes=mebibytes * 2**20)


def shape(*dims, kind=F32):
    return jax.ShapeDtypeStruct(dims, kind)


def pack_call(positions, velocity, species, region_count, neighbours):
    return pl.pallas_call(
        pack_kernel,
        name="pack",
        out_shape=(shape(9, 8, LANES), shape(9, 2, LANES), shape(9, 2, LANES)),
        in_specs=[HB] * 5,
        out_specs=(VM, VM, VM),
        scratch_shapes=(
            pltpu.VMEM((3, 3, 3, 2, 3), F32),
            pltpu.VMEM((3, 3, 3, 2, 3), F32),
            pltpu.VMEM((3, 3, 2, 3), jnp.int32),
            pltpu.VMEM((3, 3, 3), jnp.int32),
            pltpu.VMEM((3, 3, 3, 2, LISTED), jnp.int32),
            pltpu.SemaphoreType.DMA((5,)),
            pltpu.VMEM((256, LANES), F32),
            pltpu.VMEM((72, LANES), F32),
            pltpu.VMEM((72, LANES), F32),
        ),
    )(
        positions.transpose(0, 1, 2, 4, 3),
        velocity.transpose(0, 1, 2, 4, 3),
        species.transpose(0, 1, 3, 2),
        region_count,
        neighbours,
    )


def prep_call(basis_weight, species_embed, weight_map, scalar_map, energy_out, species_energy):
    return pl.pallas_call(
        prep_kernel,
        name="prep",
        out_shape=(
            shape(LAT, 16, kind=BF16),
            shape(16, LAT, kind=BF16),
            shape(CH, LAT, kind=BF16),
            shape(LAT, CH, kind=BF16),
            shape(LAT, CH, kind=BF16),
            shape(CH, LAT, kind=BF16),
            shape(LAT, LANES),
            shape(4, ROWS, LANES),
            shape(ROWS, DEPTH, kind=BF16),
            shape(8, LANES),
        ),
        in_specs=[HB] * 6,
        out_specs=(VM,) * 10,
        scratch_shapes=(
            pltpu.VMEM((NB, LAT), BF16),
            pltpu.VMEM((NSPEC, LAT), BF16),
            pltpu.VMEM((1, NSPEC), F32),
            pltpu.SemaphoreType.DMA((6,)),
        ),
        compiler_params=limit(4),
        cost_estimate=pl.CostEstimate(flops=1000000, transcendentals=0, bytes_accessed=2000000),
    )(
        basis_weight,
        species_embed,
        weight_map.T,
        scalar_map,
        energy_out[None, :],
        species_energy[None, :],
    )


def first_call(pieces, prepared):
    return pl.pallas_call(
        first_kernel,
        name="first",
        out_shape=(
            shape(72, LANES),
            shape(3, 8, LANES),
            shape(72, LANES),
            shape(1, LANES),
            shape(TILES, 24, WIDE),
            shape(2, kind=jnp.int32),
        ),
        in_specs=[VM] * (len(pieces) + len(prepared)),
        out_specs=(VM, VM, VM, VM, VM, SM),
        scratch_shapes=(
            pltpu.VMEM((ROWS, LANES), F32),
            pltpu.VMEM((2, 4 * LIST + 16, DEPTH), BF16),
            pltpu.VMEM((2, ROWS, LANES), F32),
            pltpu.VMEM((2, ROWS, LANES), F32),
            pltpu.VMEM((3 * LAYER, LAYER), BF16),
            pltpu.VMEM((OWN, LANES), F32),
            *EVAL_SCRATCH,
        ),
        compiler_params=limit(20),
    )(*pieces, *prepared)


def second_call(pieces, weights, pairs, counts, energy, live):
    return pl.pallas_call(
        second_kernel,
        name="second",
        out_shape=(shape(72, LANES), shape(1, LANES)),
        in_specs=[VM] * (len(pieces) + len(weights) + 1) + [SM, VM, VM],
        out_specs=(VM, VM),
        scratch_shapes=(
            pltpu.VMEM((3 * LAYER, LAYER), BF16),
            pltpu.VMEM((OWN, LANES), F32),
            *EVAL_SCRATCH,
        ),
        compiler_params=limit(20),
    )(*pieces, *weights, pairs, counts, energy, live)


def is_even(axis):
    return lax.axis_index(axis) % 2 == 0


def trade(across, within, axis):
    count = lax.axis_size(axis)
    inner = [(i, i ^ 1) for i in range(count)]
    outer = [(i, (i - 1) % count if i % 2 == 0 else (i + 1) % count) for i in range(count)]
    across = lax.ppermute(across, axis, outer)
    within = lax.ppermute(within, axis, inner)
    even = is_even(axis)
    return jnp.where(even, across, within), jnp.where(even, within, across)


def swap(low_part, high_part, axis):
    even = is_even(axis)
    return trade(jnp.where(even, low_part, high_part), jnp.where(even, high_part, low_part), axis)


def everywhere(row, axes, groups):
    rows = jnp.broadcast_to(row[None], (len(groups[0]), 1, LANES))
    rows = lax.all_to_all(rows, axes, 0, 0, axis_index_groups=groups, tiled=False)
    return jnp.sum(rows, axis=0)


def everyone(row):
    nx, ny, nz = (lax.axis_size(axis) for axis in ("gx", "gy", "gz"))
    part = nx // 3
    columns = [
        [(k * part + i) * ny + j for k in range(3) for j in range(ny)] for i in range(part)
    ]
    planes = [[(k * part + i) * nz + j for i in range(part) for j in range(nz)] for k in range(3)]
    return everywhere(everywhere(row, ("gx", "gy"), columns), ("gx", "gz"), planes)


def spread_rows(rows, across, within, beside):
    low, high = trade(across, within, "gz")
    low, high = (v.reshape(3, 3, 2, LANES)[..., 0:HALF] for v in (low, high))
    rows = rows.reshape(3, 3, 8, LANES)[:, :, 2:5, 0:HALF]
    rows = jnp.concatenate([low, rows, high, jnp.zeros((3, 3, 1, HALF), F32)], axis=2)

    def joined(one, two):
        return jnp.concatenate([one, two], axis=-1)

    def parted(both):
        return jnp.stack([both[..., 0:HALF], both[..., HALF:]])

    low, high = swap(joined(rows[0], rows[1]), joined(rows[1], rows[2]), "gx")
    rows = jnp.concatenate([parted(low), rows, parted(high)], axis=0)
    rows, beside = lax.optimization_barrier((rows, beside))
    low, high = swap(joined(rows[:, 0], rows[:, 1]), joined(rows[:, 1], rows[:, 2]), "gy")
    return (low, rows, high), beside


def spread_moved(rows):
    low, high = swap(rows[:, 2:4], rows[:, 3:5], "gz")
    rows = jnp.concatenate([low, rows[:, 2:5], high, jnp.zeros((3, 1, LANES), F32)], axis=1)
    low, high = trade(rows, rows, "gx")
    rows = jnp.concatenate(
        [low[..., 48:80], rows[..., 32:80], high[..., 32:64], jnp.zeros((3, 8, 16), F32)], axis=-1
    )
    low, high = swap(rows[0:2], rows[1:3], "gy")
    return low, rows, high


def unpack(force):
    own = force.reshape(3, 3, 8, LANES)[:, :, 2:5, 0:6]
    return own.reshape(3, 3, 3, 2, 3).transpose(4, 0, 1, 2, 3)


def shards(positions, velocity, species, region_count, neighbours,
           basis_weight, species_embed, weight_map, scalar_map, energy_out, species_energy):
    sent = pack_call(positions, velocity, species, region_count, neighbours)
    prepared = prep_call(
        basis_weight, species_embed, weight_map, scalar_map, energy_out, species_energy
    )
    pieces, prepared = spread_rows(*sent, prepared)
    force_one, moved, live, energy_one, pairs, counts = first_call(pieces, prepared)
    force_two, energies = second_call(
        spread_moved(moved), prepared[0:7], pairs, counts, energy_one, live
    )
    totals = everyone(energies)
    forces = jnp.stack([unpack(force_one), unpack(force_two)])
    return forces, totals[0, 0:2] / totals[0, 2:4]


def solution(mesh):
    placed = (
        P(None, "gx", "gy", "gz", None),
        P(None, "gx", "gy", "gz", None),
        P("gx", "gy", "gz", None),
        P("gx", "gy", "gz"),
        P("gx", "gy", "gz", None, None),
        P(),
        P(),
        P(),
        P(),
        P(),
        P(),
    )
    return jax.shard_map(
        shards,
        mesh=mesh,
        in_specs=placed,
        out_specs=(P(None, None, "gx", "gy", "gz", None), P()),
        check_vma=False,
    )
```

```python
import math

import jax
import jax.numpy as jnp
from jax import lax
from jax.experimental import pallas as pl
from jax.experimental.pallas import tpu as pltpu
from jax.sharding import PartitionSpec as P


cutoff = 6.0
env_scale = 0.25
domain_side = 18.0
time_step = 0.15
atom_masses = (1.008, 12.011, 14.007, 15.999, 32.06)

CH = 64
LAT = 128
NB = 8
NSPEC = 5
LIST = 24
LISTED = 40
USED = 392
ROWS = 400
LAYER = 64
DEPTH = 512
INNER = 256
OWN = 80
WIDE = 256
TILES = 26
LANES = 128
HALF = 64
POS, KIND, VEL, LIVE, NEIGH = 0, 6, 8, 14, 16
MISC = NEIGH + 2 * LIST
F32 = jnp.float32
BF16 = jnp.bfloat16


def mm(a, b):
    return lax.dot_general(a, b, (((1,), (0,)), ((), ())), preferred_element_type=F32)


def mm_nt(a, b):
    return lax.dot_general(a, b, (((1,), (1,)), ((), ())), preferred_element_type=F32)


def split2(v):
    high = v.astype(BF16)
    return high, (v - high.astype(F32)).astype(BF16)


def iota(shape, dim):
    return lax.broadcasted_iota(jnp.int32, shape, dim).astype(F32)


def sigmoid(v):
    return 1.0 / (1.0 + jnp.exp(-v))


def row_coords(row):
    xy = jnp.floor(row * 0.125)
    z = row - 8.0 * xy
    x = jnp.floor((xy + 0.5) * (1.0 / 7.0))
    return x, xy - 7.0 * x, z


def away(x, y, z):
    return jnp.maximum(jnp.maximum(jnp.abs(x - 3.0), jnp.abs(y - 3.0)), jnp.abs(z - 3.0))


def far_coords(x, y, z, entry):
    q = jnp.floor(entry * 0.5)
    a = jnp.floor((q + 0.5) * (1.0 / 25.0))
    ab = jnp.floor((q + 0.5) * (1.0 / 5.0))
    steps = (a, ab - 5.0 * a, q - 5.0 * ab)
    far = [3.0 * jnp.floor((v + 1.5) * (1.0 / 3.0)) + s - 2.0 for v, s in zip((x, y, z), steps)]
    shift = [(jnp.floor((s + 2.5) * (1.0 / 3.0)) - 1.0) * domain_side for s in steps]
    return far, shift, entry - 2.0 * q


def one_hot(index, count, depth):
    hit = (iota((count, index.shape[1]), 0) == index).astype(F32).astype(BF16)
    return deepen(hit, depth)


def deepen(values, depth):
    more = depth - values.shape[0]
    if more == 0:
        return values
    return jnp.concatenate([values, jnp.zeros((more, values.shape[1]), values.dtype)], axis=0)


def build_pairs(rows_ref, base_ref, below_ref, table, off_ref, end_ref, pairs_ref, listed_t):
    lane = iota((ROWS, LANES), 1)
    entry = rows_ref[0:ROWS]
    listed = (lane >= NEIGH) & (lane < MISC) & (entry >= 0.0)
    q = jnp.floor(entry * 0.5)
    a = jnp.floor((q + 0.5) * (1.0 / 25.0))
    ab = jnp.floor((q + 0.5) * (1.0 / 5.0))
    far = jnp.maximum(jnp.abs(base_ref[0] + a), jnp.abs(base_ref[1] + (ab - 5.0 * a)))
    far = jnp.maximum(far, jnp.abs(base_ref[2] + (q - 5.0 * ab)))
    nearest = jnp.where(listed, jnp.minimum(base_ref[3], far), 9.0)
    kept = (nearest < 1.5, (nearest > 1.5) & (nearest < 2.5))
    upto = iota((2 * LIST, LANES), 0) + NEIGH
    place = iota((2 * LIST, LANES), 1)
    keys = (place <= upto).astype(F32) + (place < upto).astype(F32)
    keys = keys.astype(BF16)
    ones = jnp.ones((LANES, LANES), BF16)
    cx, cy, cz = row_coords(iota((1, DEPTH), 1))
    keeps = [deepen(keep.astype(F32).astype(BF16), DEPTH) for keep in kept]
    counts = [mm(keep, ones) for keep in keeps]
    counts_t = [mm_nt(ones[0:16], keep).astype(BF16) for keep in keeps]
    below = below_ref[...]
    offsets = mm(below, jnp.concatenate(counts, axis=1).astype(BF16))
    offsets_t = mm_nt(jnp.concatenate(counts_t, axis=0), below)
    first = jnp.zeros((1, 1), F32)
    ends = []
    for which, keep in enumerate(keeps):
        offset = offsets[:, which * LANES : (which + 1) * LANES] + first
        end = offset + counts[which][0:ROWS]
        off_ref[which] = offset
        end_ref[which] = end
        offset_t = offsets_t[16 * which : 16 * which + 1] + first
        offset_t = jnp.concatenate([offset_t, jnp.zeros((1, DEPTH - ROWS), F32)], axis=1)
        high = jnp.floor(offset_t * (1.0 / 256.0))
        misc = jnp.concatenate(
            [high, offset_t - 256.0 * high, cx, cy, cz, jnp.zeros((11, DEPTH), F32)], axis=0
        )
        table[which, 0 : 2 * LIST] = listed_t
        table[which, 2 * LIST : 4 * LIST] = mm_nt(keys, keep).astype(BF16)
        table[which, 4 * LIST :] = misc.astype(BF16)
        first = jnp.max(jnp.max(end, axis=0, keepdims=True), axis=1, keepdims=True)
        ends.append(jnp.max(first))
    first = jnp.float32(0.0)
    totals = []
    for which, total in enumerate(ends):

        def body(k, carry, which=which, first=first, total=total):
            place = iota((1, WIDE), 1) + (k * WIDE).astype(F32)
            offset = off_ref[which]
            end = end_ref[which]
            hit = jnp.concatenate(
                [
                    ((offset <= part) & (end > part)).astype(F32).astype(BF16)
                    for part in (place[:, 0:LANES], place[:, LANES:])
                ],
                axis=1,
            )
            got = mm(table[which], deepen(hit, DEPTH))
            misc = got[4 * LIST :]
            wanted = 2.0 * (place - (256.0 * misc[0:1] + misc[1:2])) + 1.0
            chosen = (got[2 * LIST : 4 * LIST] == wanted).astype(F32)
            entry = jnp.sum(chosen * got[0 : 2 * LIST], axis=0, keepdims=True)
            slot = jnp.sum(chosen[LIST:], axis=0, keepdims=True)
            x, y, z = misc[2:3], misc[3:4], misc[4:5]
            far, shift, far_slot = far_coords(x, y, z, entry)
            valid = place < total
            away_i, away_j = away(x, y, z), away(*far)

            def where(flag, value):
                return jnp.where(flag, value, -1.0)

            def region(c):
                return c[1] * 8.0 + c[2]

            def inner(c, s):
                return (((c[0] - 1.0) * 5.0 + (c[1] - 1.0)) * 5.0 + (c[2] - 1.0)) * 2.0 + s

            def own(c):
                return ((c[0] - 2.0) * 3.0 + (c[1] - 2.0)) * 8.0 + c[2]

            near = (x, y, z)
            lines = [
                where(valid, region(near)),
                slot,
                where(valid, region(far)),
                far_slot,
                where(valid & (away_i < 2.5), inner(near, slot)),
                where(valid & (away_j < 2.5), inner(far, far_slot)),
                where(valid & (away_i < 1.5), own(near)),
                where(valid & (away_j < 1.5), own(far)),
                valid.astype(F32),
                *shift,
                (valid & (away_i < 1.5)).astype(F32),
                near[0],
                far[0],
                jnp.zeros((9, WIDE), F32),
            ]
            pairs_ref[k] = jnp.where(place < first, pairs_ref[k], jnp.concatenate(lines, axis=0))
            return carry

        last = total.astype(jnp.int32)
        lax.fori_loop(
            first.astype(jnp.int32) // WIDE, (last + (WIDE - 1)) // WIDE, body, jnp.int32(0)
        )
        totals.append((last + (WIDE - 1)) // WIDE)
        first = total
    return totals


def turns(radius):
    part = radius * (1.0 / 12.0)
    part = part - jnp.floor(part + 0.5)
    half = part * math.pi
    sq = half * half
    s = jnp.full_like(sq, -1.0 / 39916800.0)
    for c in (1.0 / 362880.0, -1.0 / 5040.0, 1.0 / 120.0, -1.0 / 6.0, 1.0):
        s = s * sq + c
    s = s * half
    c = jnp.full_like(sq, 1.0 / 479001600.0)
    for k in (-1.0 / 3628800.0, 1.0 / 40320.0, -1.0 / 720.0, 1.0 / 24.0, -0.5, 1.0):
        c = c * sq + k
    return 2.0 * s * c, 1.0 - 2.0 * s * s


def evaluate(refs, scratch, counts, own_out, moved, early=False):
    pos_t, pairs_ref, w1t, w1, wmt, wm, smt, sm, eo_ref = refs
    env_ref, envs_ref, grad_ref, geo_ref, feat_ref, lat_ref, slope_ref, h_ref, wb_ref, hp_ref = (
        scratch[:-1]
    )
    en_ref = scratch[-1]
    front, every = counts
    norm = math.sqrt(2.0 / cutoff)

    def eo():
        return jnp.concatenate([eo_ref[...], eo_ref[...]], axis=1)

    env_ref[...] = jnp.zeros(env_ref.shape, F32)
    grad_ref[...] = jnp.zeros(grad_ref.shape, F32)
    en_ref[...] = jnp.zeros(en_ref.shape, F32)
    if not early:
        own_out[...] = jnp.zeros(own_out.shape, F32)

    def gathered(place, layer, slot):
        got = mm(pos_t[...], one_hot(place, LAYER, LAYER))
        full = jnp.zeros((8, WIDE), F32)
        for x in range(7):
            at = 8 * x
            part = got[at : at + 8] + got[LAYER + at : LAYER + at + 8]
            part = part + got[2 * LAYER + at : 2 * LAYER + at + 8]
            full = full + jnp.where(layer == float(x), part, 0.0)
        second = slot > 0.5
        point = jnp.where(second, full[3:6], full[0:3])
        return point, jnp.where(second, full[7:8], full[6:7])

    def shape_pairs(t):
        pair = pairs_ref[t]
        valid = pair[8:9]
        near, near_kind = gathered(pair[0:1], pair[13:14], pair[1:2])
        far, far_kind = gathered(pair[2:3], pair[14:15], pair[3:4])
        if moved:
            near_kind, far_kind = pair[15:16], pair[16:17]
        else:
            pairs_ref[t, 15:17] = jnp.concatenate([near_kind, far_kind], axis=0)
        d = far - near + pair[9:12]
        square = jnp.sum(d * d, axis=0, keepdims=True)
        square = jnp.where(valid > 0.5, square, 1.0)
        radius = jnp.sqrt(square)
        inverse = 1.0 / radius
        u = d * inverse
        y = jnp.minimum(radius * (1.0 / cutoff), 1.0)
        y2 = y * y
        y5 = y2 * y2 * y
        f = 1.0 + y5 * y * (-28.0 + y * (48.0 - 21.0 * y))
        fd = y5 * (-168.0 + y * (336.0 - 168.0 * y)) * (1.0 / cutoff)
        sin1, cos1 = turns(radius)
        sines, cosines = [jnp.zeros_like(sin1), sin1], [jnp.ones_like(cos1), cos1]
        for _ in range(NB - 1):
            sines.append(2.0 * cos1 * sines[-1] - sines[-2])
            cosines.append(2.0 * cos1 * cosines[-1] - cosines[-2])
        basis = [norm * inverse * s for s in sines[1:]]
        slope = [
            norm * (k * (math.pi / cutoff)) * inverse * c - inverse * b
            for k, (c, b) in enumerate(zip(cosines[1:], basis), 1)
        ]
        kinds = [
            (near_kind == float(k)).astype(F32) + (far_kind == float(k)).astype(F32)
            for k in range(NSPEC)
        ]
        feats = jnp.concatenate(basis + kinds + [jnp.zeros((3, WIDE), F32)], axis=0)
        geo_ref[t, 0:16] = jnp.concatenate(
            [u, inverse, f, fd, jnp.zeros((2, WIDE), F32)] + slope, axis=0
        )
        feat_ref[t] = feats.astype(BF16)

    def stage_one(t, carry):
        shape_pairs(t)
        pair = pairs_ref[t]
        geo = geo_ref[t]
        valid, u, f = pair[8:9], geo[0:3], geo[4:5]
        pre = mm(w1t[...], feat_ref[t])
        gate = sigmoid(pre)
        lat = (pre * gate).astype(BF16)
        lat_ref[t] = lat
        slope_ref[t] = gate * (1.0 + pre * (1.0 - gate))
        h = mm(wmt[...], lat)
        h_ref[t] = h
        w = h * (f * valid)
        hit_i = one_hot(pair[4:5], INNER, INNER)
        hit_j = one_hot(pair[5:6], INNER, INNER)
        moments = jnp.concatenate([w, w * u[0:1], w * u[1:2], w * u[2:3]], axis=0).astype(BF16)
        env_ref[0:CH] += mm_nt(moments[0:CH], hit_i + hit_j)
        env_ref[CH:] += mm_nt(moments[CH:], hit_i - hit_j)
        return carry

    lax.fori_loop(0, front if early else every, stage_one, jnp.int32(0))
    envs_ref[...] = env_ref[...].astype(BF16)

    def forward(t):
        pair = pairs_ref[t]
        geo = geo_ref[t]
        valid = pair[8:9]
        u = geo[0:3]
        f = geo[4:5]
        hit = one_hot(pair[4:5], INNER, INNER)
        env = mm(envs_ref[...], hit)
        aligned = (
            env[0:CH]
            + u[0:1] * env[CH : 2 * CH]
            + u[1:2] * env[2 * CH : 3 * CH]
            + u[2:3] * env[3 * CH :]
        )
        w = h_ref[t] * (f * valid)
        coupling = (env_scale * w * aligned).astype(BF16)
        arg = lat_ref[t].astype(F32) + mm(smt[...], coupling)
        gate = sigmoid(arg)
        dotted = jnp.sum(arg * gate * eo(), axis=0, keepdims=True)
        return valid, u, f, hit, env, aligned, w, arg, gate, dotted, f * dotted * pair[12:13]

    def stage_energy(t, carry):
        en_ref[0:1] += forward(t)[-1]
        return carry

    if early:
        lax.fori_loop(0, front, stage_energy, jnp.int32(0))
        return

    def stage_two(t, carry):
        valid, u, f, hit, env, aligned, w, arg, gate, dotted, energy = forward(t)
        en_ref[0:1] += energy
        arg_bar = (f * valid) * eo() * (gate * (1.0 + arg * (1.0 - gate)))
        arg_bar = arg_bar.astype(BF16)
        hp_ref[t] = arg_bar
        c_bar = mm(sm[...], arg_bar).astype(BF16).astype(F32)
        wb_ref[t] = env_scale * aligned * c_bar
        al_bar = env_scale * w * c_bar
        geo_ref[t, 6:7] = dotted * valid
        u_bar = [
            jnp.sum(al_bar * env[(k + 1) * CH : (k + 2) * CH], axis=0, keepdims=True)
            for k in range(3)
        ]
        geo_ref[t, 16:19] = jnp.concatenate(u_bar, axis=0)
        pulls = jnp.concatenate(
            [al_bar, al_bar * u[0:1], al_bar * u[1:2], al_bar * u[2:3]], axis=0
        )
        grad_ref[...] += mm_nt(pulls.astype(BF16), hit)
        return carry

    lax.fori_loop(0, every, stage_two, jnp.int32(0))
    envs_ref[...] = grad_ref[...].astype(BF16)

    def stage_three(t, carry):
        pair = pairs_ref[t]
        geo = geo_ref[t]
        valid = pair[8:9]
        u, inverse, f, fd = geo[0:3], geo[3:4], geo[4:5], geo[5:6]
        hit_i = one_hot(pair[4:5], INNER, INNER)
        hit_j = one_hot(pair[5:6], INNER, INNER)
        grad = envs_ref[...]
        g0 = mm(grad[0:CH], hit_i + hit_j)
        gv = mm(grad[CH:], hit_i - hit_j)
        parts = [gv[k * CH : (k + 1) * CH] for k in range(3)]
        h = h_ref[t]
        w = h * (f * valid)
        w_bar = wb_ref[t] + g0 + u[0:1] * parts[0] + u[1:2] * parts[1] + u[2:3] * parts[2]
        u_bar = geo[16:19] + jnp.concatenate(
            [jnp.sum(w * part, axis=0, keepdims=True) for part in parts], axis=0
        )
        f_bar = geo[6:7] + jnp.sum(h * w_bar, axis=0, keepdims=True)
        h_bar = (w_bar * (f * valid)).astype(BF16)
        lat_bar = (mm(wm[...], h_bar).astype(BF16) + hp_ref[t]).astype(F32)
        pre_bar = (lat_bar * slope_ref[t]).astype(BF16)
        basis_bar = mm(w1[...], pre_bar)[0:NB].astype(BF16).astype(F32)
        r_bar = jnp.sum(basis_bar * geo[8:16], axis=0, keepdims=True) + f_bar * fd
        along = jnp.sum(u * u_bar, axis=0, keepdims=True)
        d_bar = (r_bar * u + (u_bar - u * along) * inverse) * valid
        blank = jnp.zeros((2, WIDE), F32)

        def slotted(values, slot):
            second = slot > 0.5
            return jnp.concatenate(
                [jnp.where(second, 0.0, values), jnp.where(second, values, 0.0), blank], axis=0
            )

        pulls = jnp.concatenate(
            [slotted(d_bar, pair[1:2]), slotted(-d_bar, pair[3:4])], axis=1
        )
        high, low = split2(jnp.concatenate([pulls, jnp.zeros((120, 2 * WIDE), F32)], axis=0))
        where = jnp.concatenate([one_hot(pair[6:7], OWN, OWN), one_hot(pair[7:8], OWN, OWN)], axis=1)
        own_out[...] += mm_nt(where, high) + mm_nt(where, low)
        return carry

    lax.fori_loop(0, front, stage_three, jnp.int32(0))


def load_rows(rows_ref, low, own, high):
    rows_ref[0:ROWS] = jnp.zeros((ROWS, LANES), F32)
    for i in range(7):
        at = i * 56
        for piece, start in ((low, 0), (high, 40)):
            both = piece[i]
            rows_ref[at + start : at + start + 8] = both
            rows_ref[at + start + 8 : at + start + 16] = pltpu.roll(both, HALF, 1)
        for j in range(3):
            rows_ref[at + 16 + 8 * j : at + 24 + 8 * j, 0:HALF] = own[i, j]


def own_rows(rows_ref):
    return jnp.concatenate(
        [rows_ref[(i * 7 + 2) * 8 : (i * 7 + 5) * 8] for i in range(2, 5)], axis=0
    )


def put_positions(turned, pos_t):
    one = turned.astype(BF16)
    rest = turned - one.astype(F32)
    two = rest.astype(BF16)
    three = (rest - two.astype(F32)).astype(BF16)
    for i, part in enumerate((one, two, three)):
        pos_t[i * LAYER : (i + 1) * LAYER] = part[:, 0:LAYER]


def fetch(copies, sems):
    made = [pltpu.make_async_copy(src, dst, sems.at[i]) for i, (src, dst) in enumerate(copies)]
    for copy in made:
        copy.start()

    def wait():
        for copy in made:
            copy.wait()

    return wait


def pack_kernel(pos_in, vel_in, kind_in, count_in, list_in, out, across, within,
                pos, vel, kind, count, lists, sems, grid, first_list, second_list):
    even = lax.axis_index("gz") % 2 == 0
    fetch(
        ((pos_in, pos), (vel_in, vel), (kind_in, kind), (count_in, count), (list_in, lists)), sems
    )()
    for x in range(3):
        for y in range(3):
            at = (3 * x + y) * 16
            for s in range(2):
                for c in range(3):
                    grid[at + POS + 3 * s + c : at + POS + 3 * s + c + 1, 2:5] = pos[c, x, y, s : s + 1]
                    grid[at + VEL + 3 * s + c : at + VEL + 3 * s + c + 1, 2:5] = vel[c, x, y, s : s + 1]
                grid[at + KIND + s : at + KIND + s + 1, 2:5] = kind[x, y, s : s + 1].astype(F32)
                grid[at + LIVE + s : at + LIVE + s + 1, 2:5] = (
                    count[x, y : y + 1] > s
                ).astype(F32)
            row = (3 * x + y) * 8 + 2
            first_list[row : row + 3, 0:LISTED] = lists[x, y, :, 0].astype(F32)
            second_list[row : row + 3, 0:LISTED] = lists[x, y, :, 1].astype(F32)
    turned = jnp.concatenate(
        [jnp.transpose(grid[0:128])[0:8], jnp.transpose(grid[128:256])[0:8]], axis=1
    )
    lane = iota((8, LANES), 1)
    row = iota((8, LANES), 0)
    inside = (row > 1.5) & (row < 4.5)
    for xy in range(9):
        half = turned[:, 0:LANES] if xy < 8 else turned[:, LANES:]
        shift = (xy % 8) * 16
        fields = pltpu.roll(half, (LANES - shift) % LANES, 1)
        one = pltpu.roll(first_list[xy * 8 : xy * 8 + 8], NEIGH, 1)
        two = pltpu.roll(second_list[xy * 8 : xy * 8 + 8], NEIGH + LIST, 1)
        merged = jnp.where(lane < NEIGH, fields, jnp.where(lane < NEIGH + LIST, one, two))
        merged = jnp.where(inside & (lane < MISC), merged, 0.0)
        out[xy] = merged
        across[xy] = jnp.where(even, merged[2:4], merged[3:5])
        within[xy] = jnp.where(even, merged[3:5], merged[2:4])


def prep_kernel(bw_in, se_in, wmt_in, sm_in, eo_in, table_in,
                w1t, w1, wmt, wm, smt, sm, eo, base, below, levels, bw, se, table, sems):
    fetch(
        (
            (bw_in, bw),
            (se_in, se),
            (wmt_in, wmt),
            (sm_in, sm),
            (eo_in, eo.at[0:1]),
            (table_in, table),
        ),
        sems,
    )()
    for k in range(NSPEC):
        levels[k : k + 1] = jnp.broadcast_to(table[0:1, k : k + 1], (1, LANES))
    both = jnp.concatenate(
        [bw[...].astype(F32), se[...].astype(F32), jnp.zeros((3, LAT), F32)], axis=0
    )
    w1[...] = both.astype(BF16)
    w1t[...] = jnp.transpose(deepen(both, LANES)).astype(BF16)[:, 0:16]
    wm[...] = jnp.transpose(deepen(wmt[...].astype(F32), LANES)).astype(BF16)[:, 0:CH]
    smt[...] = jnp.transpose(deepen(sm[...].astype(F32), LANES)).astype(BF16)[:, 0:CH]
    eo[...] = jnp.transpose(jnp.broadcast_to(eo[0:1], (LAT, LANES)))
    row = iota((ROWS, LANES), 0)
    x, y, z = row_coords(row)
    unused = (z > 6.5) | (row > USED - 0.5)
    for i, v in enumerate((x, y, z)):
        base[i] = jnp.where(unused, 99.0, 3.0 * jnp.floor((v + 1.5) * (1.0 / 3.0)) - 5.0)
    base[3] = jnp.where(unused, 99.0, away(x, y, z))
    below[...] = (iota((ROWS, DEPTH), 1) < iota((ROWS, DEPTH), 0)).astype(F32).astype(BF16)


def lanes_of(values, lane, first, second):
    return jnp.where(lane < 2.5, values[:, first : first + 1], values[:, second : second + 1])


def own_lane_row():
    lane = iota((72, LANES), 1)
    row = iota((72, LANES), 0)
    z = row - 8.0 * jnp.floor(row * 0.125)
    return lane, (z > 1.5) & (z < 4.5)


def first_kernel(low, own, high, w1t, w1, wmt, wm, smt, sm, eo, base, below, levels,
                 force_out, moved_out, live_out, energy_out, pairs_ref, counts_ref,
                 rows_ref, table, off_ref, end_ref, pos_t, own_ref, *scratch):
    load_rows(rows_ref, low, own, high)
    turned = jnp.transpose(deepen(rows_ref[0:ROWS], DEPTH))
    lane = iota((56, LANES), 1)
    layers = sum(
        pltpu.roll(jnp.where(lane < 8.0, rows_ref[x * 56 : x * 56 + 56], 0.0), 8 * x, 1)
        for x in range(7)
    )
    put_positions(jnp.transpose(deepen(layers, LANES))[0:LAYER], pos_t)
    front, every = build_pairs(
        rows_ref, base, below, table, off_ref, end_ref, pairs_ref, turned[NEIGH:MISC].astype(BF16)
    )
    counts_ref[0] = front
    counts_ref[1] = every
    refs = (pos_t, pairs_ref, w1t, w1, wmt, wm, smt, sm, eo)
    evaluate(refs, scratch, (front, every), own_ref, False)
    mine = own_rows(rows_ref)
    lane, inside = own_lane_row()
    kind3 = lanes_of(mine, lane, KIND, KIND + 1)
    speed = pltpu.roll(mine, LANES - VEL, 1)
    live3 = jnp.where(inside & (lane < 6.0), lanes_of(mine, lane, LIVE, LIVE + 1), 0.0)
    live_out[...] = live3
    force = jnp.where(inside & (lane < 6.0), own_ref[0:72] * live3, 0.0)
    force_out[...] = force
    inverse_mass = jnp.zeros((72, LANES), F32)
    for k, mass in enumerate(atom_masses):
        inverse_mass = jnp.where(kind3 == float(k), 1.0 / mass, inverse_mass)
    moved = mine + time_step * speed + 0.5 * time_step * time_step * inverse_mass * force
    moved = jnp.where(lane < 6.0, moved, 0.0)
    for y in range(3):
        moved_out[y] = sum(
            pltpu.roll(moved[(x * 3 + y) * 8 : (x * 3 + y) * 8 + 8], (x + 2) * 16, 1)
            for x in range(3)
        )
    live = pltpu.roll(mine, LANES - LIVE + KIND, 1)
    live = jnp.where(inside & (lane > 5.5) & (lane < 7.5), live, 0.0)
    atom = jnp.zeros((72, LANES), F32)
    for k in range(NSPEC):
        atom = jnp.where(mine == float(k), levels[k : k + 1], atom)
    atoms = jnp.sum(atom * live)
    energy_out[...] = energy_row(jnp.sum(scratch[-1][0:1]) + atoms, atoms, jnp.sum(live))


def moved_positions(low, own, high, pos_t):
    layers = [piece[i] for piece, width in ((low, 2), (own, 3), (high, 2)) for i in range(width)]
    turned = jnp.transpose(deepen(jnp.concatenate(layers, axis=0), LANES))
    blocks = [turned[x * 16 : x * 16 + 8] for x in range(7)] + [jnp.zeros((8, LANES), F32)]
    put_positions(jnp.concatenate(blocks, axis=0), pos_t)


def energy_kernel(low, own, high, w1t, w1, wmt, wm, smt, sm, eo, pairs_ref, counts_ref, energy_in,
                  energy_out, pos_t, *scratch):
    moved_positions(low, own, high, pos_t)
    refs = (pos_t, pairs_ref, w1t, w1, wmt, wm, smt, sm, eo)
    evaluate(refs, scratch, (counts_ref[0], counts_ref[1]), None, True, early=True)
    energy_out[...] = energy_in[...] + energy_row(0.0, jnp.sum(scratch[-1][0:1]), 0.0)


def second_kernel(low, own, high, w1t, w1, wmt, wm, smt, sm, eo, pairs_ref, counts_ref, live,
                  force_out, pos_t, own_ref, *scratch):
    moved_positions(low, own, high, pos_t)
    refs = (pos_t, pairs_ref, w1t, w1, wmt, wm, smt, sm, eo)
    evaluate(refs, scratch, (counts_ref[0], counts_ref[1]), own_ref, True)
    lane, inside = own_lane_row()
    force_out[...] = jnp.where(inside & (lane < 6.0), own_ref[0:72] * live[...], 0.0)


def energy_row(first, second, live):
    lane = iota((1, LANES), 1)
    return (
        jnp.where(lane == 0.0, first, 0.0)
        + jnp.where(lane == 1.0, second, 0.0)
        + jnp.where((lane == 2.0) | (lane == 3.0), live, 0.0)
    )


EVAL_SCRATCH = (
    pltpu.VMEM((4 * CH, INNER), F32),
    pltpu.VMEM((4 * CH, INNER), BF16),
    pltpu.VMEM((4 * CH, INNER), F32),
    pltpu.VMEM((TILES, 24, WIDE), F32),
    pltpu.VMEM((TILES, 16, WIDE), BF16),
    pltpu.VMEM((TILES, LAT, WIDE), BF16),
    pltpu.VMEM((TILES, LAT, WIDE), F32),
    pltpu.VMEM((TILES, CH, WIDE), F32),
    pltpu.VMEM((TILES, CH, WIDE), F32),
    pltpu.VMEM((TILES, LAT, WIDE), BF16),
    pltpu.VMEM((8, WIDE), F32),
)
VM = pl.BlockSpec(memory_space=pltpu.VMEM)
SM = pl.BlockSpec(memory_space=pltpu.SMEM)
HB = pl.BlockSpec(memory_space=pltpu.HBM)


def limit(mebibytes):
    return pltpu.CompilerParams(vmem_limit_bytes=mebibytes * 2**20)


def shape(*dims, kind=F32):
    return jax.ShapeDtypeStruct(dims, kind)


def pack_call(positions, velocity, species, region_count, neighbours):
    return pl.pallas_call(
        pack_kernel,
        name="pack",
        out_shape=(shape(9, 8, LANES), shape(9, 2, LANES), shape(9, 2, LANES)),
        in_specs=[HB] * 5,
        out_specs=(VM, VM, VM),
        scratch_shapes=(
            pltpu.VMEM((3, 3, 3, 2, 3), F32),
            pltpu.VMEM((3, 3, 3, 2, 3), F32),
            pltpu.VMEM((3, 3, 2, 3), jnp.int32),
            pltpu.VMEM((3, 3, 3), jnp.int32),
            pltpu.VMEM((3, 3, 3, 2, LISTED), jnp.int32),
            pltpu.SemaphoreType.DMA((5,)),
            pltpu.VMEM((256, LANES), F32),
            pltpu.VMEM((72, LANES), F32),
            pltpu.VMEM((72, LANES), F32),
        ),
    )(
        positions.transpose(0, 1, 2, 4, 3),
        velocity.transpose(0, 1, 2, 4, 3),
        species.transpose(0, 1, 3, 2),
        region_count,
        neighbours,
    )


def prep_call(basis_weight, species_embed, weight_map, scalar_map, energy_out, species_energy):
    return pl.pallas_call(
        prep_kernel,
        name="prep",
        out_shape=(
            shape(LAT, 16, kind=BF16),
            shape(16, LAT, kind=BF16),
            shape(CH, LAT, kind=BF16),
            shape(LAT, CH, kind=BF16),
            shape(LAT, CH, kind=BF16),
            shape(CH, LAT, kind=BF16),
            shape(LAT, LANES),
            shape(4, ROWS, LANES),
            shape(ROWS, DEPTH, kind=BF16),
            shape(8, LANES),
        ),
        in_specs=[HB] * 6,
        out_specs=(VM,) * 10,
        scratch_shapes=(
            pltpu.VMEM((NB, LAT), BF16),
            pltpu.VMEM((NSPEC, LAT), BF16),
            pltpu.VMEM((1, NSPEC), F32),
            pltpu.SemaphoreType.DMA((6,)),
        ),
        compiler_params=limit(4),
        cost_estimate=pl.CostEstimate(flops=1000000, transcendentals=0, bytes_accessed=2000000),
    )(
        basis_weight,
        species_embed,
        weight_map.T,
        scalar_map,
        energy_out[None, :],
        species_energy[None, :],
    )


def first_call(pieces, prepared):
    return pl.pallas_call(
        first_kernel,
        name="first",
        out_shape=(
            shape(72, LANES),
            shape(3, 8, LANES),
            shape(72, LANES),
            shape(1, LANES),
            shape(TILES, 24, WIDE),
            shape(2, kind=jnp.int32),
        ),
        in_specs=[VM] * (len(pieces) + len(prepared)),
        out_specs=(VM, VM, VM, VM, VM, SM),
        scratch_shapes=(
            pltpu.VMEM((ROWS, LANES), F32),
            pltpu.VMEM((2, 4 * LIST + 16, DEPTH), BF16),
            pltpu.VMEM((2, ROWS, LANES), F32),
            pltpu.VMEM((2, ROWS, LANES), F32),
            pltpu.VMEM((3 * LAYER, LAYER), BF16),
            pltpu.VMEM((OWN, LANES), F32),
            *EVAL_SCRATCH,
        ),
        compiler_params=limit(20),
    )(*pieces, *prepared)


def energy_call(pieces, weights, pairs, counts, energy):
    return pl.pallas_call(
        energy_kernel,
        name="energy",
        out_shape=shape(1, LANES),
        in_specs=[VM] * (len(pieces) + len(weights) + 1) + [SM, VM],
        out_specs=VM,
        scratch_shapes=(pltpu.VMEM((3 * LAYER, LAYER), BF16), *EVAL_SCRATCH),
        compiler_params=limit(20),
    )(*pieces, *weights, pairs, counts, energy)


def second_call(pieces, weights, pairs, counts, live):
    return pl.pallas_call(
        second_kernel,
        name="second",
        out_shape=shape(72, LANES),
        in_specs=[VM] * (len(pieces) + len(weights) + 1) + [SM, VM],
        out_specs=VM,
        scratch_shapes=(
            pltpu.VMEM((3 * LAYER, LAYER), BF16),
            pltpu.VMEM((OWN, LANES), F32),
            *EVAL_SCRATCH,
        ),
        compiler_params=limit(20),
        cost_estimate=pl.CostEstimate(flops=400000000, transcendentals=0, bytes_accessed=4000000),
    )(*pieces, *weights, pairs, counts, live)


def is_even(axis):
    return lax.axis_index(axis) % 2 == 0


def trade(across, within, axis):
    count = lax.axis_size(axis)
    inner = [(i, i ^ 1) for i in range(count)]
    outer = [(i, (i - 1) % count if i % 2 == 0 else (i + 1) % count) for i in range(count)]
    across = lax.ppermute(across, axis, outer)
    within = lax.ppermute(within, axis, inner)
    even = is_even(axis)
    return jnp.where(even, across, within), jnp.where(even, within, across)


def swap(low_part, high_part, axis):
    even = is_even(axis)
    return trade(jnp.where(even, low_part, high_part), jnp.where(even, high_part, low_part), axis)


def everywhere(row, axes, groups):
    rows = jnp.broadcast_to(row[None], (len(groups[0]), 1, LANES))
    rows = lax.all_to_all(rows, axes, 0, 0, axis_index_groups=groups, tiled=False)
    return jnp.sum(rows, axis=0)


def everyone(row):
    nx, ny, nz = (lax.axis_size(axis) for axis in ("gx", "gy", "gz"))
    part = nx // 3
    columns = [
        [(k * part + i) * ny + j for k in range(3) for j in range(ny)] for i in range(part)
    ]
    planes = [[(k * part + i) * nz + j for i in range(part) for j in range(nz)] for k in range(3)]
    row = everywhere(row, ("gx", "gy"), columns)
    return everywhere(row, ("gx", "gz"), planes)


def spread_rows(rows, across, within, beside):
    low, high = trade(across, within, "gz")
    low, high = (v.reshape(3, 3, 2, LANES)[..., 0:HALF] for v in (low, high))
    rows = rows.reshape(3, 3, 8, LANES)[:, :, 2:5, 0:HALF]
    rows = jnp.concatenate([low, rows, high, jnp.zeros((3, 3, 1, HALF), F32)], axis=2)

    def joined(one, two):
        return jnp.concatenate([one, two], axis=-1)

    def parted(both):
        return jnp.stack([both[..., 0:HALF], both[..., HALF:]])

    low, high = swap(joined(rows[0], rows[1]), joined(rows[1], rows[2]), "gx")
    rows = jnp.concatenate([parted(low), rows, parted(high)], axis=0)
    rows, beside = lax.optimization_barrier((rows, beside))
    low, high = swap(joined(rows[:, 0], rows[:, 1]), joined(rows[:, 1], rows[:, 2]), "gy")
    return (low, rows, high), beside


def spread_moved(rows):
    low, high = swap(rows[:, 2:4], rows[:, 3:5], "gz")
    rows = jnp.concatenate([low, rows[:, 2:5], high, jnp.zeros((3, 1, LANES), F32)], axis=1)
    low, high = trade(rows, rows, "gx")
    rows = jnp.concatenate(
        [low[..., 48:80], rows[..., 32:80], high[..., 32:64], jnp.zeros((3, 8, 16), F32)], axis=-1
    )
    low, high = swap(rows[0:2], rows[1:3], "gy")
    return low, rows, high


def unpack(force):
    own = force.reshape(3, 3, 8, LANES)[:, :, 2:5, 0:6]
    return own.reshape(3, 3, 3, 2, 3).transpose(4, 0, 1, 2, 3)


def shards(positions, velocity, species, region_count, neighbours,
           basis_weight, species_embed, weight_map, scalar_map, energy_out, species_energy):
    sent = pack_call(positions, velocity, species, region_count, neighbours)
    prepared = prep_call(
        basis_weight, species_embed, weight_map, scalar_map, energy_out, species_energy
    )
    pieces, prepared = spread_rows(*sent, prepared)
    force_one, moved, live, energy_one, pairs, counts = first_call(pieces, prepared)
    pieces = spread_moved(moved)
    energies = energy_call(pieces, prepared[0:7], pairs, counts, energy_one)
    totals = everyone(energies)
    force_two = second_call(pieces, prepared[0:7], pairs, counts, live)
    forces = jnp.stack([unpack(force_one), unpack(force_two)])
    return forces, totals[0, 0:2] / totals[0, 2:4]


def solution(mesh):
    placed = (
        P(None, "gx", "gy", "gz", None),
        P(None, "gx", "gy", "gz", None),
        P("gx", "gy", "gz", None),
        P("gx", "gy", "gz"),
        P("gx", "gy", "gz", None, None),
        P(),
        P(),
        P(),
        P(),
        P(),
        P(),
    )
    return jax.shard_map(
        shards,
        mesh=mesh,
        in_specs=placed,
        out_specs=(P(None, None, "gx", "gy", "gz", None), P()),
        check_vma=False,
    )
```

```python
import math

import jax
import jax.numpy as jnp
from jax import lax
from jax.experimental import pallas as pl
from jax.experimental.pallas import tpu as pltpu
from jax.sharding import PartitionSpec as P


cutoff = 6.0
env_scale = 0.25
domain_side = 18.0
time_step = 0.15
atom_masses = (1.008, 12.011, 14.007, 15.999, 32.06)

CH = 64
LAT = 128
NB = 8
NSPEC = 5
LIST = 24
LISTED = 40
USED = 392
ROWS = 400
LAYER = 64
DEPTH = 512
INNER = 256
OWN = 80
WIDE = 256
TILES = 26
LANES = 128
HALF = 64
POS, KIND, VEL, LIVE, NEIGH = 0, 6, 8, 14, 16
MISC = NEIGH + 2 * LIST
F32 = jnp.float32
BF16 = jnp.bfloat16


def mm(a, b):
    return lax.dot_general(a, b, (((1,), (0,)), ((), ())), preferred_element_type=F32)


def mm_nt(a, b):
    return lax.dot_general(a, b, (((1,), (1,)), ((), ())), preferred_element_type=F32)


def split2(v):
    high = v.astype(BF16)
    return high, (v - high.astype(F32)).astype(BF16)


def iota(shape, dim):
    return lax.broadcasted_iota(jnp.int32, shape, dim).astype(F32)


def sigmoid(v):
    return 1.0 / (1.0 + jnp.exp(-v))


def row_coords(row):
    xy = jnp.floor(row * 0.125)
    z = row - 8.0 * xy
    x = jnp.floor((xy + 0.5) * (1.0 / 7.0))
    return x, xy - 7.0 * x, z


def away(x, y, z):
    return jnp.maximum(jnp.maximum(jnp.abs(x - 3.0), jnp.abs(y - 3.0)), jnp.abs(z - 3.0))


def far_coords(x, y, z, entry):
    q = jnp.floor(entry * 0.5)
    a = jnp.floor((q + 0.5) * (1.0 / 25.0))
    ab = jnp.floor((q + 0.5) * (1.0 / 5.0))
    steps = (a, ab - 5.0 * a, q - 5.0 * ab)
    far = [3.0 * jnp.floor((v + 1.5) * (1.0 / 3.0)) + s - 2.0 for v, s in zip((x, y, z), steps)]
    shift = [(jnp.floor((s + 2.5) * (1.0 / 3.0)) - 1.0) * domain_side for s in steps]
    return far, shift, entry - 2.0 * q


def one_hot(index, count, depth):
    hit = (iota((count, index.shape[1]), 0) == index).astype(F32).astype(BF16)
    return deepen(hit, depth)


def deepen(values, depth):
    more = depth - values.shape[0]
    if more == 0:
        return values
    return jnp.concatenate([values, jnp.zeros((more, values.shape[1]), values.dtype)], axis=0)


def build_pairs(rows_ref, base_ref, below_ref, table, off_ref, end_ref, pairs_ref, listed_t):
    lane = iota((ROWS, LANES), 1)
    entry = rows_ref[0:ROWS]
    listed = (lane >= NEIGH) & (lane < MISC) & (entry >= 0.0)
    q = jnp.floor(entry * 0.5)
    a = jnp.floor((q + 0.5) * (1.0 / 25.0))
    ab = jnp.floor((q + 0.5) * (1.0 / 5.0))
    far = jnp.maximum(jnp.abs(base_ref[0] + a), jnp.abs(base_ref[1] + (ab - 5.0 * a)))
    far = jnp.maximum(far, jnp.abs(base_ref[2] + (q - 5.0 * ab)))
    nearest = jnp.where(listed, jnp.minimum(base_ref[3], far), 9.0)
    kept = (nearest < 1.5, (nearest > 1.5) & (nearest < 2.5))
    upto = iota((2 * LIST, LANES), 0) + NEIGH
    place = iota((2 * LIST, LANES), 1)
    keys = (place <= upto).astype(F32) + (place < upto).astype(F32)
    keys = keys.astype(BF16)
    ones = jnp.ones((LANES, LANES), BF16)
    cx, cy, cz = row_coords(iota((1, DEPTH), 1))
    keeps = [deepen(keep.astype(F32).astype(BF16), DEPTH) for keep in kept]
    counts = [mm(keep, ones) for keep in keeps]
    counts_t = [mm_nt(ones[0:16], keep).astype(BF16) for keep in keeps]
    below = below_ref[...]
    offsets = mm(below, jnp.concatenate(counts, axis=1).astype(BF16))
    offsets_t = mm_nt(jnp.concatenate(counts_t, axis=0), below)
    first = jnp.zeros((1, 1), F32)
    ends = []
    for which, keep in enumerate(keeps):
        offset = offsets[:, which * LANES : (which + 1) * LANES] + first
        end = offset + counts[which][0:ROWS]
        off_ref[which] = offset
        end_ref[which] = end
        offset_t = offsets_t[16 * which : 16 * which + 1] + first
        offset_t = jnp.concatenate([offset_t, jnp.zeros((1, DEPTH - ROWS), F32)], axis=1)
        high = jnp.floor(offset_t * (1.0 / 256.0))
        misc = jnp.concatenate(
            [high, offset_t - 256.0 * high, cx, cy, cz, jnp.zeros((11, DEPTH), F32)], axis=0
        )
        table[which, 0 : 2 * LIST] = listed_t
        table[which, 2 * LIST : 4 * LIST] = mm_nt(keys, keep).astype(BF16)
        table[which, 4 * LIST :] = misc.astype(BF16)
        first = jnp.max(jnp.max(end, axis=0, keepdims=True), axis=1, keepdims=True)
        ends.append(jnp.max(first))
    first = jnp.float32(0.0)
    totals = []
    for which, total in enumerate(ends):

        def body(k, carry, which=which, first=first, total=total):
            place = iota((1, WIDE), 1) + (k * WIDE).astype(F32)
            offset = off_ref[which]
            end = end_ref[which]
            hit = jnp.concatenate(
                [
                    ((offset <= part) & (end > part)).astype(F32).astype(BF16)
                    for part in (place[:, 0:LANES], place[:, LANES:])
                ],
                axis=1,
            )
            got = mm(table[which], deepen(hit, DEPTH))
            misc = got[4 * LIST :]
            wanted = 2.0 * (place - (256.0 * misc[0:1] + misc[1:2])) + 1.0
            chosen = (got[2 * LIST : 4 * LIST] == wanted).astype(F32)
            entry = jnp.sum(chosen * got[0 : 2 * LIST], axis=0, keepdims=True)
            slot = jnp.sum(chosen[LIST:], axis=0, keepdims=True)
            x, y, z = misc[2:3], misc[3:4], misc[4:5]
            far, shift, far_slot = far_coords(x, y, z, entry)
            valid = place < total
            away_i, away_j = away(x, y, z), away(*far)

            def where(flag, value):
                return jnp.where(flag, value, -1.0)

            def region(c):
                return c[1] * 8.0 + c[2]

            def inner(c, s):
                return (((c[0] - 1.0) * 5.0 + (c[1] - 1.0)) * 5.0 + (c[2] - 1.0)) * 2.0 + s

            def own(c):
                return ((c[0] - 2.0) * 3.0 + (c[1] - 2.0)) * 8.0 + c[2]

            near = (x, y, z)
            lines = [
                where(valid, region(near)),
                slot,
                where(valid, region(far)),
                far_slot,
                where(valid & (away_i < 2.5), inner(near, slot)),
                where(valid & (away_j < 2.5), inner(far, far_slot)),
                where(valid & (away_i < 1.5), own(near)),
                where(valid & (away_j < 1.5), own(far)),
                valid.astype(F32),
                *shift,
                (valid & (away_i < 1.5)).astype(F32),
                near[0],
                far[0],
                jnp.zeros((9, WIDE), F32),
            ]
            pairs_ref[k] = jnp.where(place < first, pairs_ref[k], jnp.concatenate(lines, axis=0))
            return carry

        last = total.astype(jnp.int32)
        lax.fori_loop(
            first.astype(jnp.int32) // WIDE, (last + (WIDE - 1)) // WIDE, body, jnp.int32(0)
        )
        totals.append((last + (WIDE - 1)) // WIDE)
        first = total
    return totals


def turns(radius):
    part = radius * (1.0 / 12.0)
    part = part - jnp.floor(part + 0.5)
    half = part * math.pi
    sq = half * half
    s = jnp.full_like(sq, -1.0 / 39916800.0)
    for c in (1.0 / 362880.0, -1.0 / 5040.0, 1.0 / 120.0, -1.0 / 6.0, 1.0):
        s = s * sq + c
    s = s * half
    c = jnp.full_like(sq, 1.0 / 479001600.0)
    for k in (-1.0 / 3628800.0, 1.0 / 40320.0, -1.0 / 720.0, 1.0 / 24.0, -0.5, 1.0):
        c = c * sq + k
    return 2.0 * s * c, 1.0 - 2.0 * s * s


def evaluate(refs, scratch, counts, own_out, moved, early=False):
    pos_t, pairs_ref, w1t, w1, wmt, wm, smt, sm, eo_ref = refs
    env_ref, envs_ref, grad_ref, geo_ref, feat_ref, lat_ref, slope_ref, h_ref, wb_ref, hp_ref = (
        scratch[:-1]
    )
    en_ref = scratch[-1]
    front, every = counts
    norm = math.sqrt(2.0 / cutoff)

    def eo():
        return jnp.concatenate([eo_ref[...], eo_ref[...]], axis=1)

    env_ref[...] = jnp.zeros(env_ref.shape, F32)
    if not early:
        grad_ref[...] = jnp.zeros(grad_ref.shape, F32)
    en_ref[...] = jnp.zeros(en_ref.shape, F32)
    if not early:
        own_out[...] = jnp.zeros(own_out.shape, F32)

    def gathered(place, layer, slot):
        got = mm(pos_t[...], one_hot(place, LAYER, LAYER))
        full = jnp.zeros((8, WIDE), F32)
        for x in range(7):
            at = 8 * x
            part = got[at : at + 8] + got[LAYER + at : LAYER + at + 8]
            part = part + got[2 * LAYER + at : 2 * LAYER + at + 8]
            full = full + jnp.where(layer == float(x), part, 0.0)
        second = slot > 0.5
        point = jnp.where(second, full[3:6], full[0:3])
        return point, jnp.where(second, full[7:8], full[6:7])

    def shape_pairs(t):
        pair = pairs_ref[t]
        valid = pair[8:9]
        near, near_kind = gathered(pair[0:1], pair[13:14], pair[1:2])
        far, far_kind = gathered(pair[2:3], pair[14:15], pair[3:4])
        if moved:
            near_kind, far_kind = pair[15:16], pair[16:17]
        else:
            pairs_ref[t, 15:17] = jnp.concatenate([near_kind, far_kind], axis=0)
        d = far - near + pair[9:12]
        square = jnp.sum(d * d, axis=0, keepdims=True)
        square = jnp.where(valid > 0.5, square, 1.0)
        radius = jnp.sqrt(square)
        inverse = 1.0 / radius
        u = d * inverse
        y = jnp.minimum(radius * (1.0 / cutoff), 1.0)
        y2 = y * y
        y5 = y2 * y2 * y
        f = 1.0 + y5 * y * (-28.0 + y * (48.0 - 21.0 * y))
        fd = y5 * (-168.0 + y * (336.0 - 168.0 * y)) * (1.0 / cutoff)
        sin1, cos1 = turns(radius)
        sines, cosines = [jnp.zeros_like(sin1), sin1], [jnp.ones_like(cos1), cos1]
        for _ in range(NB - 1):
            sines.append(2.0 * cos1 * sines[-1] - sines[-2])
            cosines.append(2.0 * cos1 * cosines[-1] - cosines[-2])
        basis = [norm * inverse * s for s in sines[1:]]
        slope = [
            norm * (k * (math.pi / cutoff)) * inverse * c - inverse * b
            for k, (c, b) in enumerate(zip(cosines[1:], basis), 1)
        ]
        kinds = [
            (near_kind == float(k)).astype(F32) + (far_kind == float(k)).astype(F32)
            for k in range(NSPEC)
        ]
        feats = jnp.concatenate(basis + kinds + [jnp.zeros((3, WIDE), F32)], axis=0)
        geo_ref[t, 0:16] = jnp.concatenate(
            [u, inverse, f, fd, jnp.zeros((2, WIDE), F32)] + slope, axis=0
        )
        feat_ref[t] = feats.astype(BF16)

    def stage_one(t, carry):
        shape_pairs(t)
        pair = pairs_ref[t]
        geo = geo_ref[t]
        valid, u, f = pair[8:9], geo[0:3], geo[4:5]
        pre = mm(w1t[...], feat_ref[t])
        gate = sigmoid(pre)
        lat = (pre * gate).astype(BF16)
        lat_ref[t] = lat
        slope_ref[t] = gate * (1.0 + pre * (1.0 - gate))
        h = mm(wmt[...], lat)
        h_ref[t] = h
        w = h * (f * valid)
        hit_i = one_hot(pair[4:5], INNER, INNER)
        hit_j = one_hot(pair[5:6], INNER, INNER)
        moments = jnp.concatenate([w, w * u[0:1], w * u[1:2], w * u[2:3]], axis=0).astype(BF16)
        env_ref[0:CH] += mm_nt(moments[0:CH], hit_i + hit_j)
        env_ref[CH:] += mm_nt(moments[CH:], hit_i - hit_j)
        return carry

    lax.fori_loop(0, front if early else every, stage_one, jnp.int32(0))
    envs_ref[...] = env_ref[...].astype(BF16)

    def forward(t):
        pair = pairs_ref[t]
        geo = geo_ref[t]
        valid = pair[8:9]
        u = geo[0:3]
        f = geo[4:5]
        hit = one_hot(pair[4:5], INNER, INNER)
        env = mm(envs_ref[...], hit)
        aligned = (
            env[0:CH]
            + u[0:1] * env[CH : 2 * CH]
            + u[1:2] * env[2 * CH : 3 * CH]
            + u[2:3] * env[3 * CH :]
        )
        w = h_ref[t] * (f * valid)
        coupling = (env_scale * w * aligned).astype(BF16)
        arg = lat_ref[t].astype(F32) + mm(smt[...], coupling)
        gate = sigmoid(arg)
        dotted = jnp.sum(arg * gate * eo(), axis=0, keepdims=True)
        return valid, u, f, hit, env, aligned, w, arg, gate, dotted, f * dotted * pair[12:13]

    def stage_energy(t, carry):
        en_ref[0:1] += forward(t)[-1]
        return carry

    if early:
        lax.fori_loop(0, front, stage_energy, jnp.int32(0))
        return

    def stage_two(t, carry):
        valid, u, f, hit, env, aligned, w, arg, gate, dotted, energy = forward(t)
        en_ref[0:1] += energy
        arg_bar = (f * valid) * eo() * (gate * (1.0 + arg * (1.0 - gate)))
        arg_bar = arg_bar.astype(BF16)
        hp_ref[t] = arg_bar
        c_bar = mm(sm[...], arg_bar).astype(BF16).astype(F32)
        wb_ref[t] = env_scale * aligned * c_bar
        al_bar = env_scale * w * c_bar
        geo_ref[t, 6:7] = dotted * valid
        u_bar = [
            jnp.sum(al_bar * env[(k + 1) * CH : (k + 2) * CH], axis=0, keepdims=True)
            for k in range(3)
        ]
        geo_ref[t, 16:19] = jnp.concatenate(u_bar, axis=0)
        pulls = jnp.concatenate(
            [al_bar, al_bar * u[0:1], al_bar * u[1:2], al_bar * u[2:3]], axis=0
        )
        grad_ref[...] += mm_nt(pulls.astype(BF16), hit)
        return carry

    lax.fori_loop(0, every, stage_two, jnp.int32(0))
    envs_ref[...] = grad_ref[...].astype(BF16)

    def stage_three(t, carry):
        pair = pairs_ref[t]
        geo = geo_ref[t]
        valid = pair[8:9]
        u, inverse, f, fd = geo[0:3], geo[3:4], geo[4:5], geo[5:6]
        hit_i = one_hot(pair[4:5], INNER, INNER)
        hit_j = one_hot(pair[5:6], INNER, INNER)
        grad = envs_ref[...]
        g0 = mm(grad[0:CH], hit_i + hit_j)
        gv = mm(grad[CH:], hit_i - hit_j)
        parts = [gv[k * CH : (k + 1) * CH] for k in range(3)]
        h = h_ref[t]
        w = h * (f * valid)
        w_bar = wb_ref[t] + g0 + u[0:1] * parts[0] + u[1:2] * parts[1] + u[2:3] * parts[2]
        u_bar = geo[16:19] + jnp.concatenate(
            [jnp.sum(w * part, axis=0, keepdims=True) for part in parts], axis=0
        )
        f_bar = geo[6:7] + jnp.sum(h * w_bar, axis=0, keepdims=True)
        h_bar = (w_bar * (f * valid)).astype(BF16)
        lat_bar = (mm(wm[...], h_bar).astype(BF16) + hp_ref[t]).astype(F32)
        pre_bar = (lat_bar * slope_ref[t]).astype(BF16)
        basis_bar = mm(w1[...], pre_bar)[0:NB].astype(BF16).astype(F32)
        r_bar = jnp.sum(basis_bar * geo[8:16], axis=0, keepdims=True) + f_bar * fd
        along = jnp.sum(u * u_bar, axis=0, keepdims=True)
        d_bar = (r_bar * u + (u_bar - u * along) * inverse) * valid
        blank = jnp.zeros((2, WIDE), F32)

        def slotted(values, slot):
            second = slot > 0.5
            return jnp.concatenate(
                [jnp.where(second, 0.0, values), jnp.where(second, values, 0.0), blank], axis=0
            )

        pulls = jnp.concatenate(
            [slotted(d_bar, pair[1:2]), slotted(-d_bar, pair[3:4])], axis=1
        )
        high, low = split2(jnp.concatenate([pulls, jnp.zeros((120, 2 * WIDE), F32)], axis=0))
        where = jnp.concatenate([one_hot(pair[6:7], OWN, OWN), one_hot(pair[7:8], OWN, OWN)], axis=1)
        own_out[...] += mm_nt(where, high) + mm_nt(where, low)
        return carry

    lax.fori_loop(0, front, stage_three, jnp.int32(0))


def load_rows(rows_ref, low, own, high):
    rows_ref[0:ROWS] = jnp.zeros((ROWS, LANES), F32)
    for i in range(7):
        at = i * 56
        for piece, start in ((low, 0), (high, 40)):
            both = piece[i]
            rows_ref[at + start : at + start + 8] = both
            rows_ref[at + start + 8 : at + start + 16] = pltpu.roll(both, HALF, 1)
        for j in range(3):
            rows_ref[at + 16 + 8 * j : at + 24 + 8 * j, 0:HALF] = own[i, j]


def own_rows(rows_ref):
    return jnp.concatenate(
        [rows_ref[(i * 7 + 2) * 8 : (i * 7 + 5) * 8] for i in range(2, 5)], axis=0
    )


def put_positions(turned, pos_t):
    one = turned.astype(BF16)
    rest = turned - one.astype(F32)
    two = rest.astype(BF16)
    three = (rest - two.astype(F32)).astype(BF16)
    for i, part in enumerate((one, two, three)):
        pos_t[i * LAYER : (i + 1) * LAYER] = part[:, 0:LAYER]


def fetch(copies, sems):
    made = [pltpu.make_async_copy(src, dst, sems.at[i]) for i, (src, dst) in enumerate(copies)]
    for copy in made:
        copy.start()

    def wait():
        for copy in made:
            copy.wait()

    return wait


def pack_kernel(pos_in, vel_in, kind_in, count_in, list_in, out, across, within,
                pos, vel, kind, count, lists, sems, grid, first_list, second_list):
    even = lax.axis_index("gz") % 2 == 0
    fetch(
        ((pos_in, pos), (vel_in, vel), (kind_in, kind), (count_in, count), (list_in, lists)), sems
    )()
    for x in range(3):
        for y in range(3):
            at = (3 * x + y) * 16
            for s in range(2):
                for c in range(3):
                    grid[at + POS + 3 * s + c : at + POS + 3 * s + c + 1, 2:5] = pos[c, x, y, s : s + 1]
                    grid[at + VEL + 3 * s + c : at + VEL + 3 * s + c + 1, 2:5] = vel[c, x, y, s : s + 1]
                grid[at + KIND + s : at + KIND + s + 1, 2:5] = kind[x, y, s : s + 1].astype(F32)
                grid[at + LIVE + s : at + LIVE + s + 1, 2:5] = (
                    count[x, y : y + 1] > s
                ).astype(F32)
            row = (3 * x + y) * 8 + 2
            first_list[row : row + 3, 0:LISTED] = lists[x, y, :, 0].astype(F32)
            second_list[row : row + 3, 0:LISTED] = lists[x, y, :, 1].astype(F32)
    turned = jnp.concatenate(
        [jnp.transpose(grid[0:128])[0:8], jnp.transpose(grid[128:256])[0:8]], axis=1
    )
    lane = iota((8, LANES), 1)
    row = iota((8, LANES), 0)
    inside = (row > 1.5) & (row < 4.5)
    for xy in range(9):
        half = turned[:, 0:LANES] if xy < 8 else turned[:, LANES:]
        shift = (xy % 8) * 16
        fields = pltpu.roll(half, (LANES - shift) % LANES, 1)
        one = pltpu.roll(first_list[xy * 8 : xy * 8 + 8], NEIGH, 1)
        two = pltpu.roll(second_list[xy * 8 : xy * 8 + 8], NEIGH + LIST, 1)
        merged = jnp.where(lane < NEIGH, fields, jnp.where(lane < NEIGH + LIST, one, two))
        merged = jnp.where(inside & (lane < MISC), merged, 0.0)
        out[xy] = merged
        across[xy] = jnp.where(even, merged[2:4], merged[3:5])
        within[xy] = jnp.where(even, merged[3:5], merged[2:4])


def prep_kernel(bw_in, se_in, wmt_in, sm_in, eo_in, table_in,
                w1t, w1, wmt, wm, smt, sm, eo, base, below, levels, bw, se, table, sems):
    fetch(
        (
            (bw_in, bw),
            (se_in, se),
            (wmt_in, wmt),
            (sm_in, sm),
            (eo_in, eo.at[0:1]),
            (table_in, table),
        ),
        sems,
    )()
    for k in range(NSPEC):
        levels[k : k + 1] = jnp.broadcast_to(table[0:1, k : k + 1], (1, LANES))
    both = jnp.concatenate(
        [bw[...].astype(F32), se[...].astype(F32), jnp.zeros((3, LAT), F32)], axis=0
    )
    w1[...] = both.astype(BF16)
    w1t[...] = jnp.transpose(deepen(both, LANES)).astype(BF16)[:, 0:16]
    wm[...] = jnp.transpose(deepen(wmt[...].astype(F32), LANES)).astype(BF16)[:, 0:CH]
    smt[...] = jnp.transpose(deepen(sm[...].astype(F32), LANES)).astype(BF16)[:, 0:CH]
    eo[...] = jnp.transpose(jnp.broadcast_to(eo[0:1], (LAT, LANES)))
    row = iota((ROWS, LANES), 0)
    x, y, z = row_coords(row)
    unused = (z > 6.5) | (row > USED - 0.5)
    for i, v in enumerate((x, y, z)):
        base[i] = jnp.where(unused, 99.0, 3.0 * jnp.floor((v + 1.5) * (1.0 / 3.0)) - 5.0)
    base[3] = jnp.where(unused, 99.0, away(x, y, z))
    below[...] = (iota((ROWS, DEPTH), 1) < iota((ROWS, DEPTH), 0)).astype(F32).astype(BF16)


def lanes_of(values, lane, first, second):
    return jnp.where(lane < 2.5, values[:, first : first + 1], values[:, second : second + 1])


def own_lane_row():
    lane = iota((72, LANES), 1)
    row = iota((72, LANES), 0)
    z = row - 8.0 * jnp.floor(row * 0.125)
    return lane, (z > 1.5) & (z < 4.5)


def first_kernel(low, own, high, w1t, w1, wmt, wm, smt, sm, eo, base, below, levels,
                 force_out, moved_out, live_out, energy_out, pairs_ref, counts_ref,
                 rows_ref, table, off_ref, end_ref, pos_t, own_ref, *scratch):
    load_rows(rows_ref, low, own, high)
    turned = jnp.transpose(deepen(rows_ref[0:ROWS], DEPTH))
    lane = iota((56, LANES), 1)
    layers = sum(
        pltpu.roll(jnp.where(lane < 8.0, rows_ref[x * 56 : x * 56 + 56], 0.0), 8 * x, 1)
        for x in range(7)
    )
    put_positions(jnp.transpose(deepen(layers, LANES))[0:LAYER], pos_t)
    front, every = build_pairs(
        rows_ref, base, below, table, off_ref, end_ref, pairs_ref, turned[NEIGH:MISC].astype(BF16)
    )
    counts_ref[0] = front
    counts_ref[1] = every
    refs = (pos_t, pairs_ref, w1t, w1, wmt, wm, smt, sm, eo)
    evaluate(refs, scratch, (front, every), own_ref, False)
    mine = own_rows(rows_ref)
    lane, inside = own_lane_row()
    kind3 = lanes_of(mine, lane, KIND, KIND + 1)
    speed = pltpu.roll(mine, LANES - VEL, 1)
    live3 = jnp.where(inside & (lane < 6.0), lanes_of(mine, lane, LIVE, LIVE + 1), 0.0)
    live_out[...] = live3
    force = jnp.where(inside & (lane < 6.0), own_ref[0:72] * live3, 0.0)
    force_out[...] = force
    inverse_mass = jnp.zeros((72, LANES), F32)
    for k, mass in enumerate(atom_masses):
        inverse_mass = jnp.where(kind3 == float(k), 1.0 / mass, inverse_mass)
    moved = mine + time_step * speed + 0.5 * time_step * time_step * inverse_mass * force
    moved = jnp.where(lane < 6.0, moved, 0.0)
    for y in range(3):
        moved_out[y] = sum(
            pltpu.roll(moved[(x * 3 + y) * 8 : (x * 3 + y) * 8 + 8], (x + 2) * 16, 1)
            for x in range(3)
        )
    live = pltpu.roll(mine, LANES - LIVE + KIND, 1)
    live = jnp.where(inside & (lane > 5.5) & (lane < 7.5), live, 0.0)
    atom = jnp.zeros((72, LANES), F32)
    for k in range(NSPEC):
        atom = jnp.where(mine == float(k), levels[k : k + 1], atom)
    atoms = jnp.sum(atom * live)
    energy_out[...] = energy_row(jnp.sum(scratch[-1][0:1]) + atoms, atoms, jnp.sum(live))


def moved_positions(low, own, high, pos_t):
    layers = [piece[i] for piece, width in ((low, 2), (own, 3), (high, 2)) for i in range(width)]
    turned = jnp.transpose(deepen(jnp.concatenate(layers, axis=0), LANES))
    blocks = [turned[x * 16 : x * 16 + 8] for x in range(7)] + [jnp.zeros((8, LANES), F32)]
    put_positions(jnp.concatenate(blocks, axis=0), pos_t)


def energy_kernel(low, own, high, w1t, w1, wmt, wm, smt, sm, eo, pairs_ref, counts_ref, energy_in,
                  energy_out, pos_t, *scratch):
    moved_positions(low, own, high, pos_t)
    refs = (pos_t, pairs_ref, w1t, w1, wmt, wm, smt, sm, eo)
    evaluate(refs, scratch, (counts_ref[0], counts_ref[1]), None, True, early=True)
    energy_out[...] = energy_in[...] + energy_row(0.0, jnp.sum(scratch[-1][0:1]), 0.0)


def second_kernel(low, own, high, w1t, w1, wmt, wm, smt, sm, eo, pairs_ref, counts_ref, live,
                  force_out, pos_t, own_ref, *scratch):
    moved_positions(low, own, high, pos_t)
    refs = (pos_t, pairs_ref, w1t, w1, wmt, wm, smt, sm, eo)
    evaluate(refs, scratch, (counts_ref[0], counts_ref[1]), own_ref, True)
    lane, inside = own_lane_row()
    force_out[...] = jnp.where(inside & (lane < 6.0), own_ref[0:72] * live[...], 0.0)


def energy_row(first, second, live):
    lane = iota((1, LANES), 1)
    return (
        jnp.where(lane == 0.0, first, 0.0)
        + jnp.where(lane == 1.0, second, 0.0)
        + jnp.where((lane == 2.0) | (lane == 3.0), live, 0.0)
    )


EVAL_SCRATCH = (
    pltpu.VMEM((4 * CH, INNER), F32),
    pltpu.VMEM((4 * CH, INNER), BF16),
    pltpu.VMEM((4 * CH, INNER), F32),
    pltpu.VMEM((TILES, 24, WIDE), F32),
    pltpu.VMEM((TILES, 16, WIDE), BF16),
    pltpu.VMEM((TILES, LAT, WIDE), BF16),
    pltpu.VMEM((TILES, LAT, WIDE), F32),
    pltpu.VMEM((TILES, CH, WIDE), F32),
    pltpu.VMEM((TILES, CH, WIDE), F32),
    pltpu.VMEM((TILES, LAT, WIDE), BF16),
    pltpu.VMEM((8, WIDE), F32),
)
VM = pl.BlockSpec(memory_space=pltpu.VMEM)
SM = pl.BlockSpec(memory_space=pltpu.SMEM)
HB = pl.BlockSpec(memory_space=pltpu.HBM)


def limit(mebibytes):
    return pltpu.CompilerParams(vmem_limit_bytes=mebibytes * 2**20)


def shape(*dims, kind=F32):
    return jax.ShapeDtypeStruct(dims, kind)


def pack_call(positions, velocity, species, region_count, neighbours):
    return pl.pallas_call(
        pack_kernel,
        name="pack",
        out_shape=(shape(9, 8, LANES), shape(9, 2, LANES), shape(9, 2, LANES)),
        in_specs=[HB] * 5,
        out_specs=(VM, VM, VM),
        scratch_shapes=(
            pltpu.VMEM((3, 3, 3, 2, 3), F32),
            pltpu.VMEM((3, 3, 3, 2, 3), F32),
            pltpu.VMEM((3, 3, 2, 3), jnp.int32),
            pltpu.VMEM((3, 3, 3), jnp.int32),
            pltpu.VMEM((3, 3, 3, 2, LISTED), jnp.int32),
            pltpu.SemaphoreType.DMA((5,)),
            pltpu.VMEM((256, LANES), F32),
            pltpu.VMEM((72, LANES), F32),
            pltpu.VMEM((72, LANES), F32),
        ),
    )(
        positions.transpose(0, 1, 2, 4, 3),
        velocity.transpose(0, 1, 2, 4, 3),
        species.transpose(0, 1, 3, 2),
        region_count,
        neighbours,
    )


def prep_call(basis_weight, species_embed, weight_map, scalar_map, energy_out, species_energy):
    return pl.pallas_call(
        prep_kernel,
        name="prep",
        out_shape=(
            shape(LAT, 16, kind=BF16),
            shape(16, LAT, kind=BF16),
            shape(CH, LAT, kind=BF16),
            shape(LAT, CH, kind=BF16),
            shape(LAT, CH, kind=BF16),
            shape(CH, LAT, kind=BF16),
            shape(LAT, LANES),
            shape(4, ROWS, LANES),
            shape(ROWS, DEPTH, kind=BF16),
            shape(8, LANES),
        ),
        in_specs=[HB] * 6,
        out_specs=(VM,) * 10,
        scratch_shapes=(
            pltpu.VMEM((NB, LAT), BF16),
            pltpu.VMEM((NSPEC, LAT), BF16),
            pltpu.VMEM((1, NSPEC), F32),
            pltpu.SemaphoreType.DMA((6,)),
        ),
        compiler_params=limit(4),
        cost_estimate=pl.CostEstimate(flops=1000000, transcendentals=0, bytes_accessed=2000000),
    )(
        basis_weight,
        species_embed,
        weight_map.T,
        scalar_map,
        energy_out[None, :],
        species_energy[None, :],
    )


def first_call(pieces, prepared):
    return pl.pallas_call(
        first_kernel,
        name="first",
        out_shape=(
            shape(72, LANES),
            shape(3, 8, LANES),
            shape(72, LANES),
            shape(1, LANES),
            shape(TILES, 24, WIDE),
            shape(2, kind=jnp.int32),
        ),
        in_specs=[VM] * (len(pieces) + len(prepared)),
        out_specs=(VM, VM, VM, VM, VM, SM),
        scratch_shapes=(
            pltpu.VMEM((ROWS, LANES), F32),
            pltpu.VMEM((2, 4 * LIST + 16, DEPTH), BF16),
            pltpu.VMEM((2, ROWS, LANES), F32),
            pltpu.VMEM((2, ROWS, LANES), F32),
            pltpu.VMEM((3 * LAYER, LAYER), BF16),
            pltpu.VMEM((OWN, LANES), F32),
            *EVAL_SCRATCH,
        ),
        compiler_params=limit(20),
    )(*pieces, *prepared)


def energy_call(pieces, weights, pairs, counts, energy):
    return pl.pallas_call(
        energy_kernel,
        name="energy",
        out_shape=shape(1, LANES),
        in_specs=[VM] * (len(pieces) + len(weights) + 1) + [SM, VM],
        out_specs=VM,
        scratch_shapes=(pltpu.VMEM((3 * LAYER, LAYER), BF16), *EVAL_SCRATCH),
        compiler_params=limit(20),
    )(*pieces, *weights, pairs, counts, energy)


def second_call(pieces, weights, pairs, counts, live):
    return pl.pallas_call(
        second_kernel,
        name="second",
        out_shape=shape(72, LANES),
        in_specs=[VM] * (len(pieces) + len(weights) + 1) + [SM, VM],
        out_specs=VM,
        scratch_shapes=(
            pltpu.VMEM((3 * LAYER, LAYER), BF16),
            pltpu.VMEM((OWN, LANES), F32),
            *EVAL_SCRATCH,
        ),
        compiler_params=limit(20),
        cost_estimate=pl.CostEstimate(flops=400000000, transcendentals=0, bytes_accessed=4000000),
    )(*pieces, *weights, pairs, counts, live)


def is_even(axis):
    return lax.axis_index(axis) % 2 == 0


def trade(across, within, axis):
    count = lax.axis_size(axis)
    inner = [(i, i ^ 1) for i in range(count)]
    outer = [(i, (i - 1) % count if i % 2 == 0 else (i + 1) % count) for i in range(count)]
    across = lax.ppermute(across, axis, outer)
    within = lax.ppermute(within, axis, inner)
    even = is_even(axis)
    return jnp.where(even, across, within), jnp.where(even, within, across)


def swap(low_part, high_part, axis):
    even = is_even(axis)
    return trade(jnp.where(even, low_part, high_part), jnp.where(even, high_part, low_part), axis)


def everywhere(row, axes, groups):
    rows = jnp.broadcast_to(row[None], (len(groups[0]), 1, LANES))
    rows = lax.all_to_all(rows, axes, 0, 0, axis_index_groups=groups, tiled=False)
    return jnp.sum(rows, axis=0)


def everyone(row):
    nx, ny, nz = (lax.axis_size(axis) for axis in ("gx", "gy", "gz"))
    part = nx // 3
    columns = [
        [(k * part + i) * ny + j for k in range(3) for j in range(ny)] for i in range(part)
    ]
    planes = [[(k * part + i) * nz + j for i in range(part) for j in range(nz)] for k in range(3)]
    row = everywhere(row, ("gx", "gz"), planes)
    return everywhere(row, ("gx", "gy"), columns)


def spread_rows(rows, across, within, beside):
    low, high = trade(across, within, "gz")
    low, high = (v.reshape(3, 3, 2, LANES)[..., 0:HALF] for v in (low, high))
    rows = rows.reshape(3, 3, 8, LANES)[:, :, 2:5, 0:HALF]
    rows = jnp.concatenate([low, rows, high, jnp.zeros((3, 3, 1, HALF), F32)], axis=2)

    def joined(one, two):
        return jnp.concatenate([one, two], axis=-1)

    def parted(both):
        return jnp.stack([both[..., 0:HALF], both[..., HALF:]])

    low, high = swap(joined(rows[0], rows[1]), joined(rows[1], rows[2]), "gx")
    rows = jnp.concatenate([parted(low), rows, parted(high)], axis=0)
    rows, beside = lax.optimization_barrier((rows, beside))
    low, high = swap(joined(rows[:, 0], rows[:, 1]), joined(rows[:, 1], rows[:, 2]), "gy")
    return (low, rows, high), beside


def spread_moved(rows):
    low, high = swap(rows[:, 2:4], rows[:, 3:5], "gz")
    rows = jnp.concatenate([low, rows[:, 2:5], high, jnp.zeros((3, 1, LANES), F32)], axis=1)
    low, high = trade(rows, rows, "gx")
    rows = jnp.concatenate(
        [low[..., 48:80], rows[..., 32:80], high[..., 32:64], jnp.zeros((3, 8, 16), F32)], axis=-1
    )
    low, high = swap(rows[0:2], rows[1:3], "gy")
    return low, rows, high


def unpack(force):
    own = force.reshape(3, 3, 8, LANES)[:, :, 2:5, 0:6]
    return own.reshape(3, 3, 3, 2, 3).transpose(4, 0, 1, 2, 3)


def shards(positions, velocity, species, region_count, neighbours,
           basis_weight, species_embed, weight_map, scalar_map, energy_out, species_energy):
    sent = pack_call(positions, velocity, species, region_count, neighbours)
    prepared = prep_call(
        basis_weight, species_embed, weight_map, scalar_map, energy_out, species_energy
    )
    pieces, prepared = spread_rows(*sent, prepared)
    force_one, moved, live, energy_one, pairs, counts = first_call(pieces, prepared)
    pieces = spread_moved(moved)
    energies = energy_call(pieces, prepared[0:7], pairs, counts, energy_one)
    totals = everyone(energies)
    force_two = second_call(pieces, prepared[0:7], pairs, counts, live)
    forces = jnp.stack([unpack(force_one), unpack(force_two)])
    return forces, totals[0, 0:2] / totals[0, 2:4]


def solution(mesh):
    placed = (
        P(None, "gx", "gy", "gz", None),
        P(None, "gx", "gy", "gz", None),
        P("gx", "gy", "gz", None),
        P("gx", "gy", "gz"),
        P("gx", "gy", "gz", None, None),
        P(),
        P(),
        P(),
        P(),
        P(),
        P(),
    )
    return jax.shard_map(
        shards,
        mesh=mesh,
        in_specs=placed,
        out_specs=(P(None, None, "gx", "gy", "gz", None), P()),
        check_vma=False,
    )
```
